32 devices in a mesh: dp: 16 (over z, y, x), head: 2 (over core).
Axes of the slice: x: 2, y: 2, z: 4, core: 2. Of those that a mesh axis runs over, the one named last changes fastest.
Arguments:
- inputs: bfloat16 [24576, 768], P(('dp', 'head')), may hold values from -6 to 6
- qkv_weight: bfloat16 [768, 3, 768], P('dp', None, 'head'), may hold values from -0.21875 to 0.21875
- qv_bias: float32 [2, 768], P(None, 'head'), may hold values from -3 to 3
- out_weight: bfloat16 [768, 768], P('dp', 'head'), may hold values from -2.5 to 2.5
- out_bias: float32 [768], replicated, may hold values from -1.75 to 1.75
- first_gain: float32 [768], replicated, may hold values from 0.5 to 1.5
- first_shift: float32 [768], replicated, may hold values from -1.75 to 1.75
- up_weight: bfloat16 [768, 3072], P('dp', 'head'), may hold values from -0.21875 to 0.21875
- up_bias: float32 [3072], P('head'), may hold values from -3 to 3
- down_weight: bfloat16 [768, 3072], P('dp', 'head'), may hold values from -0.15625 to 0.15625
- down_bias: float32 [768], replicated, may hold values from -1.75 to 1.75
- second_gain: float32 [768], replicated, may hold values from 0.5 to 1.5
- second_shift: float32 [768], replicated, may hold values from -1.75 to 1.75
- item_lengths: int32 [16, 2], P('dp'), may hold values from 0 to 1536, as said below
- random_blocks: int32 [16, 12, 24, 3], P('dp', 'head'), may hold values from 0 to 22, as said below
- out_grad: bfloat16 [24576, 768], P(('dp', 'head')), may hold values from -16 to 16
Outputs:
- layer_out: bfloat16 [24576, 768], P(('dp', 'head'))
- input_grad: bfloat16 [24576, 768], P(('dp', 'head'))
- grad_qkv: float32 [768, 3, 768], P('dp', None, 'head')
- grad_qv_bias: float32 [2, 768], P(None, 'head')
- grad_out: float32 [768, 768], P('dp', 'head')
- grad_out_bias: float32 [768], replicated
- grad_first_gain: float32 [768], replicated
- grad_first_shift: float32 [768], replicated
- grad_up: float32 [768, 3072], P('dp', 'head')
- grad_up_bias: float32 [3072], P('head')
- grad_down: float32 [768, 3072], P('dp', 'head')
- grad_down_bias: float32 [768], replicated
- grad_second_gain: float32 [768], replicated
- grad_second_shift: float32 [768], replicated
The draws below stay inside these ranges and needn't reach their ends.
Inputs may be any that keep to these rules, and one draw needn't show every extreme that they name: `item_lengths`: each row lists a data group's items in order, then zeros. A group holds either one item of 1536 tokens (filling all 1536 rows; 1 group are such) or one to 2 items of 768 tokens; some group holds 2 items. `random_blocks`: for head h and block b of a group, where b is block r of an item of n blocks with 0 < r < n - 1: three different block numbers of that item, none of them 0, n - 1, r - 1, r or r + 1. Elsewhere 0.
All inputs are finite; a program needn't handle non-finite values.
Results may differ from the reference program's by a relative error of at most 0.019.
Values may be sent and summed in bfloat16 or wider, within the bound.
No kernel may reach another device: no remote copies, remote signals or barrier semaphores. Data moves between devices by JAX's collectives and lax.ppermute only.
A program may use at most 256 MiB of HBM per device.

```python
import math
import jax
import jax.numpy as jnp
from jax import lax

D = 768
HEADS = 12
HD = 64
FF = 3072
BLK = 64
RAND = 3
SLOTS = 2
SHORT_LEN = 768
LONG_LEN = 1536
CAPB = 24
CAP = 1536
GROUPS = 16
LONG_GROUPS = 1
TOKENS = 24576


def group_layout(key):
    base = jax.random.fold_in(key, 17)
    first_key, second_key = jax.random.split(base)
    order = jax.random.permutation(first_key, GROUPS).astype(jnp.int32)
    ranks = jnp.zeros((GROUPS,), jnp.int32).at[order].set(jnp.arange(GROUPS, dtype=jnp.int32))
    counts = jax.random.randint(second_key, (GROUPS,), 1, SLOTS + 1).astype(jnp.int32)
    counts = jnp.where(ranks == LONG_GROUPS, SLOTS, counts)
    slot_ids = jnp.arange(SLOTS, dtype=jnp.int32)[None, :]
    short_rows = jnp.where(slot_ids < counts[:, None], SHORT_LEN, 0)
    long_rows = jnp.where(slot_ids == 0, LONG_LEN, 0) + jnp.zeros((GROUPS, 1), jnp.int32)
    return jnp.where((ranks < LONG_GROUPS)[:, None], long_rows, short_rows).astype(jnp.int32)


def draw_item_lengths(key, part):
    return group_layout(key)


def draw_random_blocks(key, part):
    lengths = group_layout(key)
    counts = lengths // BLK
    starts = jnp.cumsum(counts, axis=1) - counts
    blocks = jnp.arange(CAPB, dtype=jnp.int32)
    inside = (blocks[None, None, :] >= starts[:, :, None]) & (blocks[None, None, :] < (starts + counts)[:, :, None])
    member = inside.astype(jnp.int32)
    live = jnp.sum(member, axis=1)
    first = jnp.sum(member * starts[:, :, None], axis=1)
    item_blocks = jnp.sum(member * counts[:, :, None], axis=1)
    relative = blocks[None, :] - first
    sparse = (live > 0) & (relative > 0) & (relative < item_blocks - 1)
    far_apart = jnp.abs(blocks[None, None, :] - relative[:, :, None]) > 1
    eligible = (blocks[None, None, :] > 0) & (blocks[None, None, :] < item_blocks[:, :, None] - 1) & far_apart & sparse[:, :, None]
    noise = jax.random.randint(jax.random.fold_in(key, 29), (GROUPS, HEADS, CAPB, CAPB), 0, 1 << 20).astype(jnp.int32)
    scores = noise * CAPB + blocks[None, None, None, :]
    scores = jnp.where(eligible[:, None, :, :], scores, -1)
    picked = lax.top_k(scores, RAND)[1].astype(jnp.int32)
    return jnp.where(sparse[:, None, :, None], picked, 0).astype(jnp.int32)


def draw_out_grad(key, part):
    rows = jnp.arange(TOKENS, dtype=jnp.float32)[:, None] / TOKENS
    values = jax.random.normal(key, (TOKENS, D), jnp.float32) * (1.0 + 2.0 * rows)
    return jnp.clip(values, -16.0, 16.0).astype(jnp.bfloat16)


def strengthened(array, own_key, source, target, shards_of, factor):
    def block_of(position):
        return (jnp.arange(array.shape[position]) // (array.shape[position] // shards_of)).reshape((-1,) + (1,) * (array.ndim - 1 - position))

    first = jax.random.permutation(own_key, shards_of)[block_of(target)]
    second = (block_of(target) + shards_of // 2) % shards_of
    return jnp.where((block_of(source) == first) | (block_of(source) == second), factor * array, array)


def block_scale(own_key, shape, cuts, low, top_value):
    def one(axis_at, blocks):
        draws = jax.random.uniform(jax.random.fold_in(jax.random.fold_in(own_key, 6), axis_at), (blocks,), jnp.float32, low / len(cuts), top_value / len(cuts))
        return jnp.repeat(jnp.exp(draws), shape[axis_at] // blocks).reshape((-1,) + (1,) * (len(shape) - axis_at - 1))

    level = one(*cuts[0])
    for cut in cuts[1:]:
        level = level * one(*cut)
    return level


def gaussian(rng, dims, deviation, reach, cuts=(), held_as=jnp.bfloat16):
    array = deviation * jax.random.normal(rng, dims, jnp.float32)
    if cuts:
        array = array * block_scale(rng, dims, cuts, -0.22, 0.18)
    return jnp.clip(array, -reach, reach).astype(held_as)


def noise_with(own_key, extent, width, bound, shards, heavy, kind=jnp.bfloat16):
    array = width * jax.random.normal(own_key, extent, jnp.float32)
    if shards:
        array = array * block_scale(own_key, extent, shards, -0.22, 0.18)
    return jnp.clip(strengthened(array, jax.random.fold_in(own_key, 3), *heavy), -bound, bound).astype(kind)


def setup_inputs(seed: int = 0) -> dict:
    arg_keys = jax.random.split(jax.random.key(seed), 17)
    return {
        "inputs": noise_with(arg_keys[0], (TOKENS, D), 1.0, 6.0, ((0, 32),), (0, 1, 32, 2.75)),
        "qkv_weight": gaussian(arg_keys[1], (D, 3, D), D ** -0.5, 0.21875, ((0, 16), (2, 2))),
        "qv_bias": gaussian(arg_keys[2], (2, D), 0.5, 3.0, ((1, 2),), jnp.float32),
        "out_weight": gaussian(arg_keys[3], (D, D), (max(D // 128, 1)) ** -0.5, 2.5, ((0, 16), (1, 2))),
        "out_bias": gaussian(arg_keys[4], (D,), 0.3, 1.75, (), jnp.float32),
        "first_gain": jnp.clip(1.0 + 0.1 * jax.random.normal(arg_keys[5], (D,), jnp.float32), 0.5, 1.5),
        "first_shift": gaussian(arg_keys[6], (D,), 0.3, 1.75, (), jnp.float32),
        "up_weight": gaussian(arg_keys[7], (D, FF), D ** -0.5, 0.21875, ((0, 16), (1, 2))),
        "up_bias": gaussian(arg_keys[8], (FF,), 0.5, 3.0, ((0, 2),), jnp.float32),
        "down_weight": gaussian(arg_keys[9], (D, FF), (FF // 2) ** -0.5, 0.15625, ((0, 16), (1, 2))),
        "down_bias": gaussian(arg_keys[10], (D,), 0.3, 1.75, (), jnp.float32),
        "second_gain": jnp.clip(1.0 + 0.1 * jax.random.normal(arg_keys[11], (D,), jnp.float32), 0.5, 1.5),
        "second_shift": gaussian(arg_keys[12], (D,), 0.3, 1.75, (), jnp.float32),
        "item_lengths": draw_item_lengths(jax.random.fold_in(arg_keys[16], 71), 0),
        "random_blocks": draw_random_blocks(jax.random.fold_in(arg_keys[16], 71), 0),
        "out_grad": draw_out_grad(jax.random.fold_in(arg_keys[16], 71), 0),
    }


@jax.custom_vjp
def low(v):
    return lax.optimization_barrier(v.astype(jnp.bfloat16)).astype(jnp.float32)

@jax.custom_vjp
def low_back(v):
    return v

def low_keep(v):
    return (low(v), None)

def low_pass(kept, grad):
    return (grad,)

def back_keep(v):
    return (v, None)

def back_low(kept, grad):
    return (low(grad),)
low.defvjp(low_keep, low_pass)
low_back.defvjp(back_keep, back_low)
highest = lax.Precision.HIGHEST
norm_eps = 1e-06
negative = -1e+30

def layer_norm(values, gain, shift):
    centered = values - lax.optimization_barrier(jnp.mean(values, axis=-1, keepdims=True))
    inverse = lax.rsqrt(lax.optimization_barrier(jnp.mean(centered * centered, axis=-1, keepdims=True)) + norm_eps)
    return centered * inverse * gain + shift

def block_table(lengths):
    counts = lengths // BLK
    starts = jnp.cumsum(counts) - counts
    blocks = jnp.arange(CAPB, dtype=jnp.int32)
    inside = (blocks[None, :] >= starts[:, None]) & (blocks[None, :] < (starts + counts)[:, None])
    member = inside.astype(jnp.int32)
    live = lax.optimization_barrier(jnp.sum(member, axis=0))
    first = lax.optimization_barrier(jnp.sum(member * starts[:, None], axis=0))
    item_blocks = lax.optimization_barrier(jnp.sum(member * counts[:, None], axis=0))
    return (member, live, first, item_blocks)

def allowed_blocks(lengths, randoms):
    member, live, first, item_blocks = block_table(lengths)
    blocks = jnp.arange(CAPB, dtype=jnp.int32)
    relative = blocks - first
    last = item_blocks - 1
    same = lax.optimization_barrier(jnp.sum(member[:, :, None] * member[:, None, :], axis=0)) > 0
    key_rel = blocks[None, :] - first[:, None]
    is_live = live > 0
    is_global = is_live & ((relative == 0) | (relative == last))
    near = (key_rel == 0) | (key_rel == last[:, None]) | (jnp.abs(key_rel - relative[:, None]) <= 1)
    chosen = jnp.any(key_rel[None, :, :, None] == randoms[:, :, None, :], axis=-1)
    picked = same[None] & (is_global[None, :, None] | near[None] | chosen)
    alone = jnp.logical_not(is_live)[:, None] & (blocks[None, :] == blocks[:, None])
    return is_live[None, :, None] & picked | alone[None]

def forward(params, rows, mask, live_rows):
    qkv_w, qv_b, out_w, out_b, gain_one, shift_one, up_w, up_b, down_w, down_b, gain_two, shift_two = params
    bias = jnp.stack([qv_b[0], jnp.zeros_like(qv_b[0]), qv_b[1]])
    triple = low_back(low(jnp.einsum('td,dcf->tcf', rows, qkv_w, precision=highest) + bias))
    queries = triple[:, 0].reshape(CAP, HEADS, HD)
    keys_all = triple[:, 1].reshape(CAP, HEADS, HD)
    values_all = triple[:, 2].reshape(CAP, HEADS, HD)
    scores = low_back(jnp.einsum('qhe,khe->hqk', queries, keys_all, precision=highest) * (1.0 / math.sqrt(HD)))
    scores = jnp.where(mask, scores, negative)
    top = lax.optimization_barrier(jnp.max(scores, axis=-1, keepdims=True))
    expo = jnp.exp(scores - top)
    probs = expo / lax.optimization_barrier(jnp.sum(expo, axis=-1, keepdims=True))
    mixed = jnp.einsum('hqk,khe->qhe', low(probs), values_all, precision=highest).reshape(CAP, D)
    attended = low_back(low(mixed))
    proj = low_back(jnp.einsum('tf,df->td', attended, out_w, precision=highest))
    normed_one = layer_norm(proj + out_b + rows, gain_one, shift_one)
    hidden = low(normed_one)
    upper = low_back(low(jnp.einsum('td,df->tf', hidden, up_w, precision=highest) + up_b))
    active = low(jax.nn.gelu(upper, approximate=True))
    down = low_back(jnp.einsum('tf,df->td', active, down_w, precision=highest))
    result = layer_norm(down + down_b + normed_one, gain_two, shift_two)
    return result * live_rows[:, None]

def reference(inputs, qkv_weight, qv_bias, out_weight, out_bias, first_gain, first_shift, up_weight, up_bias, down_weight, down_bias, second_gain, second_shift, item_lengths, random_blocks, out_grad):
    params = tuple((value.astype(jnp.float32) for value in (qkv_weight, qv_bias, out_weight, out_bias, first_gain, first_shift, up_weight, up_bias, down_weight, down_bias, second_gain, second_shift)))
    rows_all = inputs.astype(jnp.float32).reshape(GROUPS, CAP, D)
    cot_all = out_grad.astype(jnp.float32).reshape(GROUPS, CAP, D)

    def per_group(totals, pieces):
        rows, cotangent, lengths, randoms = pieces
        allowed = allowed_blocks(lengths, randoms)
        mask = jnp.repeat(jnp.repeat(allowed, BLK, axis=1), BLK, axis=2)
        member, live, first, item_blocks = block_table(lengths)
        live_rows = jnp.repeat(live, BLK).astype(jnp.float32)

        def apply_layer(weights, values):
            return forward(weights, values, mask, live_rows)
        result, pullback = jax.vjp(apply_layer, params, rows)
        grads, row_grad = pullback(cotangent)
        totals = jax.tree.map(lambda left, right: left + right, totals, grads)
        return (totals, (result.astype(jnp.bfloat16), row_grad.astype(jnp.bfloat16)))
    zeros = jax.tree.map(jnp.zeros_like, params)
    totals, (outputs, row_grads) = lax.scan(per_group, zeros, (rows_all, cot_all, item_lengths, random_blocks))
    return (outputs.reshape(TOKENS, D), row_grads.reshape(TOKENS, D), totals[0], totals[1], totals[2], totals[3], totals[4], totals[5], totals[6], totals[7], totals[8], totals[9], totals[10], totals[11])
```

```python
import functools

import jax
import jax.numpy as jnp
from jax import lax
from jax.experimental import pallas as pl
from jax.experimental.pallas import tpu as pltpu
from jax.sharding import PartitionSpec as P

BLK = 64


norm_eps = 1e-06
negative = -1e30


def norm_forward(values, gain, shift):
    centered = values - jnp.mean(values, axis=-1, keepdims=True)
    inverse = lax.rsqrt(jnp.mean(centered * centered, axis=-1, keepdims=True) + norm_eps)
    normed = centered * inverse
    return (normed * gain + shift, normed, inverse)


def norm_backward(grad, normed, inverse, gain):
    scaled = grad * gain
    mean_one = jnp.mean(scaled, axis=-1, keepdims=True)
    mean_two = jnp.mean(scaled * normed, axis=-1, keepdims=True)
    return inverse * (scaled - mean_one - normed * mean_two)


def dot_nt(a, b):
    return lax.dot_general(a, b, (((1,), (1,)), ((), ())), preferred_element_type=jnp.float32)
def dot_nn(a, b):
    return lax.dot_general(a, b, (((1,), (0,)), ((), ())), preferred_element_type=jnp.float32)
def dot_tn(a, b):
    return lax.dot_general(a, b, (((0,), (0,)), ((), ())), preferred_element_type=jnp.float32)

def block_scalars(len_ref, b, half_blocks):
    count0 = len_ref[0] // BLK
    count1 = len_ref[1] // BLK
    in0 = b < count0
    live = b < count0 + count1
    first = jnp.where(in0, 0, jnp.where(live, count0, b))
    items = jnp.where(in0, count0, jnp.where(live, count1, 1))
    rel = b - first
    last = items - 1
    is_global = live & ((rel == 0) | (rel == last))
    return live, first, rel, last, is_global

def slot_table(live, first, rel, last, b):
    lo = jnp.where(live, b - 1, b)
    hi = jnp.where(live, b + 1, b)
    zero = jnp.float32(0.0)
    neg = jnp.float32(negative)
    item_bias = jnp.where(live, zero, neg)
    lo_bias = jnp.where(live & (rel > 1), zero, neg)
    hi_bias = jnp.where(live & (rel + 1 < last), zero, neg)
    fixed = [first, first + last, b, lo, hi]
    bias = [item_bias, item_bias, zero, lo_bias, hi_bias, item_bias, item_bias, item_bias]
    return fixed, bias

def attn_fwd_kernel(pairs, rand, half_blocks, len_ref, rb_ref, tri_ref, out_ref):
    width = pairs * 128
    blocks = tri_ref.shape[0] // BLK
    scale = jnp.bfloat16(0.125)
    even = lax.broadcasted_iota(jnp.int32, (BLK, 128), 1) < BLK

    def rows(index, column):
        return tri_ref[pl.ds(pl.multiple_of(index * BLK, BLK), BLK), column:column + 128]

    def stacked(values):
        zero = jnp.zeros_like(values)
        return jnp.concatenate([jnp.where(even, values, zero), jnp.where(even, zero, values)], axis=0)

    def unstack(values):
        return jnp.where(even, values[:BLK], values[BLK:])

    def body(b, carry):
        live, first, rel, last, is_global = block_scalars(len_ref, b, half_blocks)
        here = pl.ds(pl.multiple_of(b * BLK, BLK), BLK)

        @pl.when(jnp.logical_not(is_global))
        def sparse():
            fixed, bias = slot_table(live, first, rel, last, b)
            lane = lax.broadcasted_iota(jnp.int32, (1, 128), 1) < BLK
            bias_row = jnp.concatenate(
                [jnp.where(lane, bias[2 * i], bias[2 * i + 1]) for i in range(4)], axis=1)
            for p in range(pairs):
                at = [[first * 0 + jnp.where(live, first + rb_ref[((2 * p + s) * blocks + b) * rand + k], b) for k in range(rand)] for s in range(2)]
                def unit(column):
                    return jnp.concatenate(
                        [rows(i, column) for i in fixed]
                        + [jnp.where(even, rows(at[0][k], column), rows(at[1][k], column)) for k in range(rand)], axis=0)
                query = stacked(rows(b, p * 128)) * scale
                scores = dot_nt(query, unit(width + p * 128)) + bias_row
                top = jnp.max(scores, axis=1, keepdims=True)
                expo = jnp.exp(scores - top)
                total = jnp.sum(expo, axis=1, keepdims=True)
                mixed = dot_nn(expo.astype(jnp.bfloat16), unit(2 * width + p * 128)) / total
                out_ref[here, p * 128:(p + 1) * 128] = unstack(mixed).astype(jnp.bfloat16)

        @pl.when(is_global)
        def dense():
            span = half_blocks * BLK
            queries = [stacked(rows(b, p * 128)) * scale for p in range(pairs)]
            def chunk(c, state):
                new = []
                at = pl.ds(pl.multiple_of((first + c * half_blocks) * BLK, BLK), span)
                for p in range(pairs):
                    top, total, acc = state[p]
                    scores = dot_nt(queries[p], tri_ref[at, width + p * 128:width + (p + 1) * 128])
                    higher = jnp.maximum(top, jnp.max(scores, axis=1, keepdims=True))
                    shrink = jnp.exp(top - higher)
                    expo = jnp.exp(scores - higher)
                    total = total * shrink + jnp.sum(expo, axis=1, keepdims=True)
                    acc = acc * shrink + dot_nn(expo.astype(jnp.bfloat16), tri_ref[at, 2 * width + p * 128:2 * width + (p + 1) * 128])
                    new.append((higher, total, acc))
                return tuple(new)
            init = tuple((jnp.full((128, 1), negative, jnp.float32), jnp.zeros((128, 1), jnp.float32), jnp.zeros((128, 128), jnp.float32)) for _ in range(pairs))
            state = lax.fori_loop(0, (last + 1) // half_blocks, chunk, init)
            for p in range(pairs):
                _, total, acc = state[p]
                out_ref[here, p * 128:(p + 1) * 128] = unstack(acc / total).astype(jnp.bfloat16)
        return carry

    lax.fori_loop(0, blocks, body, 0)

def attn_bwd_kernel(pairs, rand, half_blocks, len_ref, rb_ref, tri_ref, grad_ref, out_ref, sum_ref, *accs):
    width = pairs * 128
    blocks = tri_ref.shape[0] // BLK
    scale = jnp.bfloat16(0.125)
    even = lax.broadcasted_iota(jnp.int32, (BLK, 128), 1) < BLK
    key_acc, value_acc = accs[:pairs], accs[pairs:]
    for acc in accs:
        acc[...] = jnp.zeros_like(acc)

    def spot(index):
        return pl.ds(pl.multiple_of(index * BLK, BLK), BLK)

    def rows(index, column):
        return tri_ref[spot(index), column:column + 128]

    def stacked(values):
        zero = jnp.zeros_like(values)
        return jnp.concatenate([jnp.where(even, values, zero), jnp.where(even, zero, values)], axis=0)

    def unstack(values):
        return jnp.where(even, values[:BLK], values[BLK:])

    def body(b, carry):
        live, first, rel, last, is_global = block_scalars(len_ref, b, half_blocks)

        @pl.when(jnp.logical_not(is_global))
        def sparse():
            fixed, bias = slot_table(live, first, rel, last, b)
            for p in range(pairs):
                at = [[jnp.where(live, first + rb_ref[((2 * p + s) * blocks + b) * rand + k], b) for k in range(rand)] for s in range(2)]
                def unit(column):
                    return jnp.concatenate(
                        [rows(i, column) for i in fixed]
                        + [jnp.where(even, rows(at[0][k], column), rows(at[1][k], column)) for k in range(rand)], axis=0)
                query = stacked(rows(b, p * 128)) * scale
                grad = stacked(grad_ref[spot(b), p * 128:(p + 1) * 128])
                keys = unit(width + p * 128)
                values = unit(2 * width + p * 128)
                scores = dot_nt(keys, query)
                scores = jnp.concatenate([scores[i * BLK:(i + 1) * BLK] + bias[i] for i in range(5 + rand)], axis=0)
                top = jnp.max(scores, axis=0, keepdims=True)
                expo = jnp.exp(scores - top)
                probs = expo * (1.0 / jnp.sum(expo, axis=0, keepdims=True))
                grad_probs = dot_nt(values, grad)
                delta = jnp.sum(probs * grad_probs, axis=0, keepdims=True)
                grad_scores = (probs * (grad_probs - delta)).astype(jnp.bfloat16)
                grad_query = dot_tn(grad_scores, keys) * 0.125
                out_ref[spot(b), p * 128:(p + 1) * 128] = unstack(grad_query).astype(jnp.bfloat16)
                for acc, update in ((key_acc[p], dot_nn(grad_scores, query)), (value_acc[p], dot_nn(probs.astype(jnp.bfloat16), grad))):
                    for i in range(5):
                        acc[spot(fixed[i]), :] += update[i * BLK:(i + 1) * BLK]
                    for k in range(rand):
                        piece = update[(5 + k) * BLK:(6 + k) * BLK]
                        zero = jnp.zeros_like(piece)
                        acc[spot(at[0][k]), :] += jnp.where(even, piece, zero)
                        acc[spot(at[1][k]), :] += jnp.where(even, zero, piece)

        @pl.when(is_global)
        def dense():
            span = half_blocks * BLK
            chunks = (last + 1) // half_blocks
            def place(c):
                return pl.ds(pl.multiple_of((first + c * half_blocks) * BLK, BLK), span)
            queries = [stacked(rows(b, p * 128)) * scale for p in range(pairs)]
            grads = [stacked(grad_ref[spot(b), p * 128:(p + 1) * 128]) for p in range(pairs)]
            def first_pass(c, state):
                new = []
                at = place(c)
                for p in range(pairs):
                    top, total, dot = state[p]
                    scores = dot_nt(tri_ref[at, width + p * 128:width + (p + 1) * 128], queries[p])
                    grad_probs = dot_nt(tri_ref[at, 2 * width + p * 128:2 * width + (p + 1) * 128], grads[p])
                    higher = jnp.maximum(top, jnp.max(scores, axis=0, keepdims=True))
                    shrink = jnp.exp(top - higher)
                    expo = jnp.exp(scores - higher)
                    total = total * shrink + jnp.sum(expo, axis=0, keepdims=True)
                    dot = dot * shrink + jnp.sum(expo * grad_probs, axis=0, keepdims=True)
                    new.append((higher, total, dot))
                return tuple(new)
            init = tuple((jnp.full((1, 128), negative, jnp.float32), jnp.zeros((1, 128), jnp.float32), jnp.zeros((1, 128), jnp.float32)) for _ in range(pairs))
            state = lax.fori_loop(0, chunks, first_pass, init)
            def second_pass(c, grad_queries):
                new = []
                at = place(c)
                for p in range(pairs):
                    top, total, dot = state[p]
                    inverse = 1.0 / total
                    keys = tri_ref[at, width + p * 128:width + (p + 1) * 128]
                    scores = dot_nt(keys, queries[p])
                    grad_probs = dot_nt(tri_ref[at, 2 * width + p * 128:2 * width + (p + 1) * 128], grads[p])
                    probs = jnp.exp(scores - top) * inverse
                    grad_scores = (probs * (grad_probs - dot * inverse)).astype(jnp.bfloat16)
                    new.append(grad_queries[p] + dot_tn(grad_scores, keys))
                    key_acc[p][at, :] += dot_nn(grad_scores, queries[p])
                    value_acc[p][at, :] += dot_nn(probs.astype(jnp.bfloat16), grads[p])
                return tuple(new)
            grad_queries = lax.fori_loop(0, chunks, second_pass, tuple(jnp.zeros((128, 128), jnp.float32) for _ in range(pairs)))
            for p in range(pairs):
                out_ref[spot(b), p * 128:(p + 1) * 128] = unstack(grad_queries[p] * 0.125).astype(jnp.bfloat16)
        return carry

    lax.fori_loop(0, blocks, body, 0)
    sum_ref[...] = jnp.zeros_like(sum_ref)
    for p in range(pairs):
        column = slice(p * 128, (p + 1) * 128)
        sum_ref[0:1, column] = jnp.sum(out_ref[:, column].astype(jnp.float32), axis=0, keepdims=True)
        out_ref[:, width + p * 128:width + (p + 1) * 128] = key_acc[p][...].astype(jnp.bfloat16)
        value = value_acc[p][...].astype(jnp.bfloat16)
        out_ref[:, 2 * width + p * 128:2 * width + (p + 1) * 128] = value
        sum_ref[1:2, column] = jnp.sum(value.astype(jnp.float32), axis=0, keepdims=True)

def attention_forward(lengths, randoms, triple):
    heads, blocks, rand = randoms.shape
    pairs = heads // 2
    vm = pl.BlockSpec(memory_space=pltpu.VMEM); sm = pl.BlockSpec(memory_space=pltpu.SMEM)
    return pl.pallas_call(
        functools.partial(attn_fwd_kernel, pairs, rand, blocks // 2),
        out_shape=jax.ShapeDtypeStruct((triple.shape[0], pairs * 128), jnp.bfloat16),
        in_specs=[sm, sm, vm], out_specs=vm, name="attend_forward",
        compiler_params=pltpu.CompilerParams(vmem_limit_bytes=60 << 20),
    )(lengths, randoms.reshape(-1), triple)

def attention_backward(lengths, randoms, triple, grad):
    heads, blocks, rand = randoms.shape
    pairs = heads // 2
    vm = pl.BlockSpec(memory_space=pltpu.VMEM); sm = pl.BlockSpec(memory_space=pltpu.SMEM)
    return pl.pallas_call(
        functools.partial(attn_bwd_kernel, pairs, rand, blocks // 2),
        out_shape=(jax.ShapeDtypeStruct(triple.shape, jnp.bfloat16), jax.ShapeDtypeStruct((8, pairs * 128), jnp.float32)),
        in_specs=[sm, sm, vm, vm], out_specs=(vm, vm), name="attend_backward",
        scratch_shapes=[pltpu.VMEM((triple.shape[0], 128), jnp.float32)] * (2 * pairs),
        compiler_params=pltpu.CompilerParams(vmem_limit_bytes=60 << 20),
    )(lengths, randoms.reshape(-1), triple, grad)


def on_device(
    inputs,
    qkv_weight,
    qv_bias,
    out_weight,
    out_bias,
    first_gain,
    first_shift,
    up_weight,
    up_bias,
    down_weight,
    down_bias,
    second_gain,
    second_shift,
    item_lengths,
    random_blocks,
    out_grad,
):
    half = inputs.shape[0]
    width = inputs.shape[1]
    position = lax.axis_index("head")
    head_width = qkv_weight.shape[2]
    full_qkv, full_out, full_up, full_down = (
        lax.all_gather(qkv_weight, "dp", axis=0, tiled=True),
        lax.all_gather(out_weight, "dp", axis=0, tiled=True),
        lax.all_gather(up_weight, "dp", axis=0, tiled=True),
        lax.all_gather(down_weight, "dp", axis=0, tiled=True),
    )
    tokens = lax.all_gather(inputs, "head", axis=0, tiled=True)
    capacity = tokens.shape[0]
    block_count = capacity // BLK
    counts = item_lengths[0] // BLK
    live = (jnp.arange(block_count, dtype=jnp.int32) < jnp.sum(counts)).astype(jnp.int32)
    bias = jnp.stack([qv_bias[0], jnp.zeros_like(qv_bias[0]), qv_bias[1]])
    triple = (
        jnp.einsum("td,dcf->tcf", tokens, full_qkv, preferred_element_type=jnp.float32) + bias
    ).astype(jnp.bfloat16)
    attended = attention_forward(item_lengths[0], random_blocks[0], triple.reshape(capacity, 3 * head_width))
    part = attended
    proj = lax.psum_scatter(
        jnp.einsum("tf,df->td", part, full_out, preferred_element_type=jnp.float32).astype(
            jnp.bfloat16
        ),
        "head",
        scatter_dimension=0,
        tiled=True,
    ).astype(jnp.float32)
    normed_one_out, normed_one, inverse_one = norm_forward(
        proj + out_bias + inputs.astype(jnp.float32), first_gain, first_shift
    )
    hidden = lax.all_gather(normed_one_out.astype(jnp.bfloat16), "head", axis=0, tiled=True)
    upper = (
        jnp.einsum("td,df->tf", hidden, full_up, preferred_element_type=jnp.float32) + up_bias
    ).astype(jnp.bfloat16)
    active = jax.nn.gelu(upper.astype(jnp.float32), approximate=True).astype(jnp.bfloat16)
    part = active
    down = lax.psum_scatter(
        jnp.einsum("tf,df->td", part, full_down, preferred_element_type=jnp.float32).astype(
            jnp.bfloat16
        ),
        "head",
        scatter_dimension=0,
        tiled=True,
    ).astype(jnp.float32)
    normed_two_out, normed_two, inverse_two = norm_forward(
        down + down_bias + normed_one_out, second_gain, second_shift
    )
    live_rows = jnp.repeat(live, BLK).astype(jnp.float32)
    live_half = lax.dynamic_slice_in_dim(live_rows, position * half, half, 0)
    layer_out = (normed_two_out * live_half[:, None]).astype(jnp.bfloat16)
    cotangent = out_grad.astype(jnp.float32) * live_half[:, None]
    second_gain_part = jnp.sum(cotangent * normed_two, axis=0)
    second_shift_part = jnp.sum(cotangent, axis=0)
    grad_res_two = norm_backward(cotangent, normed_two, inverse_two, second_gain)
    down_bias_part = jnp.sum(grad_res_two, axis=0)
    grad_down_rows = lax.all_gather(grad_res_two.astype(jnp.bfloat16), "head", axis=0, tiled=True)
    grad_active = jnp.einsum(
        "td,df->tf", grad_down_rows, full_down, preferred_element_type=jnp.float32
    )
    down_local = jnp.einsum("td,tf->df", grad_down_rows, active, preferred_element_type=jnp.float32)

    def gelu_tanh(values):
        return jax.nn.gelu(values, approximate=True)

    gelu_pull = jax.vjp(gelu_tanh, upper.astype(jnp.float32))[1]
    grad_upper = gelu_pull(grad_active)[0].astype(jnp.bfloat16)
    up_bias_part = jnp.sum(grad_upper.astype(jnp.float32), axis=0)
    up_local = jnp.einsum("td,tf->df", hidden, grad_upper, preferred_element_type=jnp.float32)
    part = grad_upper
    grad_norm_one = (
        lax.psum_scatter(
            jnp.einsum("tf,df->td", part, full_up, preferred_element_type=jnp.float32).astype(
                jnp.bfloat16
            ),
            "head",
            scatter_dimension=0,
            tiled=True,
        ).astype(jnp.float32)
        + grad_res_two
    )
    first_gain_part = jnp.sum(grad_norm_one * normed_one, axis=0)
    first_shift_part = jnp.sum(grad_norm_one, axis=0)
    grad_res_one = norm_backward(grad_norm_one, normed_one, inverse_one, first_gain)
    out_bias_part = jnp.sum(grad_res_one, axis=0)
    grad_proj = lax.all_gather(grad_res_one.astype(jnp.bfloat16), "head", axis=0, tiled=True)
    grad_attended = jnp.einsum(
        "td,df->tf", grad_proj, full_out, preferred_element_type=jnp.float32
    ).astype(jnp.bfloat16)
    out_local = jnp.einsum("td,tf->df", grad_proj, attended, preferred_element_type=jnp.float32)
    grad_flat, bias_sums = attention_backward(
        item_lengths[0], random_blocks[0], triple.reshape(capacity, 3 * head_width), grad_attended
    )
    grad_triple = grad_flat.reshape(capacity, 3, head_width)
    qv_bias_part = bias_sums[:2]
    qkv_local = jnp.einsum("td,tcf->dcf", tokens, grad_triple, preferred_element_type=jnp.float32)
    part = grad_triple
    input_grad = (
        lax.psum_scatter(
            jnp.einsum("tcf,dcf->td", part, full_qkv, preferred_element_type=jnp.float32).astype(
                jnp.bfloat16
            ),
            "head",
            scatter_dimension=0,
            tiled=True,
        ).astype(jnp.float32)
        + grad_res_one
    ).astype(jnp.bfloat16)
    grad_qkv, grad_out, grad_up, grad_down = (
        lax.psum_scatter(qkv_local, "dp", scatter_dimension=0, tiled=True),
        lax.psum_scatter(out_local, "dp", scatter_dimension=0, tiled=True),
        lax.psum_scatter(up_local, "dp", scatter_dimension=0, tiled=True),
        lax.psum_scatter(down_local, "dp", scatter_dimension=0, tiled=True),
    )
    up_width = up_bias.shape[0]
    qv_full = lax.dynamic_update_slice_in_dim(
        jnp.zeros((2, width), jnp.float32), qv_bias_part, position * head_width, 1
    )
    up_full = lax.dynamic_update_slice_in_dim(
        jnp.zeros((up_width * lax.axis_size("head"),), jnp.float32),
        up_bias_part,
        position * up_width,
        0,
    )
    totals = lax.psum(
        (
            qv_full,
            up_full,
            out_bias_part,
            first_gain_part,
            first_shift_part,
            down_bias_part,
            second_gain_part,
            second_shift_part,
        ),
        ("dp", "head"),
    )
    grad_qv_bias = lax.dynamic_slice_in_dim(totals[0], position * head_width, head_width, 1)
    grad_up_bias = lax.dynamic_slice_in_dim(totals[1], position * up_width, up_width, 0)
    return (
        layer_out,
        input_grad,
        grad_qkv,
        grad_qv_bias,
        grad_out,
        totals[2],
        totals[3],
        totals[4],
        grad_up,
        grad_up_bias,
        grad_down,
        totals[5],
        totals[6],
        totals[7],
    )


def solution(mesh):
    in_specs = (
        P(("dp", "head"), None),
        P("dp", None, "head"),
        P(None, "head"),
        P("dp", "head"),
        P(),
        P(),
        P(),
        P("dp", "head"),
        P("head"),
        P("dp", "head"),
        P(),
        P(),
        P(),
        P("dp", None),
        P("dp", "head", None, None),
        P(("dp", "head"), None),
    )
    out_specs = (
        P(("dp", "head"), None),
        P(("dp", "head"), None),
        P("dp", None, "head"),
        P(None, "head"),
        P("dp", "head"),
        P(),
        P(),
        P(),
        P("dp", "head"),
        P("head"),
        P("dp", "head"),
        P(),
        P(),
        P(),
    )
    return jax.shard_map(
        on_device, mesh=mesh, in_specs=in_specs, out_specs=out_specs, check_vma=False
    )
```

```python
import functools

import jax
import jax.numpy as jnp
import numpy as np
from jax import lax
from jax.experimental import pallas as pl
from jax.experimental.pallas import tpu as pltpu
from jax.sharding import Mesh
from jax.sharding import PartitionSpec as P

BLK = 64


norm_eps = 1e-06
negative = -1e30


def norm_forward(values, gain, shift):
    centered = values - jnp.mean(values, axis=-1, keepdims=True)
    inverse = lax.rsqrt(jnp.mean(centered * centered, axis=-1, keepdims=True) + norm_eps)
    normed = centered * inverse
    return (normed * gain + shift, normed, inverse)


def norm_backward(grad, normed, inverse, gain):
    scaled = grad * gain
    mean_one = jnp.mean(scaled, axis=-1, keepdims=True)
    mean_two = jnp.mean(scaled * normed, axis=-1, keepdims=True)
    return inverse * (scaled - mean_one - normed * mean_two)


def dot_nt(a, b):
    return lax.dot_general(a, b, (((1,), (1,)), ((), ())), preferred_element_type=jnp.float32)
def dot_nn(a, b):
    return lax.dot_general(a, b, (((1,), (0,)), ((), ())), preferred_element_type=jnp.float32)
def dot_tn(a, b):
    return lax.dot_general(a, b, (((0,), (0,)), ((), ())), preferred_element_type=jnp.float32)

def block_scalars(len_ref, b, half_blocks):
    count0 = len_ref[0] // BLK
    count1 = len_ref[1] // BLK
    in0 = b < count0
    live = b < count0 + count1
    first = jnp.where(in0, 0, jnp.where(live, count0, b))
    items = jnp.where(in0, count0, jnp.where(live, count1, 1))
    rel = b - first
    last = items - 1
    is_global = live & ((rel == 0) | (rel == last))
    return live, first, rel, last, is_global

def slot_table(live, first, rel, last, b):
    lo = jnp.where(live, b - 1, b)
    hi = jnp.where(live, b + 1, b)
    zero = jnp.float32(0.0)
    neg = jnp.float32(negative)
    item_bias = jnp.where(live, zero, neg)
    lo_bias = jnp.where(live & (rel > 1), zero, neg)
    hi_bias = jnp.where(live & (rel + 1 < last), zero, neg)
    fixed = [first, first + last, b, lo, hi]
    bias = [item_bias, item_bias, zero, lo_bias, hi_bias, item_bias, item_bias, item_bias]
    return fixed, bias

def attn_fwd_kernel(pairs, rand, half_blocks, len_ref, rb_ref, tri_ref, out_ref):
    width = pairs * 128
    blocks = tri_ref.shape[0] // BLK
    scale = jnp.bfloat16(0.125)
    even = lax.broadcasted_iota(jnp.int32, (BLK, 128), 1) < BLK

    shift = len_ref[2]

    def spot(index):
        moved = index + shift
        moved = jnp.where(moved >= blocks, moved - blocks, moved)
        return pl.ds(pl.multiple_of(moved * BLK, BLK), BLK)

    def span_of(index, count):
        moved = index + shift
        moved = jnp.where(moved >= blocks, moved - blocks, moved)
        return pl.ds(pl.multiple_of(moved * BLK, BLK), count * BLK)

    def rows(index, column):
        return tri_ref[spot(index), column:column + 128]

    def stacked(values):
        zero = jnp.zeros_like(values)
        return jnp.concatenate([jnp.where(even, values, zero), jnp.where(even, zero, values)], axis=0)

    def unstack(values):
        return jnp.where(even, values[:BLK], values[BLK:])

    def body(b, carry):
        live, first, rel, last, is_global = block_scalars(len_ref, b, half_blocks)
        here = spot(b)

        @pl.when(jnp.logical_not(is_global))
        def sparse():
            fixed, bias = slot_table(live, first, rel, last, b)
            lane = lax.broadcasted_iota(jnp.int32, (1, 128), 1) < BLK
            bias_row = jnp.concatenate(
                [jnp.where(lane, bias[2 * i], bias[2 * i + 1]) for i in range(4)], axis=1)
            for p in range(pairs):
                at = [[jnp.where(live, first + rb_ref[((2 * p + s) * blocks + b) * rand + k], b) for k in range(rand)] for s in range(2)]
                def unit(column):
                    return jnp.concatenate(
                        [rows(i, column) for i in fixed]
                        + [jnp.where(even, rows(at[0][k], column), rows(at[1][k], column)) for k in range(rand)], axis=0)
                query = stacked(rows(b, p * 128)) * scale
                scores = dot_nt(query, unit(width + p * 128)) + bias_row
                top = jnp.max(scores, axis=1, keepdims=True)
                expo = jnp.exp(scores - top)
                total = jnp.sum(expo, axis=1, keepdims=True)
                mixed = dot_nn(expo.astype(jnp.bfloat16), unit(2 * width + p * 128)) / total
                out_ref[here, p * 128:(p + 1) * 128] = unstack(mixed).astype(jnp.bfloat16)

        @pl.when(is_global)
        def dense():
            queries = [stacked(rows(b, p * 128)) * scale for p in range(pairs)]
            def chunk(c, state):
                new = []
                at = span_of(first + c * half_blocks, half_blocks)
                for p in range(pairs):
                    top, total, acc = state[p]
                    scores = dot_nt(queries[p], tri_ref[at, width + p * 128:width + (p + 1) * 128])
                    higher = jnp.maximum(top, jnp.max(scores, axis=1, keepdims=True))
                    shrink = jnp.exp(top - higher)
                    expo = jnp.exp(scores - higher)
                    total = total * shrink + jnp.sum(expo, axis=1, keepdims=True)
                    acc = acc * shrink + dot_nn(expo.astype(jnp.bfloat16), tri_ref[at, 2 * width + p * 128:2 * width + (p + 1) * 128])
                    new.append((higher, total, acc))
                return tuple(new)
            init = tuple((jnp.full((128, 1), negative, jnp.float32), jnp.zeros((128, 1), jnp.float32), jnp.zeros((128, 128), jnp.float32)) for _ in range(pairs))
            state = lax.fori_loop(0, (last + 1) // half_blocks, chunk, init)
            for p in range(pairs):
                _, total, acc = state[p]
                out_ref[here, p * 128:(p + 1) * 128] = unstack(acc / total).astype(jnp.bfloat16)
        return carry

    lax.fori_loop(0, blocks, body, 0)

def attn_bwd_kernel(pairs, rand, half_blocks, len_ref, rb_ref, tri_ref, grad_ref, out_ref, sum_ref, *accs):
    width = pairs * 128
    blocks = tri_ref.shape[0] // BLK
    scale = jnp.bfloat16(0.125)
    even = lax.broadcasted_iota(jnp.int32, (BLK, 128), 1) < BLK
    key_acc, value_acc = accs[:pairs], accs[pairs:]
    for acc in accs:
        acc[...] = jnp.zeros_like(acc)

    shift = len_ref[2]

    def spot(index):
        moved = index + shift
        moved = jnp.where(moved >= blocks, moved - blocks, moved)
        return pl.ds(pl.multiple_of(moved * BLK, BLK), BLK)

    def span_of(index, count):
        moved = index + shift
        moved = jnp.where(moved >= blocks, moved - blocks, moved)
        return pl.ds(pl.multiple_of(moved * BLK, BLK), count * BLK)

    def rows(index, column):
        return tri_ref[spot(index), column:column + 128]

    def stacked(values):
        zero = jnp.zeros_like(values)
        return jnp.concatenate([jnp.where(even, values, zero), jnp.where(even, zero, values)], axis=0)

    def unstack(values):
        return jnp.where(even, values[:BLK], values[BLK:])

    def body(b, carry):
        live, first, rel, last, is_global = block_scalars(len_ref, b, half_blocks)

        @pl.when(jnp.logical_not(is_global))
        def sparse():
            fixed, bias = slot_table(live, first, rel, last, b)
            for p in range(pairs):
                at = [[jnp.where(live, first + rb_ref[((2 * p + s) * blocks + b) * rand + k], b) for k in range(rand)] for s in range(2)]
                def unit(column):
                    return jnp.concatenate(
                        [rows(i, column) for i in fixed]
                        + [jnp.where(even, rows(at[0][k], column), rows(at[1][k], column)) for k in range(rand)], axis=0)
                query = stacked(rows(b, p * 128)) * scale
                grad = stacked(grad_ref[spot(b), p * 128:(p + 1) * 128])
                keys = unit(width + p * 128)
                values = unit(2 * width + p * 128)
                scores = dot_nt(keys, query)
                scores = jnp.concatenate([scores[i * BLK:(i + 1) * BLK] + bias[i] for i in range(5 + rand)], axis=0)
                top = jnp.max(scores, axis=0, keepdims=True)
                expo = jnp.exp(scores - top)
                probs = expo * (1.0 / jnp.sum(expo, axis=0, keepdims=True))
                grad_probs = dot_nt(values, grad)
                delta = jnp.sum(probs * grad_probs, axis=0, keepdims=True)
                grad_scores = (probs * (grad_probs - delta)).astype(jnp.bfloat16)
                grad_query = dot_tn(grad_scores, keys) * 0.125
                out_ref[spot(b), p * 128:(p + 1) * 128] = unstack(grad_query).astype(jnp.bfloat16)
                for acc, update in ((key_acc[p], dot_nn(grad_scores, query)), (value_acc[p], dot_nn(probs.astype(jnp.bfloat16), grad))):
                    for i in range(5):
                        acc[spot(fixed[i]), :] += update[i * BLK:(i + 1) * BLK]
                    for k in range(rand):
                        piece = update[(5 + k) * BLK:(6 + k) * BLK]
                        zero = jnp.zeros_like(piece)
                        acc[spot(at[0][k]), :] += jnp.where(even, piece, zero)
                        acc[spot(at[1][k]), :] += jnp.where(even, zero, piece)

        @pl.when(is_global)
        def dense():
            chunks = (last + 1) // half_blocks
            def place(c):
                return span_of(first + c * half_blocks, half_blocks)
            queries = [stacked(rows(b, p * 128)) * scale for p in range(pairs)]
            grads = [stacked(grad_ref[spot(b), p * 128:(p + 1) * 128]) for p in range(pairs)]
            def first_pass(c, state):
                new = []
                at = place(c)
                for p in range(pairs):
                    top, total, dot = state[p]
                    scores = dot_nt(tri_ref[at, width + p * 128:width + (p + 1) * 128], queries[p])
                    grad_probs = dot_nt(tri_ref[at, 2 * width + p * 128:2 * width + (p + 1) * 128], grads[p])
                    higher = jnp.maximum(top, jnp.max(scores, axis=0, keepdims=True))
                    shrink = jnp.exp(top - higher)
                    expo = jnp.exp(scores - higher)
                    total = total * shrink + jnp.sum(expo, axis=0, keepdims=True)
                    dot = dot * shrink + jnp.sum(expo * grad_probs, axis=0, keepdims=True)
                    new.append((higher, total, dot))
                return tuple(new)
            init = tuple((jnp.full((1, 128), negative, jnp.float32), jnp.zeros((1, 128), jnp.float32), jnp.zeros((1, 128), jnp.float32)) for _ in range(pairs))
            state = lax.fori_loop(0, chunks, first_pass, init)
            def second_pass(c, grad_queries):
                new = []
                at = place(c)
                for p in range(pairs):
                    top, total, dot = state[p]
                    inverse = 1.0 / total
                    keys = tri_ref[at, width + p * 128:width + (p + 1) * 128]
                    scores = dot_nt(keys, queries[p])
                    grad_probs = dot_nt(tri_ref[at, 2 * width + p * 128:2 * width + (p + 1) * 128], grads[p])
                    probs = jnp.exp(scores - top) * inverse
                    grad_scores = (probs * (grad_probs - dot * inverse)).astype(jnp.bfloat16)
                    new.append(grad_queries[p] + dot_tn(grad_scores, keys))
                    key_acc[p][at, :] += dot_nn(grad_scores, queries[p])
                    value_acc[p][at, :] += dot_nn(probs.astype(jnp.bfloat16), grads[p])
                return tuple(new)
            grad_queries = lax.fori_loop(0, chunks, second_pass, tuple(jnp.zeros((128, 128), jnp.float32) for _ in range(pairs)))
            for p in range(pairs):
                out_ref[spot(b), p * 128:(p + 1) * 128] = unstack(grad_queries[p] * 0.125).astype(jnp.bfloat16)
        return carry

    lax.fori_loop(0, blocks, body, 0)
    sum_ref[...] = jnp.zeros_like(sum_ref)
    for p in range(pairs):
        column = slice(p * 128, (p + 1) * 128)
        sum_ref[0:1, column] = jnp.sum(out_ref[:, column].astype(jnp.float32), axis=0, keepdims=True)
        out_ref[:, width + p * 128:width + (p + 1) * 128] = key_acc[p][...].astype(jnp.bfloat16)
        value = value_acc[p][...].astype(jnp.bfloat16)
        out_ref[:, 2 * width + p * 128:2 * width + (p + 1) * 128] = value
        sum_ref[1:2, column] = jnp.sum(value.astype(jnp.float32), axis=0, keepdims=True)

def attention_forward(lengths, randoms, triple):
    heads, blocks, rand = randoms.shape
    pairs = heads // 2
    vm = pl.BlockSpec(memory_space=pltpu.VMEM); sm = pl.BlockSpec(memory_space=pltpu.SMEM)
    return pl.pallas_call(
        functools.partial(attn_fwd_kernel, pairs, rand, blocks // 2),
        out_shape=jax.ShapeDtypeStruct((triple.shape[0], pairs * 128), jnp.bfloat16),
        in_specs=[sm, sm, vm], out_specs=vm, name="attend_forward",
        compiler_params=pltpu.CompilerParams(vmem_limit_bytes=60 << 20),
    )(lengths, randoms.reshape(-1), triple)

def attention_backward(lengths, randoms, triple, grad):
    heads, blocks, rand = randoms.shape
    pairs = heads // 2
    vm = pl.BlockSpec(memory_space=pltpu.VMEM); sm = pl.BlockSpec(memory_space=pltpu.SMEM)
    return pl.pallas_call(
        functools.partial(attn_bwd_kernel, pairs, rand, blocks // 2),
        out_shape=(jax.ShapeDtypeStruct(triple.shape, jnp.bfloat16), jax.ShapeDtypeStruct((8, pairs * 128), jnp.float32)),
        in_specs=[sm, sm, vm, vm], out_specs=(vm, vm), name="attend_backward",
        scratch_shapes=[pltpu.VMEM((triple.shape[0], 128), jnp.float32)] * (2 * pairs),
        compiler_params=pltpu.CompilerParams(vmem_limit_bytes=60 << 20),
    )(lengths, randoms.reshape(-1), triple, grad)


QUAD = 4


def group_permute(value, deep, target):
    pairs = []
    for z in range(deep):
        for q in range(QUAD):
            for h in range(2):
                to_z, to_q = target(z, q, h)
                pairs.append(((z * QUAD + q) * 2 + h, (to_z * QUAD + to_q) * 2 + h))
    return lax.ppermute(value, ("deep", "quad", "head"), pairs)


def deep_step(value, deep, bit):
    return group_permute(value, deep, lambda z, q, h: (z ^ bit, q))


def quad_step(value, deep, second):
    return group_permute(value, deep, lambda z, q, h: (z, q ^ ((2 >> h) if second else (1 << h))))


def swap(value):
    return lax.ppermute(value, "head", [(0, 1), (1, 0)])


def gather_deep(value, deep):
    z = lax.axis_index("deep")
    block = value[None]
    bit = 1
    while bit < deep:
        other = deep_step(block, deep, bit)
        low = (z & bit) == 0
        block = jnp.concatenate(
            [jnp.where(low, block, other), jnp.where(low, other, block)], axis=0
        )
        bit *= 2
    return block


def gather_quad(block, deep):
    q = lax.axis_index("quad")
    h = lax.axis_index("head")
    bit_one, bit_two = 1 << h, 2 >> h
    other = quad_step(block, deep, False)
    both = jnp.stack([block, other])
    far = quad_step(both, deep, True)
    full = jnp.zeros((deep, QUAD) + block.shape[1:], block.dtype)
    for piece, place in (
        (block, q),
        (other, q ^ bit_one),
        (far[0], q ^ bit_two),
        (far[1], q ^ 3),
    ):
        full = lax.dynamic_update_slice(full, piece[:, None], (0, place, 0, 0))
    return full.reshape(-1, block.shape[-1])


def pack_small(small):
    high = lax.reduce_precision(small, 8, 7)
    return jnp.concatenate([high, small - high]).astype(jnp.bfloat16)


def unpack_small(packed):
    rows = packed.shape[0] // 2
    return packed[:rows].astype(jnp.float32) + packed[rows:].astype(jnp.float32)


def exchange(send, small, step):
    message = jnp.concatenate([send.astype(jnp.bfloat16), pack_small(small)], axis=0)
    answer = step(message)
    return answer[: send.shape[0]], small + unpack_small(answer[send.shape[0] :])


def scatter_sum(total, small, deep):
    q = lax.axis_index("quad")
    h = lax.axis_index("head")
    z = lax.axis_index("deep")
    bit_one, bit_two = 1 << h, 2 >> h
    columns = total.shape[-1]
    rows = total.shape[0] // (deep * QUAD)
    cube = total.reshape(deep, QUAD, rows, columns)

    def slab(place):
        return lax.dynamic_slice(cube, (0, place, 0, 0), (deep, 1, rows, columns)).reshape(
            deep * rows, columns
        )

    send = jnp.concatenate([slab(q ^ bit_one), slab(q ^ 3)], axis=0)
    got, small = exchange(send, small, lambda m: quad_step(m, deep, False))
    got = got.astype(jnp.float32)
    keep = slab(q) + got[: deep * rows]
    send = slab(q ^ bit_two) + got[deep * rows :]
    got, small = exchange(send, small, lambda m: quad_step(m, deep, True))
    keep = keep + got.astype(jnp.float32)
    bit = deep // 2
    while bit:
        span = bit * rows
        own = jnp.where((z & bit) == 0, 0, span)
        send = lax.dynamic_slice_in_dim(keep, span - own, span, 0)
        got, small = exchange(send, small, lambda m, bit=bit: deep_step(m, deep, bit))
        keep = lax.dynamic_slice_in_dim(keep, own, span, 0) + got.astype(jnp.float32)
        bit //= 2
    return keep, small


def scatter_offload(total):
    part = lax.psum_scatter(total.astype(jnp.bfloat16), "deep", scatter_dimension=0, tiled=True)
    return lax.psum_scatter(part, "quad", scatter_dimension=0, tiled=True).astype(jnp.float32)


def mm(left, right):
    return jnp.einsum("td,df->tf", left, right, preferred_element_type=jnp.float32)


def mm_nt(left, right):
    return jnp.einsum("tf,df->td", left, right, preferred_element_type=jnp.float32)


def mm_tn(left, right):
    return jnp.einsum("td,tf->df", left, right, preferred_element_type=jnp.float32)


def low(value):
    return value.astype(jnp.bfloat16)


def on_device(
    inputs,
    qkv_weight,
    qv_bias,
    out_weight,
    out_bias,
    first_gain,
    first_shift,
    up_weight,
    up_bias,
    down_weight,
    down_bias,
    second_gain,
    second_shift,
    item_lengths,
    random_blocks,
    out_grad,
):
    half, width = inputs.shape
    position = lax.axis_index("head")
    deep = lax.axis_size("deep")
    shard = qkv_weight.shape[0]
    head_width = qkv_weight.shape[2]
    up_width = up_weight.shape[1]
    half_blocks = half // BLK
    lengths = item_lengths[0]
    layout = jnp.concatenate([lengths, (position * half_blocks)[None].astype(jnp.int32)])
    randoms = random_blocks[0]

    tokens = jnp.concatenate([inputs, swap(inputs)], axis=0)
    qkv_deep = gather_deep(qkv_weight.reshape(shard, 3 * head_width), deep)
    rest_deep = gather_deep(jnp.concatenate([down_weight, out_weight, up_weight], axis=1), deep)
    full_qkv = gather_quad(qkv_deep, deep)
    rest_deep, full_qkv = lax.optimization_barrier((rest_deep, full_qkv))
    offload = lax.all_gather(
        rest_deep[:, :, up_width:].reshape(deep * shard, -1), "quad", axis=0, tiled=False
    )
    offload = jnp.swapaxes(offload.reshape(QUAD, deep, shard, -1), 0, 1).reshape(width, -1)
    full_out, full_up = offload[:, :head_width], offload[:, head_width:]
    full_down = gather_quad(rest_deep[:, :, :up_width], deep)

    bias = jnp.concatenate([qv_bias[0], jnp.zeros_like(qv_bias[0]), qv_bias[1]])
    triple = low(mm(tokens, full_qkv) + bias)
    attended = attention_forward(layout, randoms, triple)

    other = swap(low(mm_nt(attended[half:], full_out)))
    proj = mm_nt(attended[:half], full_out) + other.astype(jnp.float32)
    normed_one_out, normed_one, inverse_one = norm_forward(
        proj + out_bias + inputs.astype(jnp.float32), first_gain, first_shift
    )
    hidden_own = low(normed_one_out)
    hidden_other = swap(hidden_own)
    hidden = jnp.concatenate([hidden_own, hidden_other], axis=0)

    def gelu_tanh(values):
        return jax.nn.gelu(values, approximate=True)

    upper_own = low(mm(hidden_own, full_up) + up_bias)
    upper_other = low(mm(hidden_other, full_up) + up_bias)
    active_other = low(gelu_tanh(upper_other.astype(jnp.float32)))
    active_own = low(gelu_tanh(upper_own.astype(jnp.float32)))
    other = swap(low(mm_nt(active_other, full_down)))
    down = mm_nt(active_own, full_down) + other.astype(jnp.float32)
    active = jnp.concatenate([active_own, active_other], axis=0)
    normed_two_out, normed_two, inverse_two = norm_forward(
        down + down_bias + normed_one_out, second_gain, second_shift
    )
    row = position * half + lax.broadcasted_iota(jnp.int32, (half, 1), 0)
    live = (row < jnp.sum(lengths)).astype(jnp.float32)
    layer_out = low(normed_two_out * live)
    cotangent = out_grad.astype(jnp.float32) * live
    second_gain_part = jnp.sum(cotangent * normed_two, axis=0)
    second_shift_part = jnp.sum(cotangent, axis=0)
    grad_res_two = norm_backward(cotangent, normed_two, inverse_two, second_gain)
    down_bias_part = jnp.sum(grad_res_two, axis=0)
    grad_own = low(grad_res_two)
    grad_other = swap(grad_own)
    grad_down_rows = jnp.concatenate([grad_own, grad_other], axis=0)

    def pull(grad_rows, upper_rows):
        grad_active = mm(grad_rows, full_down)
        return low(jax.vjp(gelu_tanh, upper_rows.astype(jnp.float32))[1](grad_active)[0])

    grad_upper_own = pull(grad_own, upper_own)
    grad_upper_other = pull(grad_other, upper_other)
    grad_upper = jnp.concatenate([grad_upper_own, grad_upper_other], axis=0)
    down_local = low(mm_tn(grad_down_rows, active))
    up_bias_part = jnp.sum(grad_upper.astype(jnp.float32), axis=0)
    other = swap(low(mm_nt(grad_upper_other, full_up)))
    grad_norm_one = mm_nt(grad_upper_own, full_up) + other.astype(jnp.float32) + grad_res_two
    up_local = low(mm_tn(hidden, grad_upper))
    first_gain_part = jnp.sum(grad_norm_one * normed_one, axis=0)
    first_shift_part = jnp.sum(grad_norm_one, axis=0)
    grad_res_one = norm_backward(grad_norm_one, normed_one, inverse_one, first_gain)
    out_bias_part = jnp.sum(grad_res_one, axis=0)
    grad_proj_own = low(grad_res_one)
    grad_proj = jnp.concatenate([grad_proj_own, swap(grad_proj_own)], axis=0)
    grad_attended = low(mm(grad_proj, full_out))
    out_local = low(mm_tn(grad_proj, attended))
    grad_triple, bias_sums = attention_backward(layout, randoms, triple, grad_attended)

    other = swap(low(mm_nt(grad_triple[half:], full_qkv)))
    qkv_local = mm_tn(tokens, grad_triple)
    input_grad = low(mm_nt(grad_triple[:half], full_qkv) + other.astype(jnp.float32) + grad_res_one)

    grad_down = scatter_offload(down_local)
    grad_up = scatter_offload(up_local)
    grad_out = scatter_offload(out_local)

    shared = jnp.stack(
        [
            out_bias_part,
            first_gain_part,
            first_shift_part,
            down_bias_part,
            second_gain_part,
            second_shift_part,
        ]
    )
    shared = shared + swap(shared)
    small = jnp.concatenate([shared.reshape(-1), up_bias_part, bias_sums[:2].reshape(-1)])
    grad_qkv, small = scatter_sum(qkv_local, small.reshape(-1, 3 * head_width), deep)
    small = small.reshape(-1)
    count = shared.size
    totals = small[:count].reshape(shared.shape)
    grad_up_bias = small[count : count + up_width]
    grad_qv_bias = small[count + up_width :].reshape(2, head_width)
    return (
        layer_out,
        input_grad,
        grad_qkv.reshape(shard, 3, head_width),
        grad_qv_bias,
        grad_out,
        totals[0],
        totals[1],
        totals[2],
        grad_up,
        grad_up_bias,
        grad_down,
        totals[3],
        totals[4],
        totals[5],
    )


def solution(mesh):
    devices = mesh.devices.reshape(-1, QUAD, mesh.shape["head"])
    fine = Mesh(devices, ("deep", "quad", "head"))
    rows = ("deep", "quad", "head")
    dp = ("deep", "quad")
    in_specs = (
        P(rows, None),
        P(dp, None, "head"),
        P(None, "head"),
        P(dp, "head"),
        P(),
        P(),
        P(),
        P(dp, "head"),
        P("head"),
        P(dp, "head"),
        P(),
        P(),
        P(),
        P(dp, None),
        P(dp, "head", None, None),
        P(rows, None),
    )
    out_specs = (
        P(rows, None),
        P(rows, None),
        P(dp, None, "head"),
        P(None, "head"),
        P(dp, "head"),
        P(),
        P(),
        P(),
        P(dp, "head"),
        P("head"),
        P(dp, "head"),
        P(),
        P(),
        P(),
    )
    return jax.shard_map(
        on_device, mesh=fine, in_specs=in_specs, out_specs=out_specs, check_vma=False
    )
```

```python
import functools

import jax
import jax.numpy as jnp
import numpy as np
from jax import lax
from jax.experimental import pallas as pl
from jax.experimental.pallas import tpu as pltpu
from jax.sharding import Mesh
from jax.sharding import PartitionSpec as P

BLK = 64


norm_eps = 1e-06
negative = -1e30


def norm_forward(values, gain, shift):
    centered = values - jnp.mean(values, axis=-1, keepdims=True)
    inverse = lax.rsqrt(jnp.mean(centered * centered, axis=-1, keepdims=True) + norm_eps)
    normed = centered * inverse
    return (normed * gain + shift, normed, inverse)


def norm_backward(grad, normed, inverse, gain):
    scaled = grad * gain
    mean_one = jnp.mean(scaled, axis=-1, keepdims=True)
    mean_two = jnp.mean(scaled * normed, axis=-1, keepdims=True)
    return inverse * (scaled - mean_one - normed * mean_two)


def dot_nt(a, b):
    return lax.dot_general(a, b, (((1,), (1,)), ((), ())), preferred_element_type=jnp.float32)


def dot_nn(a, b):
    return lax.dot_general(a, b, (((1,), (0,)), ((), ())), preferred_element_type=jnp.float32)


def dot_tn(a, b):
    return lax.dot_general(a, b, (((0,), (0,)), ((), ())), preferred_element_type=jnp.float32)


PAIR = 2 * BLK


def even_lanes(rows):
    return lax.broadcasted_iota(jnp.int32, (rows, PAIR), 1) < BLK


def stacked(values):
    zero = jnp.zeros_like(values)
    even = even_lanes(BLK)
    return jnp.concatenate([jnp.where(even, values, zero), jnp.where(even, zero, values)], axis=0)


def unstacked(values):
    return jnp.where(even_lanes(BLK), values[:BLK], values[BLK:])


class Layout:
    def __init__(self, len_ref, rb_ref, blocks, position):
        self.len_ref, self.rb_ref, self.blocks = len_ref, rb_ref, blocks
        self.half = blocks // 2
        self.rand = rb_ref.shape[-1]
        self.shift = position * self.half

    def moved(self, index):
        at = index + self.shift
        return jnp.where(at >= self.blocks, at - self.blocks, at)

    def spot(self, index):
        return pl.ds(pl.multiple_of(self.moved(index) * BLK, BLK), BLK)

    def part(self, index):
        return pl.ds(pl.multiple_of(self.moved(index) * BLK, BLK), self.half * BLK)

    def locate(self, b):
        count0 = self.len_ref[0, 0] // BLK
        count1 = self.len_ref[0, 1] // BLK
        in0 = b < count0
        self.live = live = b < count0 + count1
        self.first = first = jnp.where(in0, 0, jnp.where(live, count0, b))
        items = jnp.where(in0, count0, jnp.where(live, count1, 1))
        rel = b - first
        last = items - 1
        self.chunks = items // self.half
        self.is_global = live & ((rel == 0) | (rel == last))
        zero, neg = jnp.float32(0.0), jnp.float32(negative)
        item_bias = jnp.where(live, zero, neg)
        self.fixed = [
            first,
            first + last,
            b,
            jnp.where(live, b - 1, b),
            jnp.where(live, b + 1, b),
        ]
        self.bias = [
            item_bias,
            item_bias,
            zero,
            jnp.where(live & (rel > 1), zero, neg),
            jnp.where(live & (rel + 1 < last), zero, neg),
        ] + [item_bias] * self.rand
        self.b = b

    def chosen(self, head):
        return [
            jnp.where(self.live, self.first + self.rb_ref[0, head, self.b, k], self.b)
            for k in range(self.rand)
        ]


def gathered(ref, layout, column, picked):
    even = even_lanes(BLK)

    def rows(index):
        return ref[layout.spot(index), column : column + PAIR]

    return jnp.concatenate(
        [rows(i) for i in layout.fixed]
        + [jnp.where(even, rows(i), rows(j)) for i, j in zip(*picked)],
        axis=0,
    )


def attn_fwd_kernel(pairs, position, len_ref, rb_ref, tri_ref, out_ref):
    blocks = tri_ref.shape[0] // BLK
    scale = jnp.bfloat16(BLK**-0.5)
    layout = Layout(len_ref, rb_ref, blocks, position())

    def body(b, carry):
        layout.locate(b)
        here = layout.spot(b)

        def query_of(p):
            return stacked(tri_ref[here, p * 3 * PAIR : p * 3 * PAIR + PAIR]) * scale

        def put(p, mixed):
            out_ref[here, p * PAIR : (p + 1) * PAIR] = unstacked(mixed).astype(jnp.bfloat16)

        @pl.when(jnp.logical_not(layout.is_global))
        def sparse():
            lane = lax.broadcasted_iota(jnp.int32, (1, PAIR), 1) < BLK
            bias = layout.bias
            bias_row = jnp.concatenate(
                [jnp.where(lane, bias[2 * i], bias[2 * i + 1]) for i in range(len(bias) // 2)],
                axis=1,
            )
            for p in pairs:
                picked = [layout.chosen(2 * p), layout.chosen(2 * p + 1)]
                keys = gathered(tri_ref, layout, (3 * p + 1) * PAIR, picked)
                values = gathered(tri_ref, layout, (3 * p + 2) * PAIR, picked)
                scores = dot_nt(query_of(p), keys) + bias_row
                top = jnp.max(scores, axis=1, keepdims=True)
                expo = jnp.exp(scores - top)
                total = jnp.sum(expo, axis=1, keepdims=True)
                put(p, dot_nn(expo.astype(jnp.bfloat16), values) / total)

        @pl.when(layout.is_global)
        def dense():
            queries = [query_of(p) for p in pairs]

            def chunk(c, state):
                new = []
                at = layout.part(layout.first + c * layout.half)
                for query, p, (top, total, acc) in zip(queries, pairs, state):
                    keys = tri_ref[at, (3 * p + 1) * PAIR : (3 * p + 2) * PAIR]
                    values = tri_ref[at, (3 * p + 2) * PAIR : (3 * p + 3) * PAIR]
                    scores = dot_nt(query, keys)
                    higher = jnp.maximum(top, jnp.max(scores, axis=1, keepdims=True))
                    shrink = jnp.exp(top - higher)
                    expo = jnp.exp(scores - higher)
                    total = total * shrink + jnp.sum(expo, axis=1, keepdims=True)
                    acc = acc * shrink + dot_nn(expo.astype(jnp.bfloat16), values)
                    new.append((higher, total, acc))
                return tuple(new)

            column = jnp.zeros((PAIR, 1), jnp.float32)
            init = tuple(
                (column + negative, column, jnp.zeros((PAIR, PAIR), jnp.float32)) for _ in pairs
            )
            state = lax.fori_loop(0, layout.chunks, chunk, init)
            for p, (_, total, acc) in zip(pairs, state):
                put(p, acc / total)

        return carry

    lax.fori_loop(0, blocks, body, 0)


def attn_bwd_kernel(pairs, position, len_ref, rb_ref, tri_ref, grad_ref, out_ref, sum_ref, *accs):
    blocks = tri_ref.shape[0] // BLK
    scale = jnp.bfloat16(BLK**-0.5)
    back = BLK**-0.5
    layout = Layout(len_ref, rb_ref, blocks, position())
    count = len(pairs)
    key_acc, value_acc = accs[:count], accs[count:]
    for acc in accs:
        acc[...] = jnp.zeros_like(acc)

    def body(b, carry):
        layout.locate(b)
        here = layout.spot(b)

        def query_of(p):
            return stacked(tri_ref[here, p * 3 * PAIR : p * 3 * PAIR + PAIR]) * scale

        def grad_of(p):
            return stacked(grad_ref[here, p * PAIR : (p + 1) * PAIR])

        def put(i, grad_query):
            out_ref[here, i * 3 * PAIR : i * 3 * PAIR + PAIR] = unstacked(
                grad_query * back
            ).astype(jnp.bfloat16)

        @pl.when(jnp.logical_not(layout.is_global))
        def sparse():
            bias = layout.bias
            even = even_lanes(BLK)
            for i, p in enumerate(pairs):
                picked = [layout.chosen(2 * p), layout.chosen(2 * p + 1)]
                query, grad = query_of(p), grad_of(p)
                keys = gathered(tri_ref, layout, (3 * p + 1) * PAIR, picked)
                values = gathered(tri_ref, layout, (3 * p + 2) * PAIR, picked)
                scores = dot_nt(keys, query)
                scores = jnp.concatenate(
                    [scores[j * BLK : (j + 1) * BLK] + bias[j] for j in range(len(bias))], axis=0
                )
                top = jnp.max(scores, axis=0, keepdims=True)
                expo = jnp.exp(scores - top)
                probs = expo * (1.0 / jnp.sum(expo, axis=0, keepdims=True))
                grad_probs = dot_nt(values, grad)
                delta = jnp.sum(probs * grad_probs, axis=0, keepdims=True)
                grad_scores = (probs * (grad_probs - delta)).astype(jnp.bfloat16)
                put(i, dot_tn(grad_scores, keys))
                for acc, update in (
                    (key_acc[i], dot_nn(grad_scores, query)),
                    (value_acc[i], dot_nn(probs.astype(jnp.bfloat16), grad)),
                ):
                    pieces = [update[j * BLK : (j + 1) * BLK] for j in range(len(bias))]
                    for j, index in enumerate(layout.fixed):
                        acc[layout.spot(index), :] += pieces[j]
                    for j, (one, two) in enumerate(zip(*picked)):
                        piece = pieces[len(layout.fixed) + j]
                        zero = jnp.zeros_like(piece)
                        acc[layout.spot(one), :] += jnp.where(even, piece, zero)
                        acc[layout.spot(two), :] += jnp.where(even, zero, piece)

        @pl.when(layout.is_global)
        def dense():
            queries = [query_of(p) for p in pairs]
            grads = [grad_of(p) for p in pairs]

            def both(c, i, p):
                at = layout.part(layout.first + c * layout.half)
                keys = tri_ref[at, (3 * p + 1) * PAIR : (3 * p + 2) * PAIR]
                values = tri_ref[at, (3 * p + 2) * PAIR : (3 * p + 3) * PAIR]
                return at, keys, dot_nt(keys, queries[i]), dot_nt(values, grads[i])

            def first_pass(c, state):
                new = []
                for i, p in enumerate(pairs):
                    top, total, dot = state[i]
                    _, _, scores, grad_probs = both(c, i, p)
                    higher = jnp.maximum(top, jnp.max(scores, axis=0, keepdims=True))
                    shrink = jnp.exp(top - higher)
                    expo = jnp.exp(scores - higher)
                    total = total * shrink + jnp.sum(expo, axis=0, keepdims=True)
                    dot = dot * shrink + jnp.sum(expo * grad_probs, axis=0, keepdims=True)
                    new.append((higher, total, dot))
                return tuple(new)

            row = jnp.zeros((1, PAIR), jnp.float32)
            state = lax.fori_loop(
                0, layout.chunks, first_pass, tuple((row + negative, row, row) for _ in pairs)
            )

            def second_pass(c, grad_queries):
                new = []
                for i, p in enumerate(pairs):
                    top, total, dot = state[i]
                    inverse = 1.0 / total
                    at, keys, scores, grad_probs = both(c, i, p)
                    probs = jnp.exp(scores - top) * inverse
                    grad_scores = (probs * (grad_probs - dot * inverse)).astype(jnp.bfloat16)
                    new.append(grad_queries[i] + dot_tn(grad_scores, keys))
                    key_acc[i][at, :] += dot_nn(grad_scores, queries[i])
                    value_acc[i][at, :] += dot_nn(probs.astype(jnp.bfloat16), grads[i])
                return tuple(new)

            grad_queries = lax.fori_loop(
                0,
                layout.chunks,
                second_pass,
                tuple(jnp.zeros((PAIR, PAIR), jnp.float32) for _ in pairs),
            )
            for i, grad_query in enumerate(grad_queries):
                put(i, grad_query)

        return carry

    lax.fori_loop(0, blocks, body, 0)
    sum_ref[...] = jnp.zeros_like(sum_ref)
    for i in range(count):
        at = i * 3 * PAIR
        column = slice(i * PAIR, (i + 1) * PAIR)
        query_grads = out_ref[:, at : at + PAIR].astype(jnp.float32)
        sum_ref[0:1, column] = jnp.sum(query_grads, axis=0, keepdims=True)
        out_ref[:, at + PAIR : at + 2 * PAIR] = key_acc[i][...].astype(jnp.bfloat16)
        value = value_acc[i][...].astype(jnp.bfloat16)
        out_ref[:, at + 2 * PAIR : at + 3 * PAIR] = value
        sum_ref[1:2, column] = jnp.sum(value.astype(jnp.float32), axis=0, keepdims=True)


vmem = pl.BlockSpec(memory_space=pltpu.VMEM)
smem = pl.BlockSpec(memory_space=pltpu.SMEM)
VMEM_LIMIT = 60 << 20


def attention_forward(lengths, randoms, triple, position):
    pairs = randoms.shape[1] // 2
    rows = triple.shape[0]
    area = rows * rows // 3 * 2 * pairs
    return pl.pallas_call(
        functools.partial(attn_fwd_kernel, range(pairs), position),
        out_shape=jax.ShapeDtypeStruct((rows, pairs * PAIR), jnp.bfloat16),
        in_specs=[smem, smem, vmem],
        out_specs=vmem,
        name="attend_forward",
        cost_estimate=pl.CostEstimate(
            flops=16 * area * PAIR, transcendentals=area, bytes_accessed=rows * pairs * PAIR * 8
        ),
        compiler_params=pltpu.CompilerParams(vmem_limit_bytes=VMEM_LIMIT),
    )(lengths, randoms, triple)


def attention_backward(lengths, randoms, triple, grad, pairs, position):
    rows = triple.shape[0]
    count = len(pairs)
    area = rows * rows // 3 * 2 * count
    return pl.pallas_call(
        functools.partial(attn_bwd_kernel, pairs, position),
        out_shape=(
            jax.ShapeDtypeStruct((rows, count * 3 * PAIR), jnp.bfloat16),
            jax.ShapeDtypeStruct((8, count * PAIR), jnp.float32),
        ),
        in_specs=[smem, smem, vmem, vmem],
        out_specs=(vmem, vmem),
        name="attend_backward",
        scratch_shapes=[pltpu.VMEM((rows, PAIR), jnp.float32)] * (2 * count),
        cost_estimate=pl.CostEstimate(
            flops=40 * area * PAIR, transcendentals=area, bytes_accessed=rows * count * PAIR * 20
        ),
        compiler_params=pltpu.CompilerParams(vmem_limit_bytes=VMEM_LIMIT),
    )(lengths, randoms, triple, grad)


QUAD = 4


def group_permute(value, deep, target):
    pairs = []
    for z in range(deep):
        for q in range(QUAD):
            for h in range(2):
                to_z, to_q = target(z, q, h)
                pairs.append(((z * QUAD + q) * 2 + h, (to_z * QUAD + to_q) * 2 + h))
    return lax.ppermute(value, ("deep", "quad", "head"), pairs)


def deep_step(value, deep, bit):
    return group_permute(value, deep, lambda z, q, h: (z ^ bit, q))


def quad_step(value, deep, second):
    return group_permute(value, deep, lambda z, q, h: (z, q ^ ((2 >> h) if second else (1 << h))))


def swap(value):
    return lax.ppermute(value, "head", [(0, 1), (1, 0)])


def after(value, *others):
    return lax.optimization_barrier((value,) + others)[0]


class Spot:
    def __init__(self):
        self.z, self.q, self.h = (lax.axis_index(a) for a in ("deep", "quad", "head"))
        self.deep = lax.axis_size("deep")
        one, two = 1 << self.h, 2 >> self.h
        self.places = [self.q, self.q ^ one, self.q ^ two, self.q ^ 3]


def gather_deep(value, spot):
    direct = min(spot.deep, 4)
    blocks = [value] + [deep_step(value, spot.deep, k) for k in range(1, direct)]
    block = jnp.stack(blocks)
    bit = direct
    while bit < spot.deep:
        block = jnp.concatenate([block, deep_step(block, spot.deep, bit)])
        bit *= 2
    return block


def place_kernel(deep, windows, at_ref, *refs):
    pieces = refs[:3]
    outs = refs[3:]
    rows = pieces[0].shape[1]
    for k in range(deep):
        for j in range(QUAD):
            ref = pieces[j] if j < 2 else pieces[2].at[j - 2]
            row = pl.multiple_of(((at_ref[QUAD] ^ k) * QUAD + at_ref[j]) * rows, rows)
            for out, (low, high) in zip(outs, windows):
                out[pl.ds(row, rows), :] = ref[k, :, low:high]


def place(spot, pieces, widths):
    windows, low = [], 0
    for width in widths:
        windows.append((low, low + width))
        low += width
    deep, rows = pieces[0].shape[:2]
    at = jnp.stack(spot.places + [spot.z]).astype(jnp.int32)
    if rows % 16:
        order = jnp.stack([pieces[0], pieces[1], pieces[2][0], pieces[2][1]])
        full = jnp.zeros((deep, QUAD, rows, low), order.dtype)
        for k in range(deep):
            for j in range(QUAD):
                full = lax.dynamic_update_slice(
                    full, order[j, k][None, None], (spot.z ^ k, spot.places[j], 0, 0)
                )
        full = full.reshape(-1, low)
        return [full[:, a:b] for a, b in windows]
    return pl.pallas_call(
        functools.partial(place_kernel, deep, windows),
        out_shape=[
            jax.ShapeDtypeStruct((deep * QUAD * rows, width), pieces[0].dtype) for width in widths
        ],
        in_specs=[smem] + [vmem] * 3,
        out_specs=[vmem] * len(widths),
        compiler_params=pltpu.CompilerParams(vmem_limit_bytes=VMEM_LIMIT),
        name="place_pieces",
    )(at, *pieces)


def slabs(total, spot, places):
    rows = total.shape[0] // (spot.deep * QUAD)
    columns = total.shape[1]
    cube = total.reshape(spot.deep, QUAD, rows, columns)
    return [
        lax.dynamic_slice(cube, (0, p, 0, 0), (spot.deep, 1, rows, columns)).reshape(
            spot.deep * rows, columns
        )
        for p in places
    ]


def first_send(totals, spot):
    parts = [slabs(t, spot, [spot.places[1], spot.places[3]]) for t in totals]
    return jnp.concatenate([jnp.concatenate(p, axis=0) for p in parts], axis=1)


def second_send(totals, spot, got):
    rows = got.shape[0] // 2
    far = jnp.concatenate([slabs(t, spot, [spot.places[2]])[0] for t in totals], axis=1)
    return low(far.astype(jnp.float32) + got[rows:].astype(jnp.float32))


def quad_sum(totals, spot, got, got_two):
    rows = got_two.shape[0]
    own = jnp.concatenate([slabs(t, spot, [spot.places[0]])[0] for t in totals], axis=1)
    return (
        own.astype(jnp.float32) + got[:rows].astype(jnp.float32) + got_two.astype(jnp.float32)
    )


def deep_sends(total, spot, small=None):
    bit = spot.deep // 2
    rows = total.shape[0] // spot.deep
    while bit >= 4:
        span = bit * rows
        own = jnp.where((spot.z & bit) == 0, 0, span)
        send = low(lax.dynamic_slice_in_dim(total, span - own, span, 0))
        if small is not None:
            send = jnp.concatenate([send, pack_small(small)], axis=0)
        got = deep_step(send, spot.deep, bit)
        if small is not None:
            small = small + unpack_small(got[span:])
        total = lax.dynamic_slice_in_dim(total, own, span, 0) + got[:span].astype(jnp.float32)
        bit //= 2
    direct = min(spot.deep, 4)
    place = spot.z % direct

    def piece(k):
        return lax.dynamic_slice_in_dim(total, (place ^ k) * rows, rows, 0)

    packed = [] if small is None else [pack_small(small)]
    messages = [
        jnp.concatenate([low(piece(k))] + packed, axis=0) for k in range(1, direct)
    ]
    return piece(0), small, messages


def deep_finish(own, small, answers):
    rows = own.shape[0]
    for answer in answers:
        own = own + answer[:rows].astype(jnp.float32)
        if small is not None:
            small = small + unpack_small(answer[rows:])
    return own, small


def pack_small(small):
    high = lax.reduce_precision(small, 8, 7)
    return jnp.concatenate([high, small - high]).astype(jnp.bfloat16)


def unpack_small(packed):
    rows = packed.shape[0] // 2
    return packed[:rows].astype(jnp.float32) + packed[rows:].astype(jnp.float32)


def mm(left, right):
    return jnp.einsum("td,df->tf", left, right, preferred_element_type=jnp.float32)


def mm_nt(left, right):
    return jnp.einsum("tf,df->td", left, right, preferred_element_type=jnp.float32)


def mm_tn(left, right):
    return jnp.einsum("td,tf->df", left, right, preferred_element_type=jnp.float32)


def low(value):
    return value.astype(jnp.bfloat16)


def by_pair(value):
    lead, kinds, columns = value.shape[:-2], value.shape[-2], value.shape[-1]
    split = value.reshape(lead + (kinds, columns // PAIR, PAIR))
    return jnp.swapaxes(split, -3, -2).reshape(lead + (kinds * columns,))


def by_kind(value, kinds):
    lead, columns = value.shape[:-1], value.shape[-1]
    split = value.reshape(lead + (columns // (kinds * PAIR), kinds, PAIR))
    return jnp.swapaxes(split, -3, -2).reshape(lead + (kinds, columns // kinds))


def on_device(
    inputs,
    qkv_weight,
    qv_bias,
    out_weight,
    out_bias,
    first_gain,
    first_shift,
    up_weight,
    up_bias,
    down_weight,
    down_bias,
    second_gain,
    second_shift,
    item_lengths,
    random_blocks,
    out_grad,
):
    half, width = inputs.shape
    spot = Spot()
    deep = spot.deep
    shard = qkv_weight.shape[0]
    head_width = qkv_weight.shape[2]
    up_width = up_weight.shape[1]
    pair_count = head_width // PAIR

    def position():
        return lax.axis_index("head")

    qkv_deep = gather_deep(by_pair(qkv_weight), spot)
    tokens = jnp.concatenate([inputs, swap(inputs)], axis=0)
    mid = jnp.concatenate([out_weight, up_weight], axis=1)

    def first_quad(block):
        return quad_step(block, deep, False)

    def second_quad(block, other):
        return quad_step(jnp.stack([block, other]), deep, True)

    mid, qkv_deep = lax.optimization_barrier((mid, qkv_deep))
    qkv_other = first_quad(qkv_deep)
    mid_deep = gather_deep(mid, spot)
    qkv_far = second_quad(qkv_deep, qkv_other)
    (full_qkv,) = place(spot, (qkv_deep, qkv_other, qkv_far), [3 * head_width])
    mid_deep, full_qkv = lax.optimization_barrier((mid_deep, full_qkv))
    mid_other = first_quad(mid_deep)
    down_deep = gather_deep(after(down_weight, mid_deep), spot)

    bias = by_pair(jnp.stack([qv_bias[0], jnp.zeros_like(qv_bias[0]), qv_bias[1]]))
    triple = low(mm(tokens, full_qkv) + bias)
    triple, mid_other, down_deep = lax.optimization_barrier((triple, mid_other, down_deep))
    mid_far = second_quad(mid_deep, mid_other)
    down_other = first_quad(down_deep)
    attended = attention_forward(item_lengths, random_blocks, triple, position)
    attended, mid_far, down_other = lax.optimization_barrier((attended, mid_far, down_other))
    down_far = second_quad(down_deep, down_other)
    full_out, full_up = place(spot, (mid_deep, mid_other, mid_far), [head_width, up_width])

    other = swap(low(mm_nt(attended[half:], full_out)))
    proj = mm_nt(attended[:half], full_out) + other.astype(jnp.float32)
    normed_one_out, normed_one, inverse_one = norm_forward(
        proj + out_bias + inputs.astype(jnp.float32), first_gain, first_shift
    )
    hidden_own = low(normed_one_out)
    hidden_other = swap(hidden_own)
    hidden = jnp.concatenate([hidden_own, hidden_other], axis=0)

    def gelu_tanh(values):
        return jax.nn.gelu(values, approximate=True)

    upper_own = low(mm(hidden_own, full_up) + up_bias)
    upper_other = low(mm(hidden_other, full_up) + up_bias)
    active_other = low(gelu_tanh(upper_other.astype(jnp.float32)))
    active_own = low(gelu_tanh(upper_own.astype(jnp.float32)))
    active_other, active_own, down_far = lax.optimization_barrier(
        (active_other, active_own, down_far)
    )
    (full_down,) = place(spot, (down_deep, down_other, down_far), [up_width])
    other = swap(low(mm_nt(active_other, full_down)))
    down = mm_nt(active_own, full_down) + other.astype(jnp.float32)
    active = jnp.concatenate([active_own, active_other], axis=0)
    normed_two_out, normed_two, inverse_two = norm_forward(
        down + down_bias + normed_one_out, second_gain, second_shift
    )
    row = spot.h * half + lax.broadcasted_iota(jnp.int32, (half, 1), 0)
    live = (row < jnp.sum(item_lengths)).astype(jnp.float32)
    layer_out = low(normed_two_out * live)
    cotangent = out_grad.astype(jnp.float32) * live
    second_gain_part = jnp.sum(cotangent * normed_two, axis=0)
    second_shift_part = jnp.sum(cotangent, axis=0)
    grad_res_two = norm_backward(cotangent, normed_two, inverse_two, second_gain)
    down_bias_part = jnp.sum(grad_res_two, axis=0)
    grad_own = low(grad_res_two)
    grad_other = swap(grad_own)
    grad_down_rows = jnp.concatenate([grad_own, grad_other], axis=0)

    down_local = low(mm_tn(grad_down_rows, active))
    down_got = first_quad(first_send([down_local], spot))

    def pull(grad_rows, upper_rows):
        grad_active = mm(grad_rows, full_down)
        return low(jax.vjp(gelu_tanh, upper_rows.astype(jnp.float32))[1](grad_active)[0])

    grad_other, grad_own, down_local = lax.optimization_barrier((grad_other, grad_own, down_local))
    grad_upper_other = pull(grad_other, upper_other)
    grad_upper_own = pull(grad_own, upper_own)
    grad_upper = jnp.concatenate([grad_upper_own, grad_upper_other], axis=0)
    up_bias_part = jnp.sum(grad_upper.astype(jnp.float32), axis=0)
    other = swap(low(mm_nt(grad_upper_other, full_up)))
    grad_norm_one = mm_nt(grad_upper_own, full_up) + other.astype(jnp.float32) + grad_res_two
    up_local = low(mm_tn(hidden, grad_upper))
    first_gain_part = jnp.sum(grad_norm_one * normed_one, axis=0)
    first_shift_part = jnp.sum(grad_norm_one, axis=0)
    grad_res_one = norm_backward(grad_norm_one, normed_one, inverse_one, first_gain)
    out_bias_part = jnp.sum(grad_res_one, axis=0)
    grad_proj_own = low(grad_res_one)
    grad_proj = jnp.concatenate([grad_proj_own, swap(grad_proj_own)], axis=0)
    grad_attended = low(mm(grad_proj, full_out))
    out_local = low(mm_tn(grad_proj, attended))

    mids = [out_local, up_local]
    grad_attended, down_got = lax.optimization_barrier((grad_attended, down_got))
    mid_got = first_quad(first_send(mids, spot))
    down_two = quad_step(second_send([down_local], spot, down_got), deep, True)
    shared = jnp.stack(
        [
            out_bias_part,
            first_gain_part,
            first_shift_part,
            down_bias_part,
            second_gain_part,
            second_shift_part,
        ]
    )
    shared = shared + swap(shared)

    split = pair_count - 1
    grads_a, sums_a = attention_backward(
        item_lengths, random_blocks, triple, grad_attended, range(split), position
    )
    grads_a, mid_got, down_two, grad_attended = lax.optimization_barrier(
        (grads_a, mid_got, down_two, grad_attended)
    )
    local_a = low(mm_tn(tokens, grads_a))
    got_a = first_quad(first_send([local_a], spot))
    mid_two = quad_step(second_send(mids, spot, mid_got), deep, True)
    down_own, _, messages = deep_sends(quad_sum([down_local], spot, down_got, down_two), spot)
    down_answers = [deep_step(m, deep, k + 1) for k, m in enumerate(messages)]
    grad_attended, local_a = lax.optimization_barrier((grad_attended, local_a))
    grads_b, sums_b = attention_backward(
        item_lengths, random_blocks, triple, grad_attended, range(split, pair_count), position
    )
    grads_b, got_a, mid_two, *down_answers = lax.optimization_barrier(
        (grads_b, got_a, mid_two, *down_answers)
    )

    def carry(send, small, step):
        message = jnp.concatenate([send, pack_small(small)], axis=0)
        answer = step(message)
        return answer[: send.shape[0]], small + unpack_small(answer[send.shape[0] :])

    sums = jnp.concatenate([sums_a[:2], sums_b[:2]], axis=1)
    small = jnp.concatenate([shared.reshape(-1), up_bias_part, sums.reshape(-1)])
    small = small.reshape(-1, 3 * PAIR)
    local_b = low(mm_tn(tokens, grads_b))
    got_b, small = carry(first_send([local_b], spot), small, first_quad)
    two_a = quad_step(second_send([local_a], spot, got_a), deep, True)
    mid_sum = after(quad_sum(mids, spot, mid_got, mid_two), local_b)
    mid_own, _, messages = deep_sends(mid_sum, spot)
    mid_answers = [deep_step(m, deep, k + 1) for k, m in enumerate(messages)]

    cut = split * 3 * PAIR
    grads_a, grads_b, local_b = lax.optimization_barrier((grads_a, grads_b, local_b))
    other = swap(
        low(mm_nt(grads_a[half:], full_qkv[:, :cut]) + mm_nt(grads_b[half:], full_qkv[:, cut:]))
    )
    mine = mm_nt(grads_a[:half], full_qkv[:, :cut]) + mm_nt(grads_b[:half], full_qkv[:, cut:])
    mine, other, got_b, two_a = lax.optimization_barrier((mine, other, got_b, two_a))
    two_b, small = carry(
        second_send([local_b], spot, got_b), small, lambda m: quad_step(m, deep, True)
    )
    input_grad = low(mine + other.astype(jnp.float32) + grad_res_one)
    sum_a = quad_sum([local_a], spot, got_a, two_a)
    grad_down, _ = deep_finish(down_own, None, down_answers)
    input_grad, sum_a, grad_down, two_b = lax.optimization_barrier(
        (input_grad, sum_a, grad_down, two_b)
    )
    qkv_sum = jnp.concatenate([sum_a, quad_sum([local_b], spot, got_b, two_b)], axis=1)
    small = small.reshape(-1, 3 * head_width)
    qkv_own, small, messages = deep_sends(qkv_sum, spot, small)
    answers = [deep_step(m, deep, k + 1) for k, m in enumerate(messages)]
    grad_mid, _ = deep_finish(mid_own, None, mid_answers)
    grad_mid, *answers = lax.optimization_barrier((grad_mid, *answers))
    grad_qkv, small = deep_finish(qkv_own, small, answers)
    grad_out, grad_up = grad_mid[:, :head_width], grad_mid[:, head_width:]

    small = small.reshape(-1)
    count = shared.size
    totals = small[:count].reshape(shared.shape)
    grad_up_bias = small[count : count + up_width]
    grad_qv_bias = small[count + up_width :].reshape(2, head_width)
    return (
        layer_out,
        input_grad,
        by_kind(grad_qkv, 3),
        grad_qv_bias,
        grad_out,
        totals[0],
        totals[1],
        totals[2],
        grad_up,
        grad_up_bias,
        grad_down,
        totals[3],
        totals[4],
        totals[5],
    )


def solution(mesh):
    devices = mesh.devices.reshape(-1, QUAD, mesh.shape["head"])
    fine = Mesh(devices, ("deep", "quad", "head"))
    rows = ("deep", "quad", "head")
    dp = ("deep", "quad")
    in_specs = (
        P(rows, None),
        P(dp, None, "head"),
        P(None, "head"),
        P(dp, "head"),
        P(),
        P(),
        P(),
        P(dp, "head"),
        P("head"),
        P(dp, "head"),
        P(),
        P(),
        P(),
        P(dp, None),
        P(dp, "head", None, None),
        P(rows, None),
    )
    out_specs = (
        P(rows, None),
        P(rows, None),
        P(dp, None, "head"),
        P(None, "head"),
        P(dp, "head"),
        P(),
        P(),
        P(),
        P(dp, "head"),
        P("head"),
        P(dp, "head"),
        P(),
        P(),
        P(),
    )
    return jax.shard_map(
        on_device, mesh=fine, in_specs=in_specs, out_specs=out_specs, check_vma=False
    )
```

```python
import functools

import jax
import jax.numpy as jnp
import numpy as np
from jax import lax
from jax.experimental import pallas as pl
from jax.experimental.pallas import tpu as pltpu
from jax.sharding import Mesh
from jax.sharding import PartitionSpec as P

BLK = 64


norm_eps = 1e-06
negative = -1e30


def norm_forward(values, gain, shift):
    centered = values - jnp.mean(values, axis=-1, keepdims=True)
    inverse = lax.rsqrt(jnp.mean(centered * centered, axis=-1, keepdims=True) + norm_eps)
    normed = centered * inverse
    return (normed * gain + shift, normed, inverse)


def norm_backward(grad, normed, inverse, gain):
    scaled = grad * gain
    mean_one = jnp.mean(scaled, axis=-1, keepdims=True)
    mean_two = jnp.mean(scaled * normed, axis=-1, keepdims=True)
    return inverse * (scaled - mean_one - normed * mean_two)


def dot_nt(a, b):
    return lax.dot_general(a, b, (((1,), (1,)), ((), ())), preferred_element_type=jnp.float32)


def dot_nn(a, b):
    return lax.dot_general(a, b, (((1,), (0,)), ((), ())), preferred_element_type=jnp.float32)


def dot_tn(a, b):
    return lax.dot_general(a, b, (((0,), (0,)), ((), ())), preferred_element_type=jnp.float32)


PAIR = 2 * BLK


def even_lanes(rows):
    return lax.broadcasted_iota(jnp.int32, (rows, PAIR), 1) < BLK


def stacked(values):
    zero = jnp.zeros_like(values)
    even = even_lanes(BLK)
    return jnp.concatenate([jnp.where(even, values, zero), jnp.where(even, zero, values)], axis=0)


def unstacked(values):
    return jnp.where(even_lanes(BLK), values[:BLK], values[BLK:])


class Layout:
    def __init__(self, len_ref, rb_ref, blocks, position):
        self.len_ref, self.rb_ref, self.blocks = len_ref, rb_ref, blocks
        self.half = blocks // 2
        self.rand = rb_ref.shape[-1]
        self.shift = position * self.half

    def moved(self, index):
        at = index + self.shift
        return jnp.where(at >= self.blocks, at - self.blocks, at)

    def spot(self, index):
        return pl.ds(pl.multiple_of(self.moved(index) * BLK, BLK), BLK)

    def part(self, index):
        return pl.ds(pl.multiple_of(self.moved(index) * BLK, BLK), self.half * BLK)

    def counts(self):
        self.count0 = lax.div(self.len_ref[0, 0], BLK)
        self.count1 = lax.div(self.len_ref[0, 1], BLK)
        self.second = jnp.where(self.count1 > 0, 1, 0)
        self.inner = self.blocks - 2 - 2 * self.second

    def locate(self, i):
        in0 = i < self.count0 - 2
        self.b = b = jnp.where(in0, i + 1, i + 2 + self.second)
        self.live = live = b < self.count0 + self.count1
        self.first = first = jnp.where(in0, 0, jnp.where(live, self.count0, b))
        items = jnp.where(in0, self.count0, jnp.where(live, self.count1, 1))
        rel = b - first
        last = items - 1
        zero, neg = jnp.float32(0.0), jnp.float32(negative)
        self.fixed = [
            first,
            first + last,
            jnp.where(live, b - 1, b),
            jnp.where(live, b + 1, b),
            b,
        ]
        self.low_bias = jnp.where(live & (rel == 1), neg, zero)
        self.high_bias = jnp.where(live & (rel + 1 == last), neg, zero)
        return self

    def ends(self, item):
        first = jnp.where(item == 0, 0, self.count0)
        count = jnp.where(item == 0, self.count0, self.count1)
        return first, first + count - 1, lax.div(count, self.half)

    def chosen(self, head):
        return [
            jnp.where(self.live, self.first + self.rb_ref[0, head, self.b, k], self.b)
            for k in range(self.rand)
        ]


def gathered(ref, layout, column, picked):
    even = even_lanes(BLK)

    def rows(index):
        return ref[layout.spot(index), column : column + PAIR]

    return jnp.concatenate(
        [rows(i) for i in layout.fixed]
        + [jnp.where(even, rows(i), rows(j)) for i, j in zip(*picked)],
        axis=0,
    )


ROWS = 32


def soft_rows(held):
    probs, inverse = [], []
    for row in range(0, held.shape[0], ROWS):
        scores = held[row : row + ROWS, :]
        expo = jnp.exp(scores - jnp.max(scores, axis=1, keepdims=True))
        inverse.append(1.0 / jnp.sum(expo, axis=1, keepdims=True))
        probs.append(expo.astype(jnp.bfloat16))
    return jnp.concatenate(probs, axis=0), jnp.concatenate(inverse, axis=0)


def attn_fwd_kernel(pairs, position, len_ref, rb_ref, tri_ref, out_ref, wide, *held):
    blocks = tri_ref.shape[0] // BLK
    scale = jnp.bfloat16(BLK**-0.5)
    layout = Layout(len_ref, rb_ref, blocks, position())
    layout.counts()

    def query_of(p, b):
        at = layout.spot(b)
        return stacked(tri_ref[at, p * 3 * PAIR : p * 3 * PAIR + PAIR]) * scale

    def put(p, b, mixed):
        at = layout.spot(b)
        out_ref[at, p * PAIR : (p + 1) * PAIR] = unstacked(mixed).astype(jnp.bfloat16)

    def sparse_scores(i, held):
        at = layout.locate(i)
        lane = lax.broadcasted_iota(jnp.int32, (1, PAIR), 1) < BLK
        bias_row = jnp.where(lane, at.low_bias, at.high_bias)
        for n, p in enumerate(pairs):
            picked = [at.chosen(2 * p), at.chosen(2 * p + 1)]
            keys = gathered(tri_ref, at, (3 * p + 1) * PAIR, picked)
            scores = dot_nt(query_of(p, at.b), keys)
            held[n][...] = jnp.concatenate(
                [scores[:, :PAIR], scores[:, PAIR : 2 * PAIR] + bias_row, scores[:, 2 * PAIR :]],
                axis=1,
            )

    def sparse_mix(i, held):
        at = layout.locate(i)
        for n, p in enumerate(pairs):
            picked = [at.chosen(2 * p), at.chosen(2 * p + 1)]
            probs, inverse = soft_rows(held[n])
            values = gathered(tri_ref, at, (3 * p + 2) * PAIR, picked)
            put(p, at.b, dot_nn(probs, values) * inverse)

    held_a, held_b = held[: len(pairs)], held[len(pairs) :]
    sparse_scores(0, held_a)

    def two(j, carry):
        sparse_scores(2 * j + 1, held_b)
        sparse_mix(2 * j, held_a)
        sparse_scores(jnp.minimum(2 * j + 2, layout.inner - 1), held_a)
        sparse_mix(2 * j + 1, held_b)
        return carry

    lax.fori_loop(0, lax.div(layout.inner, 2), two, 0)

    def dense(item, carry):
        first, last, chunks = layout.ends(item)
        queries = [
            jnp.concatenate([query_of(p, first), query_of(p, last)], axis=0) for p in pairs
        ]

        def dense_of(spans):
            for query, p in zip(queries, pairs):
                span = layout.half * BLK
                for c, at in enumerate(spans):
                    keys = tri_ref[at, (3 * p + 1) * PAIR : (3 * p + 2) * PAIR]
                    wide[:, c * span : (c + 1) * span] = dot_nt(query, keys)
                probs, inverse = soft_rows(wide.at[:, : len(spans) * span])
                mixed = sum(
                    dot_nn(
                        probs[:, c * span : (c + 1) * span],
                        tri_ref[at, (3 * p + 2) * PAIR : (3 * p + 3) * PAIR],
                    )
                    for c, at in enumerate(spans)
                ) * inverse
                put(p, first, mixed[:PAIR])
                put(p, last, mixed[PAIR:])

        @pl.when(chunks == 1)
        def short():
            dense_of([layout.part(first)])

        @pl.when(chunks == 2)
        def long():
            dense_of([layout.part(first), layout.part(first + layout.half)])

        return carry

    lax.fori_loop(0, 1 + layout.second, dense, 0)


def grad_rows(held_scores, held_grads, probs_ref, grads_ref):
    for row in range(0, held_scores.shape[0], ROWS):
        at = slice(row, row + ROWS)
        scores = held_scores[at, :]
        grad_probs = held_grads[at, :]
        expo = jnp.exp(scores - jnp.max(scores, axis=1, keepdims=True))
        probs = expo * (1.0 / jnp.sum(expo, axis=1, keepdims=True))
        delta = jnp.sum(probs * grad_probs, axis=1, keepdims=True)
        probs_ref[at, :] = probs.astype(jnp.bfloat16)
        grads_ref[at, :] = (probs * (grad_probs - delta)).astype(jnp.bfloat16)


def attn_bwd_kernel(
    pairs, position, len_ref, rb_ref, tri_ref, grad_ref, out_ref, sum_ref, *scratch
):
    blocks = tri_ref.shape[0] // BLK
    scale = jnp.bfloat16(BLK**-0.5)
    back = BLK**-0.5
    layout = Layout(len_ref, rb_ref, blocks, position())
    layout.counts()
    count = len(pairs)
    key_acc, value_acc = scratch[:count], scratch[count : 2 * count]
    held_a, held_b, done = (scratch[n * count : (n + 2) * count] for n in (2, 4, 6))
    wide = scratch[8 * count :]

    def clear(r, carry):
        at = pl.ds(pl.multiple_of(r * BLK, BLK), BLK)
        for acc in scratch[: 2 * count]:
            acc[at, :] = jnp.zeros((BLK, PAIR), jnp.float32)
        return carry

    lax.fori_loop(0, blocks, clear, 0)

    def query_of(p, b):
        at = layout.spot(b)
        return stacked(tri_ref[at, p * 3 * PAIR : p * 3 * PAIR + PAIR]) * scale

    def grad_of(p, b):
        at = layout.spot(b)
        return stacked(grad_ref[at, p * PAIR : (p + 1) * PAIR])

    def put(i, b, grad_query):
        out_ref[layout.spot(b), i * 3 * PAIR : i * 3 * PAIR + PAIR] = unstacked(
            grad_query * back
        ).astype(jnp.bfloat16)

    def sparse_scores(n, held):
        at = layout.locate(n)
        lane = lax.broadcasted_iota(jnp.int32, (1, PAIR), 1) < BLK
        bias_row = jnp.where(lane, at.low_bias, at.high_bias)
        for i, p in enumerate(pairs):
            picked = [at.chosen(2 * p), at.chosen(2 * p + 1)]
            keys = gathered(tri_ref, at, (3 * p + 1) * PAIR, picked)
            values = gathered(tri_ref, at, (3 * p + 2) * PAIR, picked)
            scores = dot_nt(query_of(p, at.b), keys)
            held[2 * i][...] = jnp.concatenate(
                [scores[:, :PAIR], scores[:, PAIR : 2 * PAIR] + bias_row, scores[:, 2 * PAIR :]],
                axis=1,
            )
            held[2 * i + 1][...] = dot_nt(grad_of(p, at.b), values)

    def sparse_grads(n, held):
        at = layout.locate(n)
        even = even_lanes(BLK)
        for i, p in enumerate(pairs):
            grad_rows(held[2 * i], held[2 * i + 1], done[2 * i], done[2 * i + 1])
            picked = [at.chosen(2 * p), at.chosen(2 * p + 1)]
            spots = [at.spot(index) for index in at.fixed]
            spots += [(at.spot(one), at.spot(two)) for one, two in zip(*picked)]
            keys = gathered(tri_ref, at, (3 * p + 1) * PAIR, picked)
            put(i, at.b, dot_nn(done[2 * i + 1][...], keys))
            for acc, update in (
                (key_acc[i], dot_tn(done[2 * i + 1][...], query_of(p, at.b))),
                (value_acc[i], dot_tn(done[2 * i][...], grad_of(p, at.b))),
            ):
                for j, spot in enumerate(spots):
                    piece = update[j * BLK : (j + 1) * BLK]
                    if j < len(at.fixed):
                        acc[spot, :] += piece
                    else:
                        zero = jnp.zeros_like(piece)
                        acc[spot[0], :] += jnp.where(even, piece, zero)
                        acc[spot[1], :] += jnp.where(even, zero, piece)

    sparse_scores(0, held_a)

    def two(j, carry):
        sparse_scores(2 * j + 1, held_b)
        sparse_grads(2 * j, held_a)
        sparse_scores(jnp.minimum(2 * j + 2, layout.inner - 1), held_a)
        sparse_grads(2 * j + 1, held_b)
        return carry

    lax.fori_loop(0, lax.div(layout.inner, 2), two, 0)

    wide_scores, wide_grads, wide_probs, wide_out = wide

    def dense(item, carry):
        first, last, chunks = layout.ends(item)

        def dense_of(spans):
            span = layout.half * BLK
            cover = len(spans) * span
            def end(n, carry):
                b = jnp.where(n == 0, first, last)
                for i, p in enumerate(pairs):
                    query, grad = query_of(p, b), grad_of(p, b)
                    for c, at in enumerate(spans):
                        cut = slice(c * span, (c + 1) * span)
                        keys = tri_ref[at, (3 * p + 1) * PAIR : (3 * p + 2) * PAIR]
                        values = tri_ref[at, (3 * p + 2) * PAIR : (3 * p + 3) * PAIR]
                        wide_scores[:, cut] = dot_nt(query, keys)
                        wide_grads[:, cut] = dot_nt(grad, values)
                    grad_rows(*(ref.at[:, :cover] for ref in wide))
                    total = jnp.zeros((PAIR, PAIR), jnp.float32)
                    for c, at in enumerate(spans):
                        cut = slice(c * span, (c + 1) * span)
                        keys = tri_ref[at, (3 * p + 1) * PAIR : (3 * p + 2) * PAIR]
                        total += dot_nn(wide_out[:, cut], keys)
                        key_acc[i][at, :] += dot_tn(wide_out[:, cut], query)
                        value_acc[i][at, :] += dot_tn(wide_probs[:, cut], grad)
                    put(i, b, total)
                return carry

            lax.fori_loop(0, 2, end, 0)

        @pl.when(chunks == 1)
        def short():
            dense_of([layout.part(first)])

        @pl.when(chunks == 2)
        def long():
            dense_of([layout.part(first), layout.part(first + layout.half)])

        return carry

    lax.fori_loop(0, 1 + layout.second, dense, 0)

    sum_ref[...] = jnp.zeros_like(sum_ref)

    def finish(r, carry):
        at = pl.ds(pl.multiple_of(r * BLK, BLK), BLK)
        new = []
        for i in range(count):
            column = i * 3 * PAIR
            query_sum, value_sum = carry[i]
            out_ref[at, column + PAIR : column + 2 * PAIR] = key_acc[i][at, :].astype(jnp.bfloat16)
            value = value_acc[i][at, :].astype(jnp.bfloat16)
            out_ref[at, column + 2 * PAIR : column + 3 * PAIR] = value
            query = out_ref[at, column : column + PAIR].astype(jnp.float32)
            new.append(
                tuple(
                    total + jnp.sum(part.reshape(-1, 8, PAIR), axis=0)
                    for total, part in (
                        (query_sum, query),
                        (value_sum, value.astype(jnp.float32)),
                    )
                )
            )
        return tuple(new)

    zero = jnp.zeros((8, PAIR), jnp.float32)
    sums = lax.fori_loop(0, blocks, finish, tuple((zero, zero) for _ in pairs))
    for i, totals in enumerate(sums):
        for kind, total in enumerate(totals):
            sum_ref[kind : kind + 1, i * PAIR : (i + 1) * PAIR] = jnp.sum(
                total, axis=0, keepdims=True
            )


vmem = pl.BlockSpec(memory_space=pltpu.VMEM)
smem = pl.BlockSpec(memory_space=pltpu.SMEM)
def attention_forward(lengths, randoms, triple, position):
    pairs = randoms.shape[1] // 2
    rows = triple.shape[0]
    area = rows * rows // 3 * 2 * pairs
    return pl.pallas_call(
        functools.partial(attn_fwd_kernel, range(pairs), position),
        out_shape=jax.ShapeDtypeStruct((rows, pairs * PAIR), jnp.bfloat16),
        in_specs=[smem, smem, vmem],
        out_specs=vmem,
        name="attend_forward",
        scratch_shapes=[pltpu.VMEM((2 * PAIR, rows), jnp.float32)]
        + [pltpu.VMEM((PAIR, 8 * BLK), jnp.float32)] * (2 * pairs),
        cost_estimate=pl.CostEstimate(
            flops=16 * area * PAIR, transcendentals=area, bytes_accessed=rows * pairs * PAIR * 8
        ),
        compiler_params=pltpu.CompilerParams(vmem_limit_bytes=8 << 20),
    )(lengths, randoms, triple)


def attention_backward(lengths, randoms, triple, grad, pairs, position):
    rows = triple.shape[0]
    count = len(pairs)
    area = rows * rows // 3 * 2 * count
    return pl.pallas_call(
        functools.partial(attn_bwd_kernel, pairs, position),
        out_shape=(
            jax.ShapeDtypeStruct((rows, count * 3 * PAIR), jnp.bfloat16),
            jax.ShapeDtypeStruct((8, count * PAIR), jnp.float32),
        ),
        in_specs=[smem, smem, vmem, vmem],
        out_specs=(vmem, vmem),
        name="attend_backward",
        scratch_shapes=[pltpu.VMEM((rows, PAIR), jnp.float32)] * (2 * count)
        + [pltpu.VMEM((PAIR, 8 * BLK), jnp.float32)] * (4 * count)
        + [pltpu.VMEM((PAIR, 8 * BLK), jnp.bfloat16)] * (2 * count)
        + [pltpu.VMEM((PAIR, rows), kind) for kind in (jnp.float32,) * 2 + (jnp.bfloat16,) * 2],
        cost_estimate=pl.CostEstimate(
            flops=40 * area * PAIR, transcendentals=area, bytes_accessed=rows * count * PAIR * 20
        ),
        compiler_params=pltpu.CompilerParams(vmem_limit_bytes=20 << 20),
    )(lengths, randoms, triple, grad)


QUAD = 4


def group_permute(value, deep, target):
    pairs = []
    for z in range(deep):
        for q in range(QUAD):
            for h in range(2):
                to_z, to_q = target(z, q, h)
                pairs.append(((z * QUAD + q) * 2 + h, (to_z * QUAD + to_q) * 2 + h))
    return lax.ppermute(value, ("deep", "quad", "head"), pairs)


def deep_step(value, deep, bit):
    return group_permute(value, deep, lambda z, q, h: (z ^ bit, q))


def quad_step(value, deep, second):
    return group_permute(value, deep, lambda z, q, h: (z, q ^ ((2 >> h) if second else (1 << h))))


def swap(value):
    return lax.ppermute(value, "head", [(0, 1), (1, 0)])


def after(value, *others):
    return lax.optimization_barrier((value,) + others)[0]


class Spot:
    def __init__(self):
        self.z, self.q, self.h = (lax.axis_index(a) for a in ("deep", "quad", "head"))
        self.deep = lax.axis_size("deep")
        one, two = 1 << self.h, 2 >> self.h
        self.places = [self.q, self.q ^ one, self.q ^ two, self.q ^ 3]


def gather_deep(value, spot):
    direct = min(spot.deep, 4)
    blocks = [value] + [deep_step(value, spot.deep, k) for k in range(1, direct)]
    block = jnp.stack(blocks)
    bit = direct
    while bit < spot.deep:
        block = jnp.concatenate([block, deep_step(block, spot.deep, bit)])
        bit *= 2
    return block


def place_kernel(deep, windows, at_ref, *refs):
    pieces = refs[:3]
    outs = refs[3:]
    rows = pieces[0].shape[1]
    for k in range(deep):
        for j in range(QUAD):
            ref = pieces[j] if j < 2 else pieces[2].at[j - 2]
            row = pl.multiple_of(((at_ref[QUAD] ^ k) * QUAD + at_ref[j]) * rows, rows)
            for out, (low, high) in zip(outs, windows):
                out[pl.ds(row, rows), :] = ref[k, :, low:high]


def place(spot, pieces, widths):
    windows, low = [], 0
    for width in widths:
        windows.append((low, low + width))
        low += width
    deep, rows = pieces[0].shape[:2]
    at = jnp.stack(spot.places + [spot.z]).astype(jnp.int32)
    if rows % 16:
        order = jnp.stack([pieces[0], pieces[1], pieces[2][0], pieces[2][1]])
        full = jnp.zeros((deep, QUAD, rows, low), order.dtype)
        for k in range(deep):
            for j in range(QUAD):
                full = lax.dynamic_update_slice(
                    full, order[j, k][None, None], (spot.z ^ k, spot.places[j], 0, 0)
                )
        full = full.reshape(-1, low)
        return [full[:, a:b] for a, b in windows]
    return pl.pallas_call(
        functools.partial(place_kernel, deep, windows),
        out_shape=[
            jax.ShapeDtypeStruct((deep * QUAD * rows, width), pieces[0].dtype) for width in widths
        ],
        in_specs=[smem] + [vmem] * 3,
        out_specs=[vmem] * len(widths),
        compiler_params=pltpu.CompilerParams(vmem_limit_bytes=8 << 20),
        name="place_pieces",
    )(at, *pieces)


def slabs(total, spot, places):
    rows = total.shape[0] // (spot.deep * QUAD)
    columns = total.shape[1]
    cube = total.reshape(spot.deep, QUAD, rows, columns)
    return [
        lax.dynamic_slice(cube, (0, p, 0, 0), (spot.deep, 1, rows, columns)).reshape(
            spot.deep * rows, columns
        )
        for p in places
    ]


def first_send(totals, spot):
    parts = [slabs(t, spot, [spot.places[1], spot.places[3]]) for t in totals]
    return jnp.concatenate([jnp.concatenate(p, axis=0) for p in parts], axis=1)


def second_send(totals, spot, got):
    rows = got.shape[0] // 2
    far = jnp.concatenate([slabs(t, spot, [spot.places[2]])[0] for t in totals], axis=1)
    return low(far.astype(jnp.float32) + got[rows:].astype(jnp.float32))


def quad_sum(totals, spot, got, got_two):
    rows = got_two.shape[0]
    own = jnp.concatenate([slabs(t, spot, [spot.places[0]])[0] for t in totals], axis=1)
    return (
        own.astype(jnp.float32) + got[:rows].astype(jnp.float32) + got_two.astype(jnp.float32)
    )


def deep_sends(total, spot, small=None):
    bit = spot.deep // 2
    rows = total.shape[0] // spot.deep
    while bit >= 4:
        span = bit * rows
        own = jnp.where((spot.z & bit) == 0, 0, span)
        send = low(lax.dynamic_slice_in_dim(total, span - own, span, 0))
        if small is not None:
            send = jnp.concatenate([send, pack_small(small)], axis=0)
        got = deep_step(send, spot.deep, bit)
        if small is not None:
            small = small + unpack_small(got[span:])
        total = lax.dynamic_slice_in_dim(total, own, span, 0) + got[:span].astype(jnp.float32)
        bit //= 2
    direct = min(spot.deep, 4)
    place = spot.z % direct

    def piece(k):
        return lax.dynamic_slice_in_dim(total, (place ^ k) * rows, rows, 0)

    packed = [] if small is None else [pack_small(small)]
    messages = [
        jnp.concatenate([low(piece(k))] + packed, axis=0) for k in range(1, direct)
    ]
    return piece(0), small, messages


def deep_finish(own, small, answers):
    rows = own.shape[0]
    for answer in answers:
        own = own + answer[:rows].astype(jnp.float32)
        if small is not None:
            small = small + unpack_small(answer[rows:])
    return own, small


def pack_small(small):
    high = lax.reduce_precision(small, 8, 7)
    return jnp.concatenate([high, small - high]).astype(jnp.bfloat16)


def unpack_small(packed):
    rows = packed.shape[0] // 2
    return packed[:rows].astype(jnp.float32) + packed[rows:].astype(jnp.float32)


def mm(left, right):
    return jnp.einsum("td,df->tf", left, right, preferred_element_type=jnp.float32)


def mm_nt(left, right):
    return jnp.einsum("tf,df->td", left, right, preferred_element_type=jnp.float32)


def mm_tn(left, right):
    return jnp.einsum("td,tf->df", left, right, preferred_element_type=jnp.float32)


def low(value):
    return value.astype(jnp.bfloat16)


def by_pair(value):
    lead, kinds, columns = value.shape[:-2], value.shape[-2], value.shape[-1]
    split = value.reshape(lead + (kinds, columns // PAIR, PAIR))
    return jnp.swapaxes(split, -3, -2).reshape(lead + (kinds * columns,))


def by_kind(value, kinds):
    lead, columns = value.shape[:-1], value.shape[-1]
    split = value.reshape(lead + (columns // (kinds * PAIR), kinds, PAIR))
    return jnp.swapaxes(split, -3, -2).reshape(lead + (kinds, columns // kinds))


def on_device(
    inputs,
    qkv_weight,
    qv_bias,
    out_weight,
    out_bias,
    first_gain,
    first_shift,
    up_weight,
    up_bias,
    down_weight,
    down_bias,
    second_gain,
    second_shift,
    item_lengths,
    random_blocks,
    out_grad,
):
    half, width = inputs.shape
    spot = Spot()
    deep = spot.deep
    shard = qkv_weight.shape[0]
    head_width = qkv_weight.shape[2]
    up_width = up_weight.shape[1]
    pair_count = head_width // PAIR

    def position():
        return lax.axis_index("head")

    qkv_deep = gather_deep(by_pair(qkv_weight), spot)
    tokens = jnp.concatenate([inputs, swap(inputs)], axis=0)
    mid = jnp.concatenate([out_weight, up_weight], axis=1)

    def first_quad(block):
        return quad_step(block, deep, False)

    def second_quad(block, other):
        return quad_step(jnp.stack([block, other]), deep, True)

    mid, qkv_deep = lax.optimization_barrier((mid, qkv_deep))
    qkv_other = first_quad(qkv_deep)
    mid_deep = gather_deep(mid, spot)
    qkv_far = second_quad(qkv_deep, qkv_other)
    (full_qkv,) = place(spot, (qkv_deep, qkv_other, qkv_far), [3 * head_width])
    mid_deep, full_qkv = lax.optimization_barrier((mid_deep, full_qkv))
    mid_other = first_quad(mid_deep)
    down_deep = gather_deep(after(down_weight, mid_deep), spot)

    bias = by_pair(jnp.stack([qv_bias[0], jnp.zeros_like(qv_bias[0]), qv_bias[1]]))
    triple = low(mm(tokens, full_qkv) + bias)
    triple, mid_other, down_deep = lax.optimization_barrier((triple, mid_other, down_deep))
    mid_far = second_quad(mid_deep, mid_other)
    down_other = first_quad(down_deep)
    attended = attention_forward(item_lengths, random_blocks, triple, position)
    attended, mid_far, down_other = lax.optimization_barrier((attended, mid_far, down_other))
    down_far = second_quad(down_deep, down_other)
    full_out, full_up = place(spot, (mid_deep, mid_other, mid_far), [head_width, up_width])

    other = swap(low(mm_nt(attended[half:], full_out)))
    proj = mm_nt(attended[:half], full_out) + other.astype(jnp.float32)
    normed_one_out, normed_one, inverse_one = norm_forward(
        proj + out_bias + inputs.astype(jnp.float32), first_gain, first_shift
    )
    hidden_own = low(normed_one_out)
    hidden_other = swap(hidden_own)
    hidden = jnp.concatenate([hidden_own, hidden_other], axis=0)

    def gelu_tanh(values):
        return jax.nn.gelu(values, approximate=True)

    upper_own = low(mm(hidden_own, full_up) + up_bias)
    upper_other = low(mm(hidden_other, full_up) + up_bias)
    active_other = low(gelu_tanh(upper_other.astype(jnp.float32)))
    active_own = low(gelu_tanh(upper_own.astype(jnp.float32)))
    active_other, active_own, down_far = lax.optimization_barrier(
        (active_other, active_own, down_far)
    )
    (full_down,) = place(spot, (down_deep, down_other, down_far), [up_width])
    other = swap(low(mm_nt(active_other, full_down)))
    down = mm_nt(active_own, full_down) + other.astype(jnp.float32)
    active = jnp.concatenate([active_own, active_other], axis=0)
    normed_two_out, normed_two, inverse_two = norm_forward(
        down + down_bias + normed_one_out, second_gain, second_shift
    )
    row = spot.h * half + lax.broadcasted_iota(jnp.int32, (half, 1), 0)
    live = (row < jnp.sum(item_lengths)).astype(jnp.float32)
    layer_out = low(normed_two_out * live)
    cotangent = out_grad.astype(jnp.float32) * live
    second_gain_part = jnp.sum(cotangent * normed_two, axis=0)
    second_shift_part = jnp.sum(cotangent, axis=0)
    grad_res_two = norm_backward(cotangent, normed_two, inverse_two, second_gain)
    down_bias_part = jnp.sum(grad_res_two, axis=0)
    grad_own = low(grad_res_two)
    grad_other = swap(grad_own)
    grad_down_rows = jnp.concatenate([grad_own, grad_other], axis=0)

    down_local = low(mm_tn(grad_down_rows, active))
    down_got = first_quad(first_send([down_local], spot))

    def pull(grad_rows, upper_rows):
        grad_active = mm(grad_rows, full_down)
        return low(jax.vjp(gelu_tanh, upper_rows.astype(jnp.float32))[1](grad_active)[0])

    grad_other, grad_own, down_local = lax.optimization_barrier((grad_other, grad_own, down_local))
    grad_upper_other = pull(grad_other, upper_other)
    grad_upper_own = pull(grad_own, upper_own)
    grad_upper = jnp.concatenate([grad_upper_own, grad_upper_other], axis=0)
    up_bias_part = jnp.sum(grad_upper.astype(jnp.float32), axis=0)
    other = swap(low(mm_nt(grad_upper_other, full_up)))
    grad_norm_one = mm_nt(grad_upper_own, full_up) + other.astype(jnp.float32) + grad_res_two
    up_local = low(mm_tn(hidden, grad_upper))
    first_gain_part = jnp.sum(grad_norm_one * normed_one, axis=0)
    first_shift_part = jnp.sum(grad_norm_one, axis=0)
    grad_res_one = norm_backward(grad_norm_one, normed_one, inverse_one, first_gain)
    out_bias_part = jnp.sum(grad_res_one, axis=0)
    grad_proj_own = low(grad_res_one)
    grad_proj = jnp.concatenate([grad_proj_own, swap(grad_proj_own)], axis=0)
    grad_attended = low(mm(grad_proj, full_out))
    out_local = low(mm_tn(grad_proj, attended))

    mids = [out_local, up_local]
    grad_attended, down_got = lax.optimization_barrier((grad_attended, down_got))
    mid_got = first_quad(first_send(mids, spot))
    down_two = quad_step(second_send([down_local], spot, down_got), deep, True)
    shared = jnp.stack(
        [
            out_bias_part,
            first_gain_part,
            first_shift_part,
            down_bias_part,
            second_gain_part,
            second_shift_part,
        ]
    )
    shared = shared + swap(shared)

    split = pair_count - 1
    grads_a, sums_a = attention_backward(
        item_lengths, random_blocks, triple, grad_attended, range(split), position
    )
    grads_a, mid_got, down_two, grad_attended = lax.optimization_barrier(
        (grads_a, mid_got, down_two, grad_attended)
    )
    local_a = low(mm_tn(tokens, grads_a))
    got_a = first_quad(first_send([local_a], spot))
    mid_two = quad_step(second_send(mids, spot, mid_got), deep, True)
    down_own, _, messages = deep_sends(quad_sum([down_local], spot, down_got, down_two), spot)
    down_answers = [deep_step(m, deep, k + 1) for k, m in enumerate(messages)]
    grad_attended, local_a = lax.optimization_barrier((grad_attended, local_a))
    grads_b, sums_b = attention_backward(
        item_lengths, random_blocks, triple, grad_attended, range(split, pair_count), position
    )
    grads_b, got_a, mid_two, *down_answers = lax.optimization_barrier(
        (grads_b, got_a, mid_two, *down_answers)
    )

    def carry(send, small, step):
        message = jnp.concatenate([send, pack_small(small)], axis=0)
        answer = step(message)
        return answer[: send.shape[0]], small + unpack_small(answer[send.shape[0] :])

    sums = jnp.concatenate([sums_a[:2], sums_b[:2]], axis=1)
    small = jnp.concatenate([shared.reshape(-1), up_bias_part, sums.reshape(-1)])
    small = small.reshape(-1, 3 * PAIR)
    local_b = low(mm_tn(tokens, grads_b))
    got_b, small = carry(first_send([local_b], spot), small, first_quad)
    two_a = quad_step(second_send([local_a], spot, got_a), deep, True)
    mid_sum = after(quad_sum(mids, spot, mid_got, mid_two), local_b)
    mid_own, _, messages = deep_sends(mid_sum, spot)
    mid_answers = [deep_step(m, deep, k + 1) for k, m in enumerate(messages)]

    cut = split * 3 * PAIR
    grads_a, grads_b, local_b = lax.optimization_barrier((grads_a, grads_b, local_b))
    other = swap(
        low(mm_nt(grads_a[half:], full_qkv[:, :cut]) + mm_nt(grads_b[half:], full_qkv[:, cut:]))
    )
    mine = mm_nt(grads_a[:half], full_qkv[:, :cut]) + mm_nt(grads_b[:half], full_qkv[:, cut:])
    mine, other, got_b, two_a = lax.optimization_barrier((mine, other, got_b, two_a))
    two_b, small = carry(
        second_send([local_b], spot, got_b), small, lambda m: quad_step(m, deep, True)
    )
    input_grad = low(mine + other.astype(jnp.float32) + grad_res_one)
    sum_a = quad_sum([local_a], spot, got_a, two_a)
    grad_down, _ = deep_finish(down_own, None, down_answers)
    input_grad, sum_a, grad_down, two_b = lax.optimization_barrier(
        (input_grad, sum_a, grad_down, two_b)
    )
    qkv_sum = jnp.concatenate([sum_a, quad_sum([local_b], spot, got_b, two_b)], axis=1)
    small = small.reshape(-1, 3 * head_width)
    qkv_own, small, messages = deep_sends(qkv_sum, spot, small)
    answers = [deep_step(m, deep, k + 1) for k, m in enumerate(messages)]
    grad_mid, _ = deep_finish(mid_own, None, mid_answers)
    grad_mid, *answers = lax.optimization_barrier((grad_mid, *answers))
    grad_qkv, small = deep_finish(qkv_own, small, answers)
    grad_out, grad_up = grad_mid[:, :head_width], grad_mid[:, head_width:]

    small = small.reshape(-1)
    count = shared.size
    totals = small[:count].reshape(shared.shape)
    grad_up_bias = small[count : count + up_width]
    grad_qv_bias = small[count + up_width :].reshape(2, head_width)
    return (
        layer_out,
        input_grad,
        by_kind(grad_qkv, 3),
        grad_qv_bias,
        grad_out,
        totals[0],
        totals[1],
        totals[2],
        grad_up,
        grad_up_bias,
        grad_down,
        totals[3],
        totals[4],
        totals[5],
    )


def solution(mesh):
    devices = mesh.devices.reshape(-1, QUAD, mesh.shape["head"])
    fine = Mesh(devices, ("deep", "quad", "head"))
    rows = ("deep", "quad", "head")
    dp = ("deep", "quad")
    in_specs = (
        P(rows, None),
        P(dp, None, "head"),
        P(None, "head"),
        P(dp, "head"),
        P(),
        P(),
        P(),
        P(dp, "head"),
        P("head"),
        P(dp, "head"),
        P(),
        P(),
        P(),
        P(dp, None),
        P(dp, "head", None, None),
        P(rows, None),
    )
    out_specs = (
        P(rows, None),
        P(rows, None),
        P(dp, None, "head"),
        P(None, "head"),
        P(dp, "head"),
        P(),
        P(),
        P(),
        P(dp, "head"),
        P("head"),
        P(dp, "head"),
        P(),
        P(),
        P(),
    )
    return jax.shard_map(
        on_device, mesh=fine, in_specs=in_specs, out_specs=out_specs, check_vma=False
    )
```

```python
import functools

import jax
import jax.numpy as jnp
import numpy as np
from jax import lax
from jax.experimental import pallas as pl
from jax.experimental.pallas import tpu as pltpu
from jax.sharding import Mesh
from jax.sharding import PartitionSpec as P

BLK = 64


norm_eps = 1e-06
negative = -1e30


def norm_forward(values, gain, shift):
    centered = values - jnp.mean(values, axis=-1, keepdims=True)
    inverse = lax.rsqrt(jnp.mean(centered * centered, axis=-1, keepdims=True) + norm_eps)
    normed = centered * inverse
    return (normed * gain + shift, normed, inverse)


def dot_nt(a, b):
    return lax.dot_general(a, b, (((1,), (1,)), ((), ())), preferred_element_type=jnp.float32)


def dot_nn(a, b):
    return lax.dot_general(a, b, (((1,), (0,)), ((), ())), preferred_element_type=jnp.float32)


def dot_tn(a, b):
    return lax.dot_general(a, b, (((0,), (0,)), ((), ())), preferred_element_type=jnp.float32)


PAIR = 2 * BLK


def even_lanes(rows):
    return lax.broadcasted_iota(jnp.int32, (rows, PAIR), 1) < BLK


def stacked(values):
    zero = jnp.zeros_like(values)
    even = even_lanes(BLK)
    return jnp.concatenate([jnp.where(even, values, zero), jnp.where(even, zero, values)], axis=0)


def unstacked(values):
    return jnp.where(even_lanes(BLK), values[:BLK], values[BLK:])


class Layout:
    def __init__(self, len_ref, rb_ref, blocks, position):
        self.len_ref, self.rb_ref, self.blocks = len_ref, rb_ref, blocks
        self.half = blocks // 2
        self.rand = rb_ref.shape[-1]
        self.shift = position * self.half

    def moved(self, index):
        at = index + self.shift
        return jnp.where(at >= self.blocks, at - self.blocks, at)

    def spot(self, index):
        return pl.ds(pl.multiple_of(self.moved(index) * BLK, BLK), BLK)

    def part(self, index):
        return pl.ds(pl.multiple_of(self.moved(index) * BLK, BLK), self.half * BLK)

    def counts(self):
        self.count0 = lax.div(self.len_ref[0, 0], BLK)
        self.count1 = lax.div(self.len_ref[0, 1], BLK)
        self.second = jnp.where(self.count1 > 0, 1, 0)
        self.inner = self.blocks - 2 - 2 * self.second

    def locate(self, i):
        in0 = i < self.count0 - 2
        self.b = b = jnp.where(in0, i + 1, i + 2 + self.second)
        self.live = live = b < self.count0 + self.count1
        self.first = first = jnp.where(in0, 0, jnp.where(live, self.count0, b))
        items = jnp.where(in0, self.count0, jnp.where(live, self.count1, 1))
        rel = b - first
        last = items - 1
        zero, neg = jnp.float32(0.0), jnp.float32(negative)
        self.fixed = [
            first,
            first + last,
            jnp.where(live, b - 1, b),
            jnp.where(live, b + 1, b),
            b,
        ]
        self.low_bias = jnp.where(live & (rel == 1), neg, zero)
        self.high_bias = jnp.where(live & (rel + 1 == last), neg, zero)
        return self

    def ends(self, item):
        first = jnp.where(item == 0, 0, self.count0)
        count = jnp.where(item == 0, self.count0, self.count1)
        return first, first + count - 1, lax.div(count, self.half)

    def chosen(self, head):
        return [
            jnp.where(self.live, self.first + self.rb_ref[0, head, self.b, k], self.b)
            for k in range(self.rand)
        ]


def gathered(ref, layout, column, picked):
    even = even_lanes(BLK)

    def rows(index):
        return ref[layout.spot(index), column : column + PAIR]

    return jnp.concatenate(
        [rows(i) for i in layout.fixed]
        + [jnp.where(even, rows(i), rows(j)) for i, j in zip(*picked)],
        axis=0,
    )


ROWS = 32


def soft_rows(held):
    probs, inverse = [], []
    for row in range(0, held.shape[0], ROWS):
        scores = held[row : row + ROWS, :]
        expo = jnp.exp(scores - jnp.max(scores, axis=1, keepdims=True))
        inverse.append(1.0 / jnp.sum(expo, axis=1, keepdims=True))
        probs.append(expo.astype(jnp.bfloat16))
    return jnp.concatenate(probs, axis=0), jnp.concatenate(inverse, axis=0)


def attn_fwd_kernel(pairs, position, len_ref, rb_ref, tri_ref, out_ref, wide, *held):
    blocks = tri_ref.shape[0] // BLK
    scale = jnp.bfloat16(BLK**-0.5)
    layout = Layout(len_ref, rb_ref, blocks, position())
    layout.counts()

    def query_of(p, b):
        at = layout.spot(b)
        return stacked(tri_ref[at, p * 3 * PAIR : p * 3 * PAIR + PAIR]) * scale

    def put(p, b, mixed):
        at = layout.spot(b)
        out_ref[at, p * PAIR : (p + 1) * PAIR] = unstacked(mixed).astype(jnp.bfloat16)

    def sparse_scores(i, held):
        at = layout.locate(i)
        lane = lax.broadcasted_iota(jnp.int32, (1, PAIR), 1) < BLK
        bias_row = jnp.where(lane, at.low_bias, at.high_bias)
        for n, p in enumerate(pairs):
            picked = [at.chosen(2 * p), at.chosen(2 * p + 1)]
            keys = gathered(tri_ref, at, (3 * p + 1) * PAIR, picked)
            scores = dot_nt(query_of(p, at.b), keys)
            held[n][...] = jnp.concatenate(
                [scores[:, :PAIR], scores[:, PAIR : 2 * PAIR] + bias_row, scores[:, 2 * PAIR :]],
                axis=1,
            )

    def sparse_mix(i, held):
        at = layout.locate(i)
        for n, p in enumerate(pairs):
            picked = [at.chosen(2 * p), at.chosen(2 * p + 1)]
            probs, inverse = soft_rows(held[n])
            values = gathered(tri_ref, at, (3 * p + 2) * PAIR, picked)
            put(p, at.b, dot_nn(probs, values) * inverse)

    held_a, held_b = held[: len(pairs)], held[len(pairs) :]
    sparse_scores(0, held_a)

    def two(j, carry):
        sparse_scores(2 * j + 1, held_b)
        sparse_mix(2 * j, held_a)
        sparse_scores(jnp.minimum(2 * j + 2, layout.inner - 1), held_a)
        sparse_mix(2 * j + 1, held_b)
        return carry

    lax.fori_loop(0, lax.div(layout.inner, 2), two, 0)

    def dense(item, carry):
        first, last, chunks = layout.ends(item)
        queries = [
            jnp.concatenate([query_of(p, first), query_of(p, last)], axis=0) for p in pairs
        ]

        def dense_of(spans):
            for query, p in zip(queries, pairs):
                span = layout.half * BLK
                for c, at in enumerate(spans):
                    keys = tri_ref[at, (3 * p + 1) * PAIR : (3 * p + 2) * PAIR]
                    wide[:, c * span : (c + 1) * span] = dot_nt(query, keys)
                probs, inverse = soft_rows(wide.at[:, : len(spans) * span])
                mixed = sum(
                    dot_nn(
                        probs[:, c * span : (c + 1) * span],
                        tri_ref[at, (3 * p + 2) * PAIR : (3 * p + 3) * PAIR],
                    )
                    for c, at in enumerate(spans)
                ) * inverse
                put(p, first, mixed[:PAIR])
                put(p, last, mixed[PAIR:])

        @pl.when(chunks == 1)
        def short():
            dense_of([layout.part(first)])

        @pl.when(chunks == 2)
        def long():
            dense_of([layout.part(first), layout.part(first + layout.half)])

        return carry

    lax.fori_loop(0, 1 + layout.second, dense, 0)


def grad_rows(held_scores, held_grads, probs_ref, grads_ref):
    for row in range(0, held_scores.shape[0], ROWS):
        at = slice(row, row + ROWS)
        scores = held_scores[at, :]
        grad_probs = held_grads[at, :]
        expo = jnp.exp(scores - jnp.max(scores, axis=1, keepdims=True))
        probs = expo * (1.0 / jnp.sum(expo, axis=1, keepdims=True))
        delta = jnp.sum(probs * grad_probs, axis=1, keepdims=True)
        probs_ref[at, :] = probs.astype(jnp.bfloat16)
        grads_ref[at, :] = (probs * (grad_probs - delta)).astype(jnp.bfloat16)


def attn_bwd_kernel(
    pairs, position, len_ref, rb_ref, tri_ref, grad_ref, out_ref, sum_ref, *scratch
):
    blocks = tri_ref.shape[0] // BLK
    scale = jnp.bfloat16(BLK**-0.5)
    back = BLK**-0.5
    layout = Layout(len_ref, rb_ref, blocks, position())
    layout.counts()
    count = len(pairs)
    key_acc, value_acc = scratch[:count], scratch[count : 2 * count]
    held_a, held_b, done = (scratch[n * count : (n + 2) * count] for n in (2, 4, 6))
    wide = scratch[8 * count :]

    def clear(r, carry):
        at = pl.ds(pl.multiple_of(r * BLK, BLK), BLK)
        for acc in scratch[: 2 * count]:
            acc[at, :] = jnp.zeros((BLK, PAIR), jnp.float32)
        return carry

    lax.fori_loop(0, blocks, clear, 0)

    def query_of(p, b):
        at = layout.spot(b)
        return stacked(tri_ref[at, p * 3 * PAIR : p * 3 * PAIR + PAIR]) * scale

    def grad_of(p, b):
        at = layout.spot(b)
        return stacked(grad_ref[at, p * PAIR : (p + 1) * PAIR])

    def put(i, b, grad_query):
        out_ref[layout.spot(b), i * 3 * PAIR : i * 3 * PAIR + PAIR] = unstacked(
            grad_query * back
        ).astype(jnp.bfloat16)

    def sparse_scores(n, held):
        at = layout.locate(n)
        lane = lax.broadcasted_iota(jnp.int32, (1, PAIR), 1) < BLK
        bias_row = jnp.where(lane, at.low_bias, at.high_bias)
        for i, p in enumerate(pairs):
            picked = [at.chosen(2 * p), at.chosen(2 * p + 1)]
            keys = gathered(tri_ref, at, (3 * p + 1) * PAIR, picked)
            values = gathered(tri_ref, at, (3 * p + 2) * PAIR, picked)
            scores = dot_nt(query_of(p, at.b), keys)
            held[2 * i][...] = jnp.concatenate(
                [scores[:, :PAIR], scores[:, PAIR : 2 * PAIR] + bias_row, scores[:, 2 * PAIR :]],
                axis=1,
            )
            held[2 * i + 1][...] = dot_nt(grad_of(p, at.b), values)

    def sparse_grads(n, held):
        at = layout.locate(n)
        even = even_lanes(BLK)
        for i, p in enumerate(pairs):
            grad_rows(held[2 * i], held[2 * i + 1], done[2 * i], done[2 * i + 1])
            picked = [at.chosen(2 * p), at.chosen(2 * p + 1)]
            spots = [at.spot(index) for index in at.fixed]
            spots += [(at.spot(one), at.spot(two)) for one, two in zip(*picked)]
            keys = gathered(tri_ref, at, (3 * p + 1) * PAIR, picked)
            put(i, at.b, dot_nn(done[2 * i + 1][...], keys))
            for acc, update in (
                (key_acc[i], dot_tn(done[2 * i + 1][...], query_of(p, at.b))),
                (value_acc[i], dot_tn(done[2 * i][...], grad_of(p, at.b))),
            ):
                for j, spot in enumerate(spots):
                    piece = update[j * BLK : (j + 1) * BLK]
                    if j < len(at.fixed):
                        acc[spot, :] += piece
                    else:
                        zero = jnp.zeros_like(piece)
                        acc[spot[0], :] += jnp.where(even, piece, zero)
                        acc[spot[1], :] += jnp.where(even, zero, piece)

    sparse_scores(0, held_a)

    def two(j, carry):
        sparse_scores(2 * j + 1, held_b)
        sparse_grads(2 * j, held_a)
        sparse_scores(jnp.minimum(2 * j + 2, layout.inner - 1), held_a)
        sparse_grads(2 * j + 1, held_b)
        return carry

    lax.fori_loop(0, lax.div(layout.inner, 2), two, 0)

    wide_scores, wide_grads, wide_probs, wide_out = wide

    def dense(item, carry):
        first, last, chunks = layout.ends(item)

        def dense_of(spans):
            span = layout.half * BLK
            cover = len(spans) * span
            def end(n, carry):
                b = jnp.where(n == 0, first, last)
                for i, p in enumerate(pairs):
                    query, grad = query_of(p, b), grad_of(p, b)
                    for c, at in enumerate(spans):
                        cut = slice(c * span, (c + 1) * span)
                        keys = tri_ref[at, (3 * p + 1) * PAIR : (3 * p + 2) * PAIR]
                        values = tri_ref[at, (3 * p + 2) * PAIR : (3 * p + 3) * PAIR]
                        wide_scores[:, cut] = dot_nt(query, keys)
                        wide_grads[:, cut] = dot_nt(grad, values)
                    grad_rows(*(ref.at[:, :cover] for ref in wide))
                    total = jnp.zeros((PAIR, PAIR), jnp.float32)
                    for c, at in enumerate(spans):
                        cut = slice(c * span, (c + 1) * span)
                        keys = tri_ref[at, (3 * p + 1) * PAIR : (3 * p + 2) * PAIR]
                        total += dot_nn(wide_out[:, cut], keys)
                        key_acc[i][at, :] += dot_tn(wide_out[:, cut], query)
                        value_acc[i][at, :] += dot_tn(wide_probs[:, cut], grad)
                    put(i, b, total)
                return carry

            lax.fori_loop(0, 2, end, 0)

        @pl.when(chunks == 1)
        def short():
            dense_of([layout.part(first)])

        @pl.when(chunks == 2)
        def long():
            dense_of([layout.part(first), layout.part(first + layout.half)])

        return carry

    lax.fori_loop(0, 1 + layout.second, dense, 0)

    sum_ref[...] = jnp.zeros_like(sum_ref)

    def finish(r, carry):
        at = pl.ds(pl.multiple_of(r * BLK, BLK), BLK)
        new = []
        for i in range(count):
            column = i * 3 * PAIR
            query_sum, value_sum = carry[i]
            out_ref[at, column + PAIR : column + 2 * PAIR] = key_acc[i][at, :].astype(jnp.bfloat16)
            value = value_acc[i][at, :].astype(jnp.bfloat16)
            out_ref[at, column + 2 * PAIR : column + 3 * PAIR] = value
            query = out_ref[at, column : column + PAIR].astype(jnp.float32)
            new.append(
                tuple(
                    total + jnp.sum(part.reshape(-1, 8, PAIR), axis=0)
                    for total, part in (
                        (query_sum, query),
                        (value_sum, value.astype(jnp.float32)),
                    )
                )
            )
        return tuple(new)

    zero = jnp.zeros((8, PAIR), jnp.float32)
    sums = lax.fori_loop(0, blocks, finish, tuple((zero, zero) for _ in pairs))
    for i, totals in enumerate(sums):
        for kind, total in enumerate(totals):
            sum_ref[kind : kind + 1, i * PAIR : (i + 1) * PAIR] = jnp.sum(
                total, axis=0, keepdims=True
            )


vmem = pl.BlockSpec(memory_space=pltpu.VMEM)
smem = pl.BlockSpec(memory_space=pltpu.SMEM)
def attention_forward(lengths, randoms, triple, position):
    pairs = randoms.shape[1] // 2
    rows = triple.shape[0]
    area = rows * rows // 3 * 2 * pairs
    return pl.pallas_call(
        functools.partial(attn_fwd_kernel, range(pairs), position),
        out_shape=jax.ShapeDtypeStruct((rows, pairs * PAIR), jnp.bfloat16),
        in_specs=[smem, smem, vmem],
        out_specs=vmem,
        name="attend_forward",
        scratch_shapes=[pltpu.VMEM((2 * PAIR, rows), jnp.float32)]
        + [pltpu.VMEM((PAIR, 8 * BLK), jnp.float32)] * (2 * pairs),
        cost_estimate=pl.CostEstimate(
            flops=16 * area * PAIR, transcendentals=area, bytes_accessed=rows * pairs * PAIR * 8
        ),
        compiler_params=pltpu.CompilerParams(vmem_limit_bytes=8 << 20),
    )(lengths, randoms, triple)


def attention_backward(lengths, randoms, triple, grad, pairs, position):
    rows = triple.shape[0]
    count = len(pairs)
    area = rows * rows // 3 * 2 * count
    return pl.pallas_call(
        functools.partial(attn_bwd_kernel, pairs, position),
        out_shape=(
            jax.ShapeDtypeStruct((rows, count * 3 * PAIR), jnp.bfloat16),
            jax.ShapeDtypeStruct((8, count * PAIR), jnp.float32),
        ),
        in_specs=[smem, smem, vmem, vmem],
        out_specs=(vmem, vmem),
        name="attend_backward",
        scratch_shapes=[pltpu.VMEM((rows, PAIR), jnp.float32)] * (2 * count)
        + [pltpu.VMEM((PAIR, 8 * BLK), jnp.float32)] * (4 * count)
        + [pltpu.VMEM((PAIR, 8 * BLK), jnp.bfloat16)] * (2 * count)
        + [pltpu.VMEM((PAIR, rows), kind) for kind in (jnp.float32,) * 2 + (jnp.bfloat16,) * 2],
        cost_estimate=pl.CostEstimate(
            flops=40 * area * PAIR, transcendentals=area, bytes_accessed=rows * count * PAIR * 20
        ),
        compiler_params=pltpu.CompilerParams(vmem_limit_bytes=20 << 20),
    )(lengths, randoms, triple, grad)


TILE = 256
EPS = 1e-06


def tile_at(n):
    return pl.ds(pl.multiple_of(n * TILE, TILE), TILE)


def up_kernel(rows_ref, weight_ref, bias_ref, active_ref, slope_ref, held_a, held_b):
    tiles = weight_ref.shape[1] // TILE
    root = (2.0 / np.pi) ** 0.5
    cube = 0.044715 * root

    def product(n, held):
        held[...] = dot_nn(rows_ref[...], weight_ref[:, tile_at(n)])

    def gelu(n, held):
        bias = bias_ref[:, tile_at(n)]
        for row in range(0, held.shape[0], ROWS):
            at = slice(row, row + ROWS)
            upper = (held[at, :] + bias).astype(jnp.bfloat16).astype(jnp.float32)
            square = upper * upper
            half = 0.5 + 0.5 * jnp.tanh(upper * (square * cube + root))
            active = upper * half
            active_ref[at, tile_at(n)] = active.astype(jnp.bfloat16)
            bend = (1.0 - half) * (square * (6.0 * cube) + 2.0 * root)
            slope_ref[at, tile_at(n)] = (half + active * bend).astype(jnp.bfloat16)

    product(0, held_a)

    def two(j, carry):
        product(2 * j + 1, held_b)
        gelu(2 * j, held_a)
        product(jnp.minimum(2 * j + 2, tiles - 1), held_a)
        gelu(2 * j + 1, held_b)
        return carry

    lax.fori_loop(0, tiles // 2, two, 0)


def up_gelu(rows, weight, bias):
    count, width = rows.shape[0], weight.shape[1]
    shape = jax.ShapeDtypeStruct((count, width), jnp.bfloat16)
    return pl.pallas_call(
        up_kernel,
        out_shape=(shape, shape),
        in_specs=[vmem] * 3,
        out_specs=(vmem, vmem),
        name="up_gelu",
        scratch_shapes=[pltpu.VMEM((count, TILE), jnp.float32)] * 2,
        cost_estimate=pl.CostEstimate(
            flops=2 * count * width * rows.shape[1],
            transcendentals=count * width,
            bytes_accessed=2 * (rows.size + weight.size + 2 * count * width),
        ),
        compiler_params=pltpu.CompilerParams(vmem_limit_bytes=12 << 20),
    )(rows, weight, bias.reshape(1, -1))


def back_kernel(grad_ref, weight_ref, slope_ref, out_ref, sum_ref):
    def step(n, carry):
        grad_active = dot_nn(grad_ref[...], weight_ref[:, tile_at(n)])
        total = jnp.zeros((8, TILE), jnp.float32)
        for row in range(0, grad_active.shape[0], ROWS):
            at = slice(row, row + ROWS)
            grad = grad_active[at] * slope_ref[at, tile_at(n)].astype(jnp.float32)
            grad = grad.astype(jnp.bfloat16)
            out_ref[at, tile_at(n)] = grad
            total += jnp.sum(grad.astype(jnp.float32).reshape(-1, 8, TILE), axis=0)
        sum_ref[:, tile_at(n)] = total
        return carry

    lax.fori_loop(0, weight_ref.shape[1] // TILE, step, 0)


def back_slope(grad, weight, slope):
    count, width = slope.shape
    return pl.pallas_call(
        back_kernel,
        out_shape=(
            jax.ShapeDtypeStruct((count, width), jnp.bfloat16),
            jax.ShapeDtypeStruct((8, width), jnp.float32),
        ),
        in_specs=[vmem] * 3,
        out_specs=(vmem, vmem),
        name="back_slope",
        cost_estimate=pl.CostEstimate(
            flops=2 * count * width * grad.shape[1],
            transcendentals=0,
            bytes_accessed=2 * (grad.size + weight.size + 2 * count * width),
        ),
        compiler_params=pltpu.CompilerParams(vmem_limit_bytes=12 << 20),
    )(grad, weight, slope)


def outer_kernel(count, *refs):
    lefts, rights, out_ref = refs[:count], refs[count:-1], refs[-1]
    if len(rights) < count:
        rows = lefts[0].shape[0]
        rights = [rights[0].at[n * rows : (n + 1) * rows] for n in range(count)]

    def step(at):
        total = sum(dot_tn(a[...], b[:, at]) for a, b in zip(lefts, rights))
        out_ref[:, at] = total.astype(jnp.bfloat16)

    width = out_ref.shape[1]
    if width % TILE:
        step(slice(0, width))
    else:

        def body(n, carry):
            step(tile_at(n))
            return carry

        lax.fori_loop(0, width // TILE, body, 0)


def outer(lefts, rights):
    shape = (lefts[0].shape[1], rights[0].shape[1])
    inner = sum(a.shape[0] for a in lefts)
    return pl.pallas_call(
        functools.partial(outer_kernel, len(lefts)),
        out_shape=jax.ShapeDtypeStruct(shape, jnp.bfloat16),
        in_specs=[vmem] * (len(lefts) + len(rights)),
        out_specs=vmem,
        name="outer",
        cost_estimate=pl.CostEstimate(
            flops=2 * inner * shape[0] * shape[1],
            transcendentals=0,
            bytes_accessed=2 * inner * sum(shape),
        ),
        compiler_params=pltpu.CompilerParams(vmem_limit_bytes=12 << 20),
    )(*lefts, *rights)


def project_kernel(own_ref, other_ref, weight_ref, out_ref):
    rows = own_ref.shape[0]
    for n, ref in enumerate((own_ref, other_ref)):
        product = dot_nn(ref[...], weight_ref[...])
        out_ref[n * rows : (n + 1) * rows, :] = product.astype(jnp.bfloat16)


def project_both(own, other, weight):
    return pl.pallas_call(
        project_kernel,
        out_shape=jax.ShapeDtypeStruct((2 * own.shape[0], weight.shape[1]), jnp.bfloat16),
        in_specs=[vmem] * 3,
        out_specs=vmem,
        name="project_both",
        compiler_params=pltpu.CompilerParams(vmem_limit_bytes=12 << 20),
    )(own, other, weight)


GROUP = 16
SPLIT = 4


def groups_at(r):
    return [
        (r * SPLIT + n, pl.ds(pl.multiple_of((r * SPLIT + n) * GROUP, GROUP), GROUP))
        for n in range(SPLIT)
    ]


def row_mean(values):
    return jnp.sum(values, axis=1, keepdims=True) * (1.0 / values.shape[1])


def folded(values):
    return jnp.sum(values.reshape(-1, 8, values.shape[1]), axis=0)


def norm_two_kernel(position, len_ref, down_ref, other_ref, resid_ref, cot_ref, vec_ref, out_ref, grad_ref, low_ref, sum_ref):
    count, width = down_ref.shape
    live_rows = len_ref[0, 0] + len_ref[0, 1] - position() * count
    bias, gain, shift = (vec_ref[n : n + 1, :] for n in range(3))

    def group(r, at, sums):
        row = r * GROUP + lax.broadcasted_iota(jnp.int32, (GROUP, 1), 0)
        live = jnp.where(row < live_rows, 1.0, 0.0)
        values = down_ref[at, :] + other_ref[at, :].astype(jnp.float32) + bias + resid_ref[at, :]
        centered = values - row_mean(values)
        inverse = lax.rsqrt(row_mean(centered * centered) + EPS)
        normed = centered * inverse
        out_ref[at, :] = ((normed * gain + shift) * live).astype(jnp.bfloat16)
        cot = cot_ref[at, :].astype(jnp.float32) * live
        scaled = cot * gain
        grad = inverse * (scaled - row_mean(scaled) - normed * row_mean(scaled * normed))
        grad_ref[at, :] = grad
        low_ref[at, :] = grad.astype(jnp.bfloat16)
        return tuple(s + folded(v) for s, v in zip(sums, (grad, cot * normed, cot)))

    def step(r, sums):
        for n, at in groups_at(r):
            sums = group(n, at, sums)
        return sums

    zero = jnp.zeros((8, width), jnp.float32)
    sums = lax.fori_loop(0, count // (GROUP * SPLIT), step, (zero,) * 3)
    for n, total in enumerate(sums):
        sum_ref[n : n + 1, :] = jnp.sum(total, axis=0, keepdims=True)
    sum_ref[3:8, :] = jnp.zeros((5, width), jnp.float32)


def norm_two(lengths, down, other, resid, cot, bias, gain, shift, position):
    shape = down.shape
    row = jax.ShapeDtypeStruct((8, shape[1]), jnp.float32)
    return pl.pallas_call(
        functools.partial(norm_two_kernel, position),
        out_shape=(
            jax.ShapeDtypeStruct(shape, jnp.bfloat16),
            jax.ShapeDtypeStruct(shape, jnp.float32),
            jax.ShapeDtypeStruct(shape, jnp.bfloat16),
            row,
        ),
        in_specs=[smem] + [vmem] * 5,
        out_specs=(vmem,) * 4,
        name="norm_two",
        cost_estimate=pl.CostEstimate(
            flops=40 * down.size, transcendentals=0, bytes_accessed=20 * down.size
        ),
        compiler_params=pltpu.CompilerParams(vmem_limit_bytes=12 << 20),
    )(lengths, down, other, resid, cot, jnp.stack([bias, gain, shift]))


def norm_one_kernel(own_ref, other_ref, grad_ref, normed_ref, inverse_ref, gain_ref, out_ref, low_ref, sum_ref):
    count, width = own_ref.shape
    gain = gain_ref[...]

    def group(r, at, sums):
        grad = own_ref[at, :] + other_ref[at, :].astype(jnp.float32) + grad_ref[at, :]
        normed = normed_ref[at, :]
        scaled = grad * gain
        result = inverse_ref[at, :] * (
            scaled - row_mean(scaled) - normed * row_mean(scaled * normed)
        )
        out_ref[at, :] = result
        low_ref[at, :] = result.astype(jnp.bfloat16)
        return tuple(s + folded(v) for s, v in zip(sums, (result, grad * normed, grad)))

    def step(r, sums):
        for n, at in groups_at(r):
            sums = group(n, at, sums)
        return sums

    zero = jnp.zeros((8, width), jnp.float32)
    sums = lax.fori_loop(0, count // (GROUP * SPLIT), step, (zero,) * 3)
    for n, total in enumerate(sums):
        sum_ref[n : n + 1, :] = jnp.sum(total, axis=0, keepdims=True)
    sum_ref[3:8, :] = jnp.zeros((5, width), jnp.float32)


def norm_one_back(own, other, grad, normed, inverse, gain):
    shape = own.shape
    return pl.pallas_call(
        norm_one_kernel,
        out_shape=(
            jax.ShapeDtypeStruct(shape, jnp.float32),
            jax.ShapeDtypeStruct(shape, jnp.bfloat16),
            jax.ShapeDtypeStruct((8, shape[1]), jnp.float32),
        ),
        in_specs=[vmem] * 6,
        out_specs=(vmem,) * 3,
        name="norm_one_back",
        cost_estimate=pl.CostEstimate(
            flops=20 * own.size, transcendentals=0, bytes_accessed=20 * own.size
        ),
        compiler_params=pltpu.CompilerParams(vmem_limit_bytes=12 << 20),
    )(own, other, grad, normed, inverse, gain.reshape(1, -1))


def pack_rows(ref, at, small):
    rows = small.shape[0]
    high = small.astype(jnp.bfloat16)
    ref[at : at + rows, :] = high
    ref[at + rows : at + 2 * rows, :] = (small - high.astype(jnp.float32)).astype(jnp.bfloat16)


def unpack_rows(ref, at, rows):
    high = ref[at : at + rows, :].astype(jnp.float32)
    return high + ref[at + rows : at + 2 * rows, :].astype(jnp.float32)


def slab_at(at_ref, place, z, rows):
    return pl.ds(pl.multiple_of((z * QUAD + at_ref[place]) * rows, rows), rows)


def columns_of(totals):
    cuts, low = [], 0
    for total in totals:
        cuts.append(slice(low, low + total.shape[1]))
        low += total.shape[1]
    return cuts


def sum_first_kernel(count, deep, at_ref, *refs):
    totals, rest = refs[:count], refs[count:]
    out_ref = rest[-1]
    rows = totals[0].shape[0] // (deep * QUAD)
    for part, place in enumerate((1, 3)):
        for z in range(deep):
            row = (part * deep + z) * rows
            for total, cut in zip(totals, columns_of(totals)):
                out_ref[row : row + rows, cut] = total[slab_at(at_ref, place, z, rows), :]
    if len(rest) > 1:
        pack_rows(out_ref, 2 * deep * rows, rest[0][...])


def sum_second_kernel(count, deep, at_ref, *refs):
    totals, got_ref = refs[:count], refs[count]
    rows = totals[0].shape[0] // (deep * QUAD)
    if len(refs) > count + 2:
        small_ref, out_ref, new_ref = refs[count + 1 :]
        small = small_ref[...] + unpack_rows(got_ref, 2 * deep * rows, small_ref.shape[0])
        new_ref[...] = small
        pack_rows(out_ref, deep * rows, small)
    else:
        out_ref = refs[-1]
    for z in range(deep):
        for total, cut in zip(totals, columns_of(totals)):
            far = total[slab_at(at_ref, 2, z, rows), :].astype(jnp.float32)
            row = (deep + z) * rows
            far = far + got_ref[row : row + rows, cut].astype(jnp.float32)
            out_ref[z * rows : (z + 1) * rows, cut] = far.astype(jnp.bfloat16)


def sum_deep_kernel(groups, deep, small_rows, at_ref, *refs):
    count = sum(groups)
    totals, refs = refs[:count], refs[count:]
    gots, twos, refs = refs[: len(groups)], refs[len(groups) : 2 * len(groups)], refs[2 * len(groups) :]
    rows = totals[0].shape[0] // (deep * QUAD)
    small = None
    if small_rows:
        small_ref, new_ref, refs = refs[0], refs[1], refs[2:]
        small = small_ref[...] + unpack_rows(twos[-1], deep * rows, small_rows)
        wide = refs[0].shape[1] // small.shape[1]
        part = small_rows // wide
        small = jnp.concatenate([small[n * part : (n + 1) * part] for n in range(wide)], axis=1)
        new_ref[...] = small
    out_cuts = columns_of(totals)
    for k in range(deep):
        z = at_ref[QUAD] ^ k
        near = pl.ds(pl.multiple_of(z * rows, rows), rows)
        n = 0
        for group, got_ref, two_ref in zip(groups, gots, twos):
            members = totals[n : n + group]
            for total, cut, out_cut in zip(members, columns_of(members), out_cuts[n : n + group]):
                value = (
                    total[slab_at(at_ref, 0, z, rows), :].astype(jnp.float32)
                    + got_ref[near, cut].astype(jnp.float32)
                    + two_ref[near, cut].astype(jnp.float32)
                )
                refs[k][:rows, out_cut] = value.astype(refs[k].dtype)
            n += group
        if k and small is not None:
            pack_rows(refs[k], rows, small)


def sum_last_kernel(count, small_rows, *refs):
    own_ref, answers = refs[0], refs[1 : 1 + count]
    rows = own_ref.shape[0]
    own = own_ref[...]
    for answer in answers:
        own = own + answer[:rows, :].astype(jnp.float32)
    if small_rows:
        small_ref, out_ref, new_ref = refs[1 + count :]
        small = small_ref[...]
        for answer in answers:
            small = small + unpack_rows(answer, rows, small_rows)
        new_ref[...] = small
        out_ref[...] = own
    else:
        low = 0
        for out_ref in refs[1 + count :]:
            out_ref[...] = own[:, low : low + out_ref.shape[1]]
            low += out_ref.shape[1]


def vmem_call(kernel, outs, operands, name, scalars=1, limit=12):
    outs = [jax.ShapeDtypeStruct(shape, dtype) for shape, dtype in outs]
    return pl.pallas_call(
        kernel,
        out_shape=outs,
        in_specs=[smem] * scalars + [vmem] * (len(operands) - scalars),
        out_specs=[vmem] * len(outs),
        name=name,
        compiler_params=pltpu.CompilerParams(vmem_limit_bytes=limit << 20),
    )(*operands)


def sum_first(totals, spot, small=None):
    span = totals[0].shape[0] // QUAD
    extra = 0 if small is None else 2 * small.shape[0]
    shape = (2 * span + extra, sum(t.shape[1] for t in totals))
    operands = [spot.at, *totals] + ([] if small is None else [small])
    kernel = functools.partial(sum_first_kernel, len(totals), spot.deep)
    return vmem_call(kernel, [(shape, jnp.bfloat16)], operands, "sum_first")[0]


def sum_second(totals, spot, got, small=None):
    span = totals[0].shape[0] // QUAD
    kernel = functools.partial(sum_second_kernel, len(totals), spot.deep)
    operands = [spot.at, *totals, got]
    if small is None:
        outs = [((span, got.shape[1]), jnp.bfloat16)]
        return vmem_call(kernel, outs, operands, "sum_second")[0]
    outs = [((span + 2 * small.shape[0], got.shape[1]), jnp.bfloat16), (small.shape, jnp.float32)]
    return vmem_call(kernel, outs, operands + [small], "sum_second")


def sum_deep(groups, spot, gots, twos, small=None):
    totals = [total for group in groups for total in group]
    rows = totals[0].shape[0] // (QUAD * spot.deep)
    columns = sum(t.shape[1] for t in totals)
    small_rows = 0 if small is None else small.shape[0]
    kernel = functools.partial(
        sum_deep_kernel, [len(group) for group in groups], spot.deep, small_rows
    )
    operands = [spot.at, *totals, *gots, *twos] + ([] if small is None else [small])
    outs, extra = [], 0
    if small is not None:
        part = small_rows * small.shape[1] // columns
        outs, extra = [((part, columns), jnp.float32)], 2 * part
    outs += [((rows, columns), jnp.float32)]
    outs += [((rows + extra, columns), jnp.bfloat16)] * (spot.deep - 1)
    return vmem_call(kernel, outs, operands, "sum_deep")


def sum_last(own, answers, widths, small=None):
    kernel = functools.partial(
        sum_last_kernel, len(answers), 0 if small is None else small.shape[0]
    )
    operands = [own, *answers] + ([] if small is None else [small])
    outs = [((own.shape[0], w), jnp.float32) for w in widths]
    outs += [] if small is None else [(small.shape, jnp.float32)]
    return vmem_call(kernel, outs, operands, "sum_last", scalars=0)


def small_kernel(own_ref, swapped_ref, up_one_ref, up_two_ref, *refs):
    out_ref = refs[-1]
    columns = out_ref.shape[1]
    both = own_ref[...] + swapped_ref[...]
    rows = [both[0:3], both[8:11]]
    row = 0
    for low in range(0, both.shape[1], columns):
        for part in rows:
            out_ref[row : row + 3, :] = part[:, low : low + columns]
            row += 3
    up = jnp.sum(up_one_ref[...] + up_two_ref[...], axis=0, keepdims=True)
    for low in range(0, up.shape[1], columns):
        out_ref[row : row + 1, :] = up[:, low : low + columns]
        row += 1
    low = 0
    for ref in refs[:-1]:
        out_ref[row : row + 2, low : low + ref.shape[1]] = ref[0:2, :]
        low += ref.shape[1]


def small_sums(own, swapped, up_one, up_two, sums):
    columns = sum(s.shape[1] for s in sums)
    rows = 6 * own.shape[1] // columns + up_one.shape[1] // columns + 2
    return vmem_call(
        small_kernel,
        [((rows, columns), jnp.float32)],
        [own, swapped, up_one, up_two, *sums],
        "small_sums",
        scalars=0,
    )[0]


QUAD = 4


def group_permute(value, deep, target):
    pairs = []
    for z in range(deep):
        for q in range(QUAD):
            for h in range(2):
                to_z, to_q = target(z, q, h)
                pairs.append(((z * QUAD + q) * 2 + h, (to_z * QUAD + to_q) * 2 + h))
    return lax.ppermute(value, ("deep", "quad", "head"), pairs)


def deep_step(value, deep, bit):
    return group_permute(value, deep, lambda z, q, h: (z ^ bit, q))


def quad_step(value, deep, second):
    return group_permute(value, deep, lambda z, q, h: (z, q ^ ((2 >> h) if second else (1 << h))))


def swap(value):
    return lax.ppermute(value, "head", [(0, 1), (1, 0)])


def after(value, *others):
    return lax.optimization_barrier((value,) + others)[0]


class Spot:
    def __init__(self):
        self.z, self.q, self.h = (lax.axis_index(a) for a in ("deep", "quad", "head"))
        self.deep = lax.axis_size("deep")
        one, two = 1 << self.h, 2 >> self.h
        self.places = [self.q, self.q ^ one, self.q ^ two, self.q ^ 3]
        self.at = jnp.stack(self.places + [self.z]).astype(jnp.int32)


def gather_deep(value, spot):
    return jnp.stack([value] + [deep_step(value, spot.deep, k) for k in range(1, spot.deep)])


def place_kernel(deep, windows, at_ref, *refs):
    pieces = refs[:3]
    outs = refs[3:]
    rows = pieces[0].shape[1]
    for k in range(deep):
        for j in range(QUAD):
            ref = pieces[j] if j < 2 else pieces[2].at[j - 2]
            row = pl.multiple_of(((at_ref[QUAD] ^ k) * QUAD + at_ref[j]) * rows, rows)
            for out, (low, high) in zip(outs, windows):
                out[pl.ds(row, rows), :] = ref[k, :, low:high]


def place(spot, pieces, widths):
    windows, low = [], 0
    for width in widths:
        windows.append((low, low + width))
        low += width
    deep, rows = pieces[0].shape[:2]
    return pl.pallas_call(
        functools.partial(place_kernel, deep, windows),
        out_shape=[
            jax.ShapeDtypeStruct((deep * QUAD * rows, width), pieces[0].dtype) for width in widths
        ],
        in_specs=[smem] + [vmem] * 3,
        out_specs=[vmem] * len(widths),
        compiler_params=pltpu.CompilerParams(vmem_limit_bytes=8 << 20),
        name="place_pieces",
    )(spot.at, *pieces)


def mm(left, right):
    return jnp.einsum("td,df->tf", left, right, preferred_element_type=jnp.float32)


def mm_nt(left, right):
    return jnp.einsum("tf,df->td", left, right, preferred_element_type=jnp.float32)


def mm_tn(left, right):
    return jnp.einsum("td,tf->df", left, right, preferred_element_type=jnp.float32)


def low(value):
    return value.astype(jnp.bfloat16)


def by_pair(value):
    lead, kinds, columns = value.shape[:-2], value.shape[-2], value.shape[-1]
    split = value.reshape(lead + (kinds, columns // PAIR, PAIR))
    return jnp.swapaxes(split, -3, -2).reshape(lead + (kinds * columns,))


def by_kind(value, kinds):
    lead, columns = value.shape[:-1], value.shape[-1]
    split = value.reshape(lead + (columns // (kinds * PAIR), kinds, PAIR))
    return jnp.swapaxes(split, -3, -2).reshape(lead + (kinds, columns // kinds))


def on_device(
    inputs,
    qkv_weight,
    qv_bias,
    out_weight,
    out_bias,
    first_gain,
    first_shift,
    up_weight,
    up_bias,
    down_weight,
    down_bias,
    second_gain,
    second_shift,
    item_lengths,
    random_blocks,
    out_grad,
):
    half, width = inputs.shape
    spot = Spot()
    deep = spot.deep
    shard = qkv_weight.shape[0]
    head_width = qkv_weight.shape[2]
    up_width = up_weight.shape[1]
    pair_count = head_width // PAIR

    def position():
        return lax.axis_index("head")

    staged = deep == 4 and shard % 16 == 0
    every = ("deep", "quad")

    def gathered_whole(block):
        return lax.all_gather(block, every, axis=0, tiled=True)

    def scattered(total):
        return lax.psum_scatter(total, every, scatter_dimension=0, tiled=True).astype(jnp.float32)

    def first_quad(block):
        return quad_step(block, deep, False)

    def second_quad(block):
        return quad_step(block, deep, True)

    tokens_other = swap(inputs)
    tokens = jnp.concatenate([inputs, tokens_other], axis=0)
    qkv_block = by_pair(qkv_weight)
    mid = jnp.concatenate([out_weight, up_weight], axis=1)
    if staged:
        qkv_deep = gather_deep(qkv_block, spot)
        mid, qkv_deep = lax.optimization_barrier((mid, qkv_deep))
        qkv_other = first_quad(qkv_deep)
        mid_deep = gather_deep(mid, spot)
        qkv_far = second_quad(jnp.stack([qkv_deep, qkv_other]))
        (full_qkv,) = place(spot, (qkv_deep, qkv_other, qkv_far), [3 * head_width])
        mid_deep, full_qkv = lax.optimization_barrier((mid_deep, full_qkv))
        mid_other = first_quad(mid_deep)
        down_deep = gather_deep(after(down_weight, mid_deep), spot)
    else:
        full_qkv = gathered_whole(qkv_block)
        full_mid = gathered_whole(mid)
        full_out, full_up = full_mid[:, :head_width], full_mid[:, head_width:]
        full_down = gathered_whole(down_weight)

    bias = by_pair(jnp.stack([qv_bias[0], jnp.zeros_like(qv_bias[0]), qv_bias[1]]))
    triple = low(mm(tokens, full_qkv) + bias)
    if staged:
        triple, mid_other, down_deep = lax.optimization_barrier((triple, mid_other, down_deep))
        mid_far = second_quad(jnp.stack([mid_deep, mid_other]))
        down_other = first_quad(down_deep)
    attended = attention_forward(item_lengths, random_blocks, triple, position)
    if staged:
        attended, mid_far, down_other = lax.optimization_barrier((attended, mid_far, down_other))
        down_far = second_quad(jnp.stack([down_deep, down_other]))
        full_out, full_up = place(spot, (mid_deep, mid_other, mid_far), [head_width, up_width])

    other = swap(low(mm_nt(attended[half:], full_out)))
    proj = mm_nt(attended[:half], full_out) + other.astype(jnp.float32)
    normed_one_out, normed_one, inverse_one = norm_forward(
        proj + out_bias + inputs.astype(jnp.float32), first_gain, first_shift
    )
    hidden_own = low(normed_one_out)
    hidden_other = swap(hidden_own)
    active_own, slope_own = up_gelu(hidden_own, full_up, up_bias)
    active_other, slope_other = up_gelu(hidden_other, full_up, up_bias)
    if staged:
        active_other, active_own, down_far = lax.optimization_barrier(
            (active_other, active_own, down_far)
        )
        (full_down,) = place(spot, (down_deep, down_other, down_far), [up_width])
    other = swap(low(mm_nt(active_other, full_down)))
    layer_out, grad_res_two, grad_own, sums_two = norm_two(
        item_lengths,
        mm_nt(active_own, full_down),
        other,
        normed_one_out,
        out_grad,
        down_bias,
        second_gain,
        second_shift,
        position,
    )
    grad_other = swap(grad_own)
    grad_upper_own, up_sum_own = back_slope(grad_own, full_down, slope_own)
    down_local = outer([grad_own, grad_other], [active_own, active_other])
    grad_other, down_local = lax.optimization_barrier((grad_other, down_local))
    if staged:
        down_got = first_quad(sum_first([down_local], spot))
    grad_upper_other, up_sum_other = back_slope(grad_other, full_down, slope_other)
    other = swap(low(mm_nt(grad_upper_other, full_up)))
    up_local = outer([hidden_own, hidden_other], [grad_upper_own, grad_upper_other])
    grad_res_one, grad_proj_own, sums_one = norm_one_back(
        mm_nt(grad_upper_own, full_up), other, grad_res_two, normed_one, inverse_one, first_gain
    )
    grad_proj_other = swap(grad_proj_own)
    shared = jnp.concatenate([sums_one, sums_two], axis=0)
    shared_other = swap(shared)
    grad_attended = project_both(grad_proj_own, grad_proj_other, full_out)
    out_local = outer([grad_proj_own, grad_proj_other], [attended])

    mids = [out_local, up_local]
    split = pair_count - 1
    if staged:
        grad_attended, down_got = lax.optimization_barrier((grad_attended, down_got))
        mid_got = first_quad(sum_first(mids, spot))
        down_two = second_quad(sum_second([down_local], spot, down_got))
    grads_a, sums_a = attention_backward(
        item_lengths, random_blocks, triple, grad_attended, range(split), position
    )
    if staged:
        grads_a, mid_got, down_two, grad_attended = lax.optimization_barrier(
            (grads_a, mid_got, down_two, grad_attended)
        )
        down_sum, *messages = sum_deep([[down_local]], spot, [down_got], [down_two])
        down_answers = [deep_step(m, deep, k + 1) for k, m in enumerate(messages)]
        mid_two = second_quad(sum_second(mids, spot, mid_got))
    local_a = outer([inputs, tokens_other], [grads_a])
    if staged:
        got_a = first_quad(sum_first([local_a], spot))
        grad_attended, local_a = lax.optimization_barrier((grad_attended, local_a))
    grads_b, sums_b = attention_backward(
        item_lengths, random_blocks, triple, grad_attended, range(split, pair_count), position
    )
    if staged:
        grads_b, got_a, mid_two, *down_answers = lax.optimization_barrier(
            (grads_b, got_a, mid_two, *down_answers)
        )
    local_b = outer([inputs, tokens_other], [grads_b])
    small = small_sums(shared, shared_other, up_sum_own, up_sum_other, [sums_a, sums_b])
    if staged:
        got_b = first_quad(sum_first([local_b], spot, small))
        two_a = second_quad(sum_second([local_a], spot, got_a))
        mid_sum, *messages = sum_deep([mids], spot, [after(mid_got, local_b)], [mid_two])
        mid_answers = [deep_step(m, deep, k + 1) for k, m in enumerate(messages)]

    cut = split * 3 * PAIR
    grads_a, grads_b, local_b = lax.optimization_barrier((grads_a, grads_b, local_b))
    other = swap(
        low(mm_nt(grads_a[half:], full_qkv[:, :cut]) + mm_nt(grads_b[half:], full_qkv[:, cut:]))
    )
    mine = mm_nt(grads_a[:half], full_qkv[:, :cut]) + mm_nt(grads_b[:half], full_qkv[:, cut:])
    if staged:
        mine, other, got_b, two_a = lax.optimization_barrier((mine, other, got_b, two_a))
        message, small = sum_second([local_b], spot, got_b, small)
        two_b = second_quad(message)
    input_grad = low(mine + other.astype(jnp.float32) + grad_res_one)
    if staged:
        (grad_down,) = sum_last(down_sum, down_answers, [up_width])
        input_grad, grad_down, two_b = lax.optimization_barrier((input_grad, grad_down, two_b))
        small, qkv_sum, *messages = sum_deep(
            [[local_a], [local_b]], spot, [got_a, got_b], [two_a, two_b], small
        )
        answers = [deep_step(m, deep, k + 1) for k, m in enumerate(messages)]
        grad_out, grad_up = sum_last(mid_sum, mid_answers, [head_width, up_width])
        grad_out, grad_up, *answers = lax.optimization_barrier((grad_out, grad_up, *answers))
        grad_qkv, small = sum_last(qkv_sum, answers, [3 * head_width], small)
    else:
        grad_down, grad_up, grad_out = (scattered(v) for v in (down_local, up_local, out_local))
        grad_qkv = scattered(jnp.concatenate([local_a, local_b], axis=1))
        small = lax.psum(small, every)
        part = small.shape[0] // 3
        small = jnp.concatenate([small[n * part : (n + 1) * part] for n in range(3)], axis=1)

    totals = small[:, :width]
    grad_up_bias = small[: up_width // head_width, width:].reshape(up_width)
    grad_qv_bias = small[up_width // head_width :, width:]
    return (
        layer_out,
        input_grad,
        by_kind(grad_qkv, 3),
        grad_qv_bias,
        grad_out,
        totals[0],
        totals[1],
        totals[2],
        grad_up,
        grad_up_bias,
        grad_down,
        totals[3],
        totals[4],
        totals[5],
    )


def solution(mesh):
    devices = mesh.devices.reshape(-1, QUAD, mesh.shape["head"])
    fine = Mesh(devices, ("deep", "quad", "head"))
    rows = ("deep", "quad", "head")
    dp = ("deep", "quad")
    in_specs = (
        P(rows, None),
        P(dp, None, "head"),
        P(None, "head"),
        P(dp, "head"),
        P(),
        P(),
        P(),
        P(dp, "head"),
        P("head"),
        P(dp, "head"),
        P(),
        P(),
        P(),
        P(dp, None),
        P(dp, "head", None, None),
        P(rows, None),
    )
    out_specs = (
        P(rows, None),
        P(rows, None),
        P(dp, None, "head"),
        P(None, "head"),
        P(dp, "head"),
        P(),
        P(),
        P(),
        P(dp, "head"),
        P("head"),
        P(dp, "head"),
        P(),
        P(),
        P(),
    )
    return jax.shard_map(
        on_device, mesh=fine, in_specs=in_specs, out_specs=out_specs, check_vma=False
    )
```

```python
import functools

import jax
import jax.numpy as jnp
import numpy as np
from jax import lax
from jax.experimental import pallas as pl
from jax.experimental.pallas import tpu as pltpu
from jax.sharding import Mesh
from jax.sharding import PartitionSpec as P

BLK = 64


norm_eps = 1e-06
negative = -1e30


def norm_forward(values, gain, shift):
    centered = values - jnp.mean(values, axis=-1, keepdims=True)
    inverse = lax.rsqrt(jnp.mean(centered * centered, axis=-1, keepdims=True) + norm_eps)
    normed = centered * inverse
    return (normed * gain + shift, normed, inverse)


def dot_nt(a, b):
    return lax.dot_general(a, b, (((1,), (1,)), ((), ())), preferred_element_type=jnp.float32)


def dot_nn(a, b):
    return lax.dot_general(a, b, (((1,), (0,)), ((), ())), preferred_element_type=jnp.float32)


def dot_tn(a, b):
    return lax.dot_general(a, b, (((0,), (0,)), ((), ())), preferred_element_type=jnp.float32)


PAIR = 2 * BLK


def even_lanes(rows):
    return lax.broadcasted_iota(jnp.int32, (rows, PAIR), 1) < BLK


def stacked(values):
    zero = jnp.zeros_like(values)
    even = even_lanes(BLK)
    return jnp.concatenate([jnp.where(even, values, zero), jnp.where(even, zero, values)], axis=0)


def unstacked(values):
    return jnp.where(even_lanes(BLK), values[:BLK], values[BLK:])


class Layout:
    def __init__(self, len_ref, rb_ref, blocks, position):
        self.len_ref, self.rb_ref, self.blocks = len_ref, rb_ref, blocks
        self.half = blocks // 2
        self.rand = rb_ref.shape[-1]
        self.shift = position * self.half

    def moved(self, index):
        at = index + self.shift
        return jnp.where(at >= self.blocks, at - self.blocks, at)

    def spot(self, index):
        return pl.ds(pl.multiple_of(self.moved(index) * BLK, BLK), BLK)

    def part(self, index):
        return pl.ds(pl.multiple_of(self.moved(index) * BLK, BLK), self.half * BLK)

    def counts(self):
        self.count0 = lax.div(self.len_ref[0, 0], BLK)
        self.count1 = lax.div(self.len_ref[0, 1], BLK)
        self.second = jnp.where(self.count1 > 0, 1, 0)
        self.inner = self.blocks - 2 - 2 * self.second

    def locate(self, i):
        in0 = i < self.count0 - 2
        self.b = b = jnp.where(in0, i + 1, i + 2 + self.second)
        self.live = live = b < self.count0 + self.count1
        self.first = first = jnp.where(in0, 0, jnp.where(live, self.count0, b))
        items = jnp.where(in0, self.count0, jnp.where(live, self.count1, 1))
        rel = b - first
        last = items - 1
        zero, neg = jnp.float32(0.0), jnp.float32(negative)
        self.fixed = [
            first,
            first + last,
            jnp.where(live, b - 1, b),
            jnp.where(live, b + 1, b),
            b,
        ]
        self.low_bias = jnp.where(live & (rel == 1), neg, zero)
        self.high_bias = jnp.where(live & (rel + 1 == last), neg, zero)
        return self

    def ends(self, item):
        first = jnp.where(item == 0, 0, self.count0)
        count = jnp.where(item == 0, self.count0, self.count1)
        return first, first + count - 1, lax.div(count, self.half)

    def chosen(self, head):
        return [
            jnp.where(self.live, self.first + self.rb_ref[0, head, self.b, k], self.b)
            for k in range(self.rand)
        ]


def gathered(ref, layout, column, picked):
    even = even_lanes(BLK)

    def rows(index):
        return ref[layout.spot(index), column : column + PAIR]

    return jnp.concatenate(
        [rows(i) for i in layout.fixed]
        + [jnp.where(even, rows(i), rows(j)) for i, j in zip(*picked)],
        axis=0,
    )


ROWS = 32


def soft_rows(held):
    probs, inverse = [], []
    for row in range(0, held.shape[0], ROWS):
        scores = held[row : row + ROWS, :]
        expo = jnp.exp(scores - jnp.max(scores, axis=1, keepdims=True))
        inverse.append(1.0 / jnp.sum(expo, axis=1, keepdims=True))
        probs.append(expo.astype(jnp.bfloat16))
    return jnp.concatenate(probs, axis=0), jnp.concatenate(inverse, axis=0)


def attn_fwd_kernel(pairs, position, len_ref, rb_ref, tri_ref, out_ref, wide, *held):
    blocks = tri_ref.shape[0] // BLK
    scale = jnp.bfloat16(BLK**-0.5)
    layout = Layout(len_ref, rb_ref, blocks, position())
    layout.counts()

    def query_of(p, b):
        at = layout.spot(b)
        return stacked(tri_ref[at, p * 3 * PAIR : p * 3 * PAIR + PAIR]) * scale

    def put(p, b, mixed):
        at = layout.spot(b)
        out_ref[at, p * PAIR : (p + 1) * PAIR] = unstacked(mixed).astype(jnp.bfloat16)

    def sparse_scores(i, held):
        at = layout.locate(i)
        lane = lax.broadcasted_iota(jnp.int32, (1, PAIR), 1) < BLK
        bias_row = jnp.where(lane, at.low_bias, at.high_bias)
        for n, p in enumerate(pairs):
            picked = [at.chosen(2 * p), at.chosen(2 * p + 1)]
            keys = gathered(tri_ref, at, (3 * p + 1) * PAIR, picked)
            scores = dot_nt(query_of(p, at.b), keys)
            held[n][...] = jnp.concatenate(
                [scores[:, :PAIR], scores[:, PAIR : 2 * PAIR] + bias_row, scores[:, 2 * PAIR :]],
                axis=1,
            )

    def sparse_mix(i, held):
        at = layout.locate(i)
        for n, p in enumerate(pairs):
            picked = [at.chosen(2 * p), at.chosen(2 * p + 1)]
            probs, inverse = soft_rows(held[n])
            values = gathered(tri_ref, at, (3 * p + 2) * PAIR, picked)
            put(p, at.b, dot_nn(probs, values) * inverse)

    held_a, held_b = held[: len(pairs)], held[len(pairs) :]
    sparse_scores(0, held_a)

    def two(j, carry):
        sparse_scores(2 * j + 1, held_b)
        sparse_mix(2 * j, held_a)
        sparse_scores(jnp.minimum(2 * j + 2, layout.inner - 1), held_a)
        sparse_mix(2 * j + 1, held_b)
        return carry

    lax.fori_loop(0, lax.div(layout.inner, 2), two, 0)

    def dense(item, carry):
        first, last, chunks = layout.ends(item)
        queries = [
            jnp.concatenate([query_of(p, first), query_of(p, last)], axis=0) for p in pairs
        ]

        def dense_of(spans):
            for query, p in zip(queries, pairs):
                span = layout.half * BLK
                for c, at in enumerate(spans):
                    keys = tri_ref[at, (3 * p + 1) * PAIR : (3 * p + 2) * PAIR]
                    wide[:, c * span : (c + 1) * span] = dot_nt(query, keys)
                probs, inverse = soft_rows(wide.at[:, : len(spans) * span])
                mixed = sum(
                    dot_nn(
                        probs[:, c * span : (c + 1) * span],
                        tri_ref[at, (3 * p + 2) * PAIR : (3 * p + 3) * PAIR],
                    )
                    for c, at in enumerate(spans)
                ) * inverse
                put(p, first, mixed[:PAIR])
                put(p, last, mixed[PAIR:])

        @pl.when(chunks == 1)
        def short():
            dense_of([layout.part(first)])

        @pl.when(chunks == 2)
        def long():
            dense_of([layout.part(first), layout.part(first + layout.half)])

        return carry

    lax.fori_loop(0, 1 + layout.second, dense, 0)


def grad_rows(held_scores, held_grads, probs_ref, grads_ref):
    for row in range(0, held_scores.shape[0], ROWS):
        at = slice(row, row + ROWS)
        scores = held_scores[at, :]
        grad_probs = held_grads[at, :]
        expo = jnp.exp(scores - jnp.max(scores, axis=1, keepdims=True))
        probs = expo * (1.0 / jnp.sum(expo, axis=1, keepdims=True))
        delta = jnp.sum(probs * grad_probs, axis=1, keepdims=True)
        probs_ref[at, :] = probs.astype(jnp.bfloat16)
        grads_ref[at, :] = (probs * (grad_probs - delta)).astype(jnp.bfloat16)


def attn_bwd_kernel(
    pairs, position, len_ref, rb_ref, tri_ref, grad_ref, out_ref, sum_ref, *scratch
):
    blocks = tri_ref.shape[0] // BLK
    scale = jnp.bfloat16(BLK**-0.5)
    back = BLK**-0.5
    layout = Layout(len_ref, rb_ref, blocks, position())
    layout.counts()
    count = len(pairs)
    key_acc, value_acc = scratch[:count], scratch[count : 2 * count]
    held_a, held_b, done = (scratch[n * count : (n + 2) * count] for n in (2, 4, 6))
    wide = scratch[8 * count :]

    def clear(r, carry):
        at = pl.ds(pl.multiple_of(r * BLK, BLK), BLK)
        for acc in scratch[: 2 * count]:
            acc[at, :] = jnp.zeros((BLK, PAIR), jnp.float32)
        return carry

    lax.fori_loop(0, blocks, clear, 0)

    def query_of(p, b):
        at = layout.spot(b)
        return stacked(tri_ref[at, p * 3 * PAIR : p * 3 * PAIR + PAIR]) * scale

    def grad_of(p, b):
        at = layout.spot(b)
        return stacked(grad_ref[at, p * PAIR : (p + 1) * PAIR])

    def put(i, b, grad_query):
        out_ref[layout.spot(b), i * 3 * PAIR : i * 3 * PAIR + PAIR] = unstacked(
            grad_query * back
        ).astype(jnp.bfloat16)

    def sparse_scores(n, held):
        at = layout.locate(n)
        lane = lax.broadcasted_iota(jnp.int32, (1, PAIR), 1) < BLK
        bias_row = jnp.where(lane, at.low_bias, at.high_bias)
        for i, p in enumerate(pairs):
            picked = [at.chosen(2 * p), at.chosen(2 * p + 1)]
            keys = gathered(tri_ref, at, (3 * p + 1) * PAIR, picked)
            values = gathered(tri_ref, at, (3 * p + 2) * PAIR, picked)
            scores = dot_nt(query_of(p, at.b), keys)
            held[2 * i][...] = jnp.concatenate(
                [scores[:, :PAIR], scores[:, PAIR : 2 * PAIR] + bias_row, scores[:, 2 * PAIR :]],
                axis=1,
            )
            held[2 * i + 1][...] = dot_nt(grad_of(p, at.b), values)

    def sparse_grads(n, held):
        at = layout.locate(n)
        even = even_lanes(BLK)
        for i, p in enumerate(pairs):
            grad_rows(held[2 * i], held[2 * i + 1], done[2 * i], done[2 * i + 1])
            picked = [at.chosen(2 * p), at.chosen(2 * p + 1)]
            spots = [at.spot(index) for index in at.fixed]
            spots += [(at.spot(one), at.spot(two)) for one, two in zip(*picked)]
            keys = gathered(tri_ref, at, (3 * p + 1) * PAIR, picked)
            put(i, at.b, dot_nn(done[2 * i + 1][...], keys))
            for acc, update in (
                (key_acc[i], dot_tn(done[2 * i + 1][...], query_of(p, at.b))),
                (value_acc[i], dot_tn(done[2 * i][...], grad_of(p, at.b))),
            ):
                for j, spot in enumerate(spots):
                    piece = update[j * BLK : (j + 1) * BLK]
                    if j < len(at.fixed):
                        acc[spot, :] += piece
                    else:
                        zero = jnp.zeros_like(piece)
                        acc[spot[0], :] += jnp.where(even, piece, zero)
                        acc[spot[1], :] += jnp.where(even, zero, piece)

    sparse_scores(0, held_a)

    def two(j, carry):
        sparse_scores(2 * j + 1, held_b)
        sparse_grads(2 * j, held_a)
        sparse_scores(jnp.minimum(2 * j + 2, layout.inner - 1), held_a)
        sparse_grads(2 * j + 1, held_b)
        return carry

    lax.fori_loop(0, lax.div(layout.inner, 2), two, 0)

    wide_scores, wide_grads, wide_probs, wide_out = wide

    def dense(item, carry):
        first, last, chunks = layout.ends(item)

        def dense_of(spans):
            span = layout.half * BLK
            cover = len(spans) * span
            def end(n, carry):
                b = jnp.where(n == 0, first, last)
                for i, p in enumerate(pairs):
                    query, grad = query_of(p, b), grad_of(p, b)
                    for c, at in enumerate(spans):
                        cut = slice(c * span, (c + 1) * span)
                        keys = tri_ref[at, (3 * p + 1) * PAIR : (3 * p + 2) * PAIR]
                        values = tri_ref[at, (3 * p + 2) * PAIR : (3 * p + 3) * PAIR]
                        wide_scores[:, cut] = dot_nt(query, keys)
                        wide_grads[:, cut] = dot_nt(grad, values)
                    grad_rows(*(ref.at[:, :cover] for ref in wide))
                    total = jnp.zeros((PAIR, PAIR), jnp.float32)
                    for c, at in enumerate(spans):
                        cut = slice(c * span, (c + 1) * span)
                        keys = tri_ref[at, (3 * p + 1) * PAIR : (3 * p + 2) * PAIR]
                        total += dot_nn(wide_out[:, cut], keys)
                        key_acc[i][at, :] += dot_tn(wide_out[:, cut], query)
                        value_acc[i][at, :] += dot_tn(wide_probs[:, cut], grad)
                    put(i, b, total)
                return carry

            lax.fori_loop(0, 2, end, 0)

        @pl.when(chunks == 1)
        def short():
            dense_of([layout.part(first)])

        @pl.when(chunks == 2)
        def long():
            dense_of([layout.part(first), layout.part(first + layout.half)])

        return carry

    lax.fori_loop(0, 1 + layout.second, dense, 0)

    sum_ref[...] = jnp.zeros_like(sum_ref)

    def finish(r, carry):
        at = pl.ds(pl.multiple_of(r * BLK, BLK), BLK)
        new = []
        for i in range(count):
            column = i * 3 * PAIR
            query_sum, value_sum = carry[i]
            out_ref[at, column + PAIR : column + 2 * PAIR] = key_acc[i][at, :].astype(jnp.bfloat16)
            value = value_acc[i][at, :].astype(jnp.bfloat16)
            out_ref[at, column + 2 * PAIR : column + 3 * PAIR] = value
            query = out_ref[at, column : column + PAIR].astype(jnp.float32)
            new.append(
                tuple(
                    total + jnp.sum(part.reshape(-1, 8, PAIR), axis=0)
                    for total, part in (
                        (query_sum, query),
                        (value_sum, value.astype(jnp.float32)),
                    )
                )
            )
        return tuple(new)

    zero = jnp.zeros((8, PAIR), jnp.float32)
    sums = lax.fori_loop(0, blocks, finish, tuple((zero, zero) for _ in pairs))
    for i, totals in enumerate(sums):
        for kind, total in enumerate(totals):
            sum_ref[kind : kind + 1, i * PAIR : (i + 1) * PAIR] = jnp.sum(
                total, axis=0, keepdims=True
            )


vmem = pl.BlockSpec(memory_space=pltpu.VMEM)
smem = pl.BlockSpec(memory_space=pltpu.SMEM)
def attention_forward(lengths, randoms, triple, position):
    pairs = randoms.shape[1] // 2
    rows = triple.shape[0]
    area = rows * rows // 3 * 2 * pairs
    return pl.pallas_call(
        functools.partial(attn_fwd_kernel, range(pairs), position),
        out_shape=jax.ShapeDtypeStruct((rows, pairs * PAIR), jnp.bfloat16),
        in_specs=[smem, smem, vmem],
        out_specs=vmem,
        name="attend_forward",
        scratch_shapes=[pltpu.VMEM((2 * PAIR, rows), jnp.float32)]
        + [pltpu.VMEM((PAIR, 8 * BLK), jnp.float32)] * (2 * pairs),
        cost_estimate=pl.CostEstimate(
            flops=16 * area * PAIR, transcendentals=area, bytes_accessed=rows * pairs * PAIR * 8
        ),
        compiler_params=pltpu.CompilerParams(vmem_limit_bytes=8 << 20),
    )(lengths, randoms, triple)


def attention_backward(lengths, randoms, triple, grad, pairs, position):
    rows = triple.shape[0]
    count = len(pairs)
    area = rows * rows // 3 * 2 * count
    return pl.pallas_call(
        functools.partial(attn_bwd_kernel, pairs, position),
        out_shape=(
            jax.ShapeDtypeStruct((rows, count * 3 * PAIR), jnp.bfloat16),
            jax.ShapeDtypeStruct((8, count * PAIR), jnp.float32),
        ),
        in_specs=[smem, smem, vmem, vmem],
        out_specs=(vmem, vmem),
        name="attend_backward",
        scratch_shapes=[pltpu.VMEM((rows, PAIR), jnp.float32)] * (2 * count)
        + [pltpu.VMEM((PAIR, 8 * BLK), jnp.float32)] * (4 * count)
        + [pltpu.VMEM((PAIR, 8 * BLK), jnp.bfloat16)] * (2 * count)
        + [pltpu.VMEM((PAIR, rows), kind) for kind in (jnp.float32,) * 2 + (jnp.bfloat16,) * 2],
        cost_estimate=pl.CostEstimate(
            flops=40 * area * PAIR, transcendentals=area, bytes_accessed=rows * count * PAIR * 20
        ),
        compiler_params=pltpu.CompilerParams(vmem_limit_bytes=20 << 20),
    )(lengths, randoms, triple, grad)


TILE = 256
EPS = 1e-06


def tile_at(n):
    return pl.ds(pl.multiple_of(n * TILE, TILE), TILE)


def up_kernel(rows_ref, weight_ref, bias_ref, active_ref, slope_ref, held_a, held_b):
    tiles = weight_ref.shape[1] // TILE
    root = (2.0 / np.pi) ** 0.5
    cube = 0.044715 * root

    def product(n, held):
        held[...] = dot_nn(rows_ref[...], weight_ref[:, tile_at(n)])

    def gelu(n, held):
        bias = bias_ref[:, tile_at(n)]
        for row in range(0, held.shape[0], ROWS):
            at = slice(row, row + ROWS)
            upper = (held[at, :] + bias).astype(jnp.bfloat16).astype(jnp.float32)
            square = upper * upper
            half = 0.5 + 0.5 * jnp.tanh(upper * (square * cube + root))
            active = upper * half
            active_ref[at, tile_at(n)] = active.astype(jnp.bfloat16)
            bend = (1.0 - half) * (square * (6.0 * cube) + 2.0 * root)
            slope_ref[at, tile_at(n)] = (half + active * bend).astype(jnp.bfloat16)

    product(0, held_a)

    def two(j, carry):
        product(2 * j + 1, held_b)
        gelu(2 * j, held_a)
        product(jnp.minimum(2 * j + 2, tiles - 1), held_a)
        gelu(2 * j + 1, held_b)
        return carry

    lax.fori_loop(0, tiles // 2, two, 0)


def up_gelu(rows, weight, bias):
    count, width = rows.shape[0], weight.shape[1]
    shape = jax.ShapeDtypeStruct((count, width), jnp.bfloat16)
    return pl.pallas_call(
        up_kernel,
        out_shape=(shape, shape),
        in_specs=[vmem] * 3,
        out_specs=(vmem, vmem),
        name="up_gelu",
        scratch_shapes=[pltpu.VMEM((count, TILE), jnp.float32)] * 2,
        cost_estimate=pl.CostEstimate(
            flops=2 * count * width * rows.shape[1],
            transcendentals=count * width,
            bytes_accessed=2 * (rows.size + weight.size + 2 * count * width),
        ),
        compiler_params=pltpu.CompilerParams(vmem_limit_bytes=12 << 20),
    )(rows, weight, bias.reshape(1, -1))


def back_kernel(grad_ref, weight_ref, slope_ref, out_ref, sum_ref):
    def step(n, carry):
        grad_active = dot_nn(grad_ref[...], weight_ref[:, tile_at(n)])
        total = jnp.zeros((8, TILE), jnp.float32)
        for row in range(0, grad_active.shape[0], ROWS):
            at = slice(row, row + ROWS)
            grad = grad_active[at] * slope_ref[at, tile_at(n)].astype(jnp.float32)
            grad = grad.astype(jnp.bfloat16)
            out_ref[at, tile_at(n)] = grad
            total += jnp.sum(grad.astype(jnp.float32).reshape(-1, 8, TILE), axis=0)
        sum_ref[:, tile_at(n)] = total
        return carry

    lax.fori_loop(0, weight_ref.shape[1] // TILE, step, 0)


def back_slope(grad, weight, slope):
    count, width = slope.shape
    return pl.pallas_call(
        back_kernel,
        out_shape=(
            jax.ShapeDtypeStruct((count, width), jnp.bfloat16),
            jax.ShapeDtypeStruct((8, width), jnp.float32),
        ),
        in_specs=[vmem] * 3,
        out_specs=(vmem, vmem),
        name="back_slope",
        cost_estimate=pl.CostEstimate(
            flops=2 * count * width * grad.shape[1],
            transcendentals=0,
            bytes_accessed=2 * (grad.size + weight.size + 2 * count * width),
        ),
        compiler_params=pltpu.CompilerParams(vmem_limit_bytes=12 << 20),
    )(grad, weight, slope)


def outer_kernel(count, *refs):
    lefts, rights, out_ref = refs[:count], refs[count:-1], refs[-1]
    if len(rights) < count:
        rows = lefts[0].shape[0]
        rights = [rights[0].at[n * rows : (n + 1) * rows] for n in range(count)]

    def step(at):
        total = sum(dot_tn(a[...], b[:, at]) for a, b in zip(lefts, rights))
        out_ref[:, at] = total.astype(jnp.bfloat16)

    width = out_ref.shape[1]
    if width % TILE:
        step(slice(0, width))
    else:

        def body(n, carry):
            step(tile_at(n))
            return carry

        lax.fori_loop(0, width // TILE, body, 0)


def outer(lefts, rights):
    shape = (lefts[0].shape[1], rights[0].shape[1])
    inner = sum(a.shape[0] for a in lefts)
    return pl.pallas_call(
        functools.partial(outer_kernel, len(lefts)),
        out_shape=jax.ShapeDtypeStruct(shape, jnp.bfloat16),
        in_specs=[vmem] * (len(lefts) + len(rights)),
        out_specs=vmem,
        name="outer",
        cost_estimate=pl.CostEstimate(
            flops=2 * inner * shape[0] * shape[1],
            transcendentals=0,
            bytes_accessed=2 * inner * sum(shape),
        ),
        compiler_params=pltpu.CompilerParams(vmem_limit_bytes=12 << 20),
    )(*lefts, *rights)


def project_kernel(own_ref, other_ref, weight_ref, out_ref):
    rows = own_ref.shape[0]
    for n, ref in enumerate((own_ref, other_ref)):
        product = dot_nn(ref[...], weight_ref[...])
        out_ref[n * rows : (n + 1) * rows, :] = product.astype(jnp.bfloat16)


def project_both(own, other, weight):
    return pl.pallas_call(
        project_kernel,
        out_shape=jax.ShapeDtypeStruct((2 * own.shape[0], weight.shape[1]), jnp.bfloat16),
        in_specs=[vmem] * 3,
        out_specs=vmem,
        name="project_both",
        compiler_params=pltpu.CompilerParams(vmem_limit_bytes=12 << 20),
    )(own, other, weight)


GROUP = 16
SPLIT = 4


def groups_at(r):
    return [
        (r * SPLIT + n, pl.ds(pl.multiple_of((r * SPLIT + n) * GROUP, GROUP), GROUP))
        for n in range(SPLIT)
    ]


def row_mean(values):
    return jnp.sum(values, axis=1, keepdims=True) * (1.0 / values.shape[1])


def folded(values):
    return jnp.sum(values.reshape(-1, 8, values.shape[1]), axis=0)


def norm_two_kernel(position, len_ref, down_ref, other_ref, resid_ref, cot_ref, vec_ref, out_ref, grad_ref, low_ref, sum_ref):
    count, width = down_ref.shape
    live_rows = len_ref[0, 0] + len_ref[0, 1] - position() * count
    bias, gain, shift = (vec_ref[n : n + 1, :] for n in range(3))

    def group(r, at, sums):
        row = r * GROUP + lax.broadcasted_iota(jnp.int32, (GROUP, 1), 0)
        live = jnp.where(row < live_rows, 1.0, 0.0)
        values = down_ref[at, :] + other_ref[at, :].astype(jnp.float32) + bias + resid_ref[at, :]
        centered = values - row_mean(values)
        inverse = lax.rsqrt(row_mean(centered * centered) + EPS)
        normed = centered * inverse
        out_ref[at, :] = ((normed * gain + shift) * live).astype(jnp.bfloat16)
        cot = cot_ref[at, :].astype(jnp.float32) * live
        scaled = cot * gain
        grad = inverse * (scaled - row_mean(scaled) - normed * row_mean(scaled * normed))
        grad_ref[at, :] = grad
        low_ref[at, :] = grad.astype(jnp.bfloat16)
        return tuple(s + folded(v) for s, v in zip(sums, (grad, cot * normed, cot)))

    def step(r, sums):
        for n, at in groups_at(r):
            sums = group(n, at, sums)
        return sums

    zero = jnp.zeros((8, width), jnp.float32)
    sums = lax.fori_loop(0, count // (GROUP * SPLIT), step, (zero,) * 3)
    for n, total in enumerate(sums):
        sum_ref[n : n + 1, :] = jnp.sum(total, axis=0, keepdims=True)
    sum_ref[3:8, :] = jnp.zeros((5, width), jnp.float32)


def norm_two(lengths, down, other, resid, cot, bias, gain, shift, position):
    shape = down.shape
    row = jax.ShapeDtypeStruct((8, shape[1]), jnp.float32)
    return pl.pallas_call(
        functools.partial(norm_two_kernel, position),
        out_shape=(
            jax.ShapeDtypeStruct(shape, jnp.bfloat16),
            jax.ShapeDtypeStruct(shape, jnp.float32),
            jax.ShapeDtypeStruct(shape, jnp.bfloat16),
            row,
        ),
        in_specs=[smem] + [vmem] * 5,
        out_specs=(vmem,) * 4,
        name="norm_two",
        cost_estimate=pl.CostEstimate(
            flops=40 * down.size, transcendentals=0, bytes_accessed=20 * down.size
        ),
        compiler_params=pltpu.CompilerParams(vmem_limit_bytes=12 << 20),
    )(lengths, down, other, resid, cot, jnp.stack([bias, gain, shift]))


def norm_one_kernel(own_ref, other_ref, grad_ref, normed_ref, inverse_ref, gain_ref, out_ref, low_ref, sum_ref):
    count, width = own_ref.shape
    gain = gain_ref[...]

    def group(r, at, sums):
        grad = own_ref[at, :] + other_ref[at, :].astype(jnp.float32) + grad_ref[at, :]
        normed = normed_ref[at, :]
        scaled = grad * gain
        result = inverse_ref[at, :] * (
            scaled - row_mean(scaled) - normed * row_mean(scaled * normed)
        )
        out_ref[at, :] = result
        low_ref[at, :] = result.astype(jnp.bfloat16)
        return tuple(s + folded(v) for s, v in zip(sums, (result, grad * normed, grad)))

    def step(r, sums):
        for n, at in groups_at(r):
            sums = group(n, at, sums)
        return sums

    zero = jnp.zeros((8, width), jnp.float32)
    sums = lax.fori_loop(0, count // (GROUP * SPLIT), step, (zero,) * 3)
    for n, total in enumerate(sums):
        sum_ref[n : n + 1, :] = jnp.sum(total, axis=0, keepdims=True)
    sum_ref[3:8, :] = jnp.zeros((5, width), jnp.float32)


def norm_one_back(own, other, grad, normed, inverse, gain):
    shape = own.shape
    return pl.pallas_call(
        norm_one_kernel,
        out_shape=(
            jax.ShapeDtypeStruct(shape, jnp.float32),
            jax.ShapeDtypeStruct(shape, jnp.bfloat16),
            jax.ShapeDtypeStruct((8, shape[1]), jnp.float32),
        ),
        in_specs=[vmem] * 6,
        out_specs=(vmem,) * 3,
        name="norm_one_back",
        cost_estimate=pl.CostEstimate(
            flops=20 * own.size, transcendentals=0, bytes_accessed=20 * own.size
        ),
        compiler_params=pltpu.CompilerParams(vmem_limit_bytes=12 << 20),
    )(own, other, grad, normed, inverse, gain.reshape(1, -1))


def pack_rows(ref, at, small):
    rows = small.shape[0]
    high = small.astype(jnp.bfloat16)
    ref[at : at + rows, :] = high
    ref[at + rows : at + 2 * rows, :] = (small - high.astype(jnp.float32)).astype(jnp.bfloat16)


def unpack_rows(ref, at, rows):
    high = ref[at : at + rows, :].astype(jnp.float32)
    return high + ref[at + rows : at + 2 * rows, :].astype(jnp.float32)


def slab_at(at_ref, place, z, rows):
    return pl.ds(pl.multiple_of((z * QUAD + at_ref[place]) * rows, rows), rows)


def columns_of(totals):
    cuts, low = [], 0
    for total in totals:
        cuts.append(slice(low, low + total.shape[1]))
        low += total.shape[1]
    return cuts


def sum_first_kernel(count, deep, at_ref, *refs):
    totals, rest = refs[:count], refs[count:]
    out_ref = rest[-1]
    rows = totals[0].shape[0] // (deep * QUAD)
    for part, place in enumerate((1, 3)):
        for z in range(deep):
            row = (part * deep + z) * rows
            for total, cut in zip(totals, columns_of(totals)):
                out_ref[row : row + rows, cut] = total[slab_at(at_ref, place, z, rows), :]
    if len(rest) > 1:
        pack_rows(out_ref, 2 * deep * rows, rest[0][...])


def sum_second_kernel(count, deep, at_ref, *refs):
    totals, got_ref = refs[:count], refs[count]
    rows = totals[0].shape[0] // (deep * QUAD)
    if len(refs) > count + 2:
        small_ref, out_ref, new_ref = refs[count + 1 :]
        small = small_ref[...] + unpack_rows(got_ref, 2 * deep * rows, small_ref.shape[0])
        new_ref[...] = small
        pack_rows(out_ref, deep * rows, small)
    else:
        out_ref = refs[-1]
    for z in range(deep):
        for total, cut in zip(totals, columns_of(totals)):
            far = total[slab_at(at_ref, 2, z, rows), :].astype(jnp.float32)
            row = (deep + z) * rows
            far = far + got_ref[row : row + rows, cut].astype(jnp.float32)
            out_ref[z * rows : (z + 1) * rows, cut] = far.astype(jnp.bfloat16)


def sum_deep_kernel(groups, deep, small_rows, at_ref, *refs):
    count = sum(groups)
    totals, refs = refs[:count], refs[count:]
    gots, twos, refs = refs[: len(groups)], refs[len(groups) : 2 * len(groups)], refs[2 * len(groups) :]
    rows = totals[0].shape[0] // (deep * QUAD)
    small = None
    if small_rows:
        small_ref, new_ref, refs = refs[0], refs[1], refs[2:]
        small = small_ref[...] + unpack_rows(twos[-1], deep * rows, small_rows)
        part = new_ref.shape[0]
        cuts = [small[n * part : (n + 1) * part] for n in range(small_rows // part)]
        small = jnp.concatenate(cuts, axis=1)
        new_ref[...] = small
    out_cuts = columns_of(totals)
    for k in range(deep):
        z = at_ref[QUAD] ^ k
        near = pl.ds(pl.multiple_of(z * rows, rows), rows)
        n = 0
        for group, got_ref, two_ref in zip(groups, gots, twos):
            members = totals[n : n + group]
            for total, cut, out_cut in zip(members, columns_of(members), out_cuts[n : n + group]):
                value = (
                    total[slab_at(at_ref, 0, z, rows), :].astype(jnp.float32)
                    + got_ref[near, cut].astype(jnp.float32)
                    + two_ref[near, cut].astype(jnp.float32)
                )
                refs[k][:rows, out_cut] = value.astype(refs[k].dtype)
            n += group
        if k and small is not None:
            pack_rows(refs[k], rows, small)


def sum_last_kernel(count, small_rows, *refs):
    own_ref, answers = refs[0], refs[1 : 1 + count]
    rows = own_ref.shape[0]
    own = own_ref[...]
    for answer in answers:
        own = own + answer[:rows, :].astype(jnp.float32)
    outs = refs[1 + count :]
    if small_rows:
        small_ref, new_ref, outs = outs[0], outs[-1], outs[1:-1]
        small = small_ref[...]
        for answer in answers:
            small = small + unpack_rows(answer, rows, small_rows)
        new_ref[...] = small
    for out_ref, cut in zip(outs, columns_of(outs)):
        out_ref[...] = own[:, cut]


def vmem_call(kernel, outs, operands, name, scalars=1, limit=12):
    outs = [jax.ShapeDtypeStruct(shape, dtype) for shape, dtype in outs]
    return pl.pallas_call(
        kernel,
        out_shape=outs,
        in_specs=[smem] * scalars + [vmem] * (len(operands) - scalars),
        out_specs=[vmem] * len(outs),
        name=name,
        compiler_params=pltpu.CompilerParams(vmem_limit_bytes=limit << 20),
    )(*operands)


def sum_first(totals, spot, small=None):
    span = totals[0].shape[0] // QUAD
    extra = 0 if small is None else 2 * small.shape[0]
    shape = (2 * span + extra, sum(t.shape[1] for t in totals))
    operands = [spot.at, *totals] + ([] if small is None else [small])
    kernel = functools.partial(sum_first_kernel, len(totals), spot.deep)
    return vmem_call(kernel, [(shape, jnp.bfloat16)], operands, "sum_first")[0]


def sum_second(totals, spot, got, small=None):
    span = totals[0].shape[0] // QUAD
    kernel = functools.partial(sum_second_kernel, len(totals), spot.deep)
    operands = [spot.at, *totals, got]
    if small is None:
        outs = [((span, got.shape[1]), jnp.bfloat16)]
        return vmem_call(kernel, outs, operands, "sum_second")[0]
    outs = [((span + 2 * small.shape[0], got.shape[1]), jnp.bfloat16), (small.shape, jnp.float32)]
    return vmem_call(kernel, outs, operands + [small], "sum_second")


def sum_deep(groups, spot, gots, twos, small=None):
    totals = [total for group in groups for total in group]
    rows = totals[0].shape[0] // (QUAD * spot.deep)
    columns = sum(t.shape[1] for t in totals)
    small_rows = 0 if small is None else small.shape[0]
    kernel = functools.partial(
        sum_deep_kernel, [len(group) for group in groups], spot.deep, small_rows
    )
    operands = [spot.at, *totals, *gots, *twos] + ([] if small is None else [small])
    outs, extra = [], 0
    if small is not None:
        part = small_rows // 3
        outs, extra = [((part, columns), jnp.float32)], 2 * part
    outs += [((rows, columns), jnp.float32)]
    outs += [((rows + extra, columns), jnp.bfloat16)] * (spot.deep - 1)
    return vmem_call(kernel, outs, operands, "sum_deep")


def sum_last(own, answers, widths, small=None):
    kernel = functools.partial(
        sum_last_kernel, len(answers), 0 if small is None else small.shape[0]
    )
    operands = [own, *answers] + ([] if small is None else [small])
    outs = [((own.shape[0], w), jnp.float32) for w in widths]
    outs += [] if small is None else [(small.shape, jnp.float32)]
    return vmem_call(kernel, outs, operands, "sum_last", scalars=0)


def small_kernel(own_ref, swapped_ref, up_one_ref, up_two_ref, *refs):
    out_ref = refs[-1]
    columns = out_ref.shape[1]
    both = own_ref[...] + swapped_ref[...]
    rows = [both[0:3], both[8:11]]
    row = 0
    for low in range(0, both.shape[1], columns):
        for part in rows:
            out_ref[row : row + 3, :] = part[:, low : low + columns]
            row += 3
    up = jnp.sum(up_one_ref[...] + up_two_ref[...], axis=0, keepdims=True)
    for low in range(0, up.shape[1], columns):
        out_ref[row : row + 1, :] = up[:, low : low + columns]
        row += 1
    low = 0
    for ref in refs[:-1]:
        out_ref[row : row + 2, low : low + ref.shape[1]] = ref[0:2, :]
        low += ref.shape[1]


def small_sums(own, swapped, up_one, up_two, sums):
    columns = sum(s.shape[1] for s in sums)
    rows = 6 * own.shape[1] // columns + up_one.shape[1] // columns + 2
    return vmem_call(
        small_kernel,
        [((rows, columns), jnp.float32)],
        [own, swapped, up_one, up_two, *sums],
        "small_sums",
        scalars=0,
    )[0]


def rows_kernel(window, cuts, *refs):
    lefts, weight_ref, out_ref = refs[:-2], refs[-2], refs[-1]
    rows = slice(*window)

    def step(n, carry):
        total = sum(
            dot_nt(left[rows, :], weight_ref[tile_at(n), cut]) for left, cut in zip(lefts, cuts)
        )
        out_ref[:, tile_at(n)] = total.astype(out_ref.dtype)
        return carry

    lax.fori_loop(0, out_ref.shape[1] // TILE, step, 0)


def rows_product(lefts, weight, window, dtype):
    shape = (window[1] - window[0], weight.shape[0])
    return pl.pallas_call(
        functools.partial(rows_kernel, window, columns_of(lefts)),
        out_shape=jax.ShapeDtypeStruct(shape, dtype),
        in_specs=[vmem] * (len(lefts) + 1),
        out_specs=vmem,
        name="rows_product",
        cost_estimate=pl.CostEstimate(
            flops=2 * shape[0] * weight.size,
            transcendentals=0,
            bytes_accessed=2 * (shape[0] * sum(weight.shape) + weight.size),
        ),
        compiler_params=pltpu.CompilerParams(vmem_limit_bytes=12 << 20),
    )(*lefts, weight)


def triple_kernel(own_ref, other_ref, weight_ref, bias_ref, out_ref):
    rows = own_ref.shape[0]
    span = 3 * PAIR

    def step(n, carry):
        at = pl.ds(pl.multiple_of(n * span, span), span)
        for k, ref in enumerate((own_ref, other_ref)):
            product = dot_nn(ref[...], weight_ref[:, at]) + bias_ref[:, at]
            out_ref[k * rows : (k + 1) * rows, at] = product.astype(jnp.bfloat16)
        return carry

    lax.fori_loop(0, out_ref.shape[1] // span, step, 0)


def triple_of(own, other, weight, bias):
    shape = (2 * own.shape[0], weight.shape[1])
    return pl.pallas_call(
        triple_kernel,
        out_shape=jax.ShapeDtypeStruct(shape, jnp.bfloat16),
        in_specs=[vmem] * 4,
        out_specs=vmem,
        name="triple",
        cost_estimate=pl.CostEstimate(
            flops=2 * shape[0] * weight.size,
            transcendentals=0,
            bytes_accessed=2 * (shape[0] * sum(weight.shape) + weight.size),
        ),
        compiler_params=pltpu.CompilerParams(vmem_limit_bytes=12 << 20),
    )(own, other, weight, bias.reshape(1, -1))


QUAD = 4


def group_permute(value, deep, target):
    pairs = []
    for z in range(deep):
        for q in range(QUAD):
            for h in range(2):
                to_z, to_q = target(z, q, h)
                pairs.append(((z * QUAD + q) * 2 + h, (to_z * QUAD + to_q) * 2 + h))
    return lax.ppermute(value, ("deep", "quad", "head"), pairs)


def deep_step(value, deep, bit):
    return group_permute(value, deep, lambda z, q, h: (z ^ bit, q))


def quad_step(value, deep, second):
    return group_permute(value, deep, lambda z, q, h: (z, q ^ ((2 >> h) if second else (1 << h))))


def swap(value):
    return lax.ppermute(value, "head", [(0, 1), (1, 0)])


def after(value, *others):
    return lax.optimization_barrier((value,) + others)[0]


class Spot:
    def __init__(self):
        self.z, self.q, self.h = (lax.axis_index(a) for a in ("deep", "quad", "head"))
        self.deep = lax.axis_size("deep")
        one, two = 1 << self.h, 2 >> self.h
        self.places = [self.q, self.q ^ one, self.q ^ two, self.q ^ 3]
        self.at = jnp.stack(self.places + [self.z]).astype(jnp.int32)


def deep_pieces(value, spot):
    return [deep_step(value, spot.deep, k) for k in range(1, spot.deep)]


def place_kernel(deep, windows, at_ref, *refs):
    pieces, outs = refs[:QUAD], refs[QUAD:]
    rows = pieces[0].shape[1]
    for k in range(deep):
        for j, piece in enumerate(pieces):
            row = pl.multiple_of(((at_ref[QUAD] ^ k) * QUAD + at_ref[j]) * rows, rows)
            for out, (low, high) in zip(outs, windows):
                out[pl.ds(row, rows), :] = piece[k, :, low:high]


def place(spot, pieces, widths):
    windows, low = [], 0
    for width in widths:
        windows.append((low, low + width))
        low += width
    deep, rows = pieces[0].shape[:2]
    outs = [((deep * QUAD * rows, width), pieces[0].dtype) for width in widths]
    kernel = functools.partial(place_kernel, deep, windows)
    return vmem_call(kernel, outs, [spot.at, *pieces], "place_pieces", limit=8)


def low(value):
    return value.astype(jnp.bfloat16)


def by_pair(value):
    lead, kinds, columns = value.shape[:-2], value.shape[-2], value.shape[-1]
    split = value.reshape(lead + (kinds, columns // PAIR, PAIR))
    return jnp.swapaxes(split, -3, -2).reshape(lead + (kinds * columns,))


def by_kind(value, kinds):
    lead, columns = value.shape[:-1], value.shape[-1]
    split = value.reshape(lead + (columns // (kinds * PAIR), kinds, PAIR))
    return jnp.swapaxes(split, -3, -2).reshape(lead + (kinds, columns // kinds))


def on_device(
    inputs,
    qkv_weight,
    qv_bias,
    out_weight,
    out_bias,
    first_gain,
    first_shift,
    up_weight,
    up_bias,
    down_weight,
    down_bias,
    second_gain,
    second_shift,
    item_lengths,
    random_blocks,
    out_grad,
):
    half, width = inputs.shape
    spot = Spot()
    deep = spot.deep
    shard = qkv_weight.shape[0]
    head_width = qkv_weight.shape[2]
    up_width = up_weight.shape[1]
    pair_count = head_width // PAIR

    def position():
        return lax.axis_index("head")

    staged = deep == 4 and shard % 16 == 0
    every = ("deep", "quad")

    def gathered_whole(block):
        return lax.all_gather(block, every, axis=0, tiled=True)

    def scattered(total):
        return lax.psum_scatter(total, every, scatter_dimension=0, tiled=True).astype(jnp.float32)

    def first_quad(block):
        return quad_step(block, deep, False)

    def second_quad(block):
        return quad_step(block, deep, True)

    tokens_other = swap(inputs)
    qkv_block = by_pair(qkv_weight)
    mid = jnp.concatenate([out_weight, up_weight], axis=1)
    if staged:
        qkv_pieces = deep_pieces(qkv_block, spot)
        mid_pieces = deep_pieces(after(mid, *qkv_pieces), spot)
        qkv_deep = jnp.stack([qkv_block] + qkv_pieces)
        qkv_other, qkv_far = first_quad(qkv_deep), second_quad(qkv_deep)
        qkv_other, qkv_far, *mid_pieces = lax.optimization_barrier(
            (qkv_other, qkv_far, *mid_pieces)
        )
        qkv_across = second_quad(qkv_other)
        (full_qkv,) = place(spot, (qkv_deep, qkv_other, qkv_far, qkv_across), [3 * head_width])
        full_qkv, *mid_pieces = lax.optimization_barrier((full_qkv, *mid_pieces))
        mid_deep = jnp.stack([mid] + mid_pieces)
        mid_other, mid_far = first_quad(mid_deep), second_quad(mid_deep)
        full_qkv, mid_deep = lax.optimization_barrier((full_qkv, mid_deep))
        down_pieces = deep_pieces(after(down_weight, *mid_pieces), spot)
    else:
        full_qkv = gathered_whole(qkv_block)
        full_mid = gathered_whole(mid)
        full_out, full_up = full_mid[:, :head_width], full_mid[:, head_width:]
        full_down = gathered_whole(down_weight)

    bias = by_pair(jnp.stack([qv_bias[0], jnp.zeros_like(qv_bias[0]), qv_bias[1]]))
    triple = triple_of(inputs, tokens_other, full_qkv, bias)
    attended = attention_forward(item_lengths, random_blocks, triple, position)
    if staged:
        attended, mid_other, mid_far, *down_pieces = lax.optimization_barrier(
            (attended, mid_other, mid_far, *down_pieces)
        )
        mid_across = second_quad(mid_other)
        down_deep = jnp.stack([down_weight] + down_pieces)
        full_out, full_up = place(
            spot, (mid_deep, mid_other, mid_far, mid_across), [head_width, up_width]
        )
        full_out, down_deep = lax.optimization_barrier((full_out, down_deep))
        down_other, down_far = first_quad(down_deep), second_quad(down_deep)

    whole = (half, 2 * half)
    other = swap(rows_product([attended], full_out, whole, jnp.bfloat16))
    proj = rows_product([attended], full_out, (0, half), jnp.float32) + other.astype(jnp.float32)
    normed_one_out, normed_one, inverse_one = norm_forward(
        proj + out_bias + inputs.astype(jnp.float32), first_gain, first_shift
    )
    hidden_own = low(normed_one_out)
    hidden_other = swap(hidden_own)
    active_own, slope_own = up_gelu(hidden_own, full_up, up_bias)
    if staged:
        active_own, down_other, down_far = lax.optimization_barrier(
            (active_own, down_other, down_far)
        )
        down_across = second_quad(down_other)
    active_other, slope_other = up_gelu(hidden_other, full_up, up_bias)
    if staged:
        active_other, active_own, down_across = lax.optimization_barrier(
            (active_other, active_own, down_across)
        )
        (full_down,) = place(spot, (down_deep, down_other, down_far, down_across), [up_width])
    other = swap(rows_product([active_other], full_down, (0, half), jnp.bfloat16))
    layer_out, grad_res_two, grad_own, sums_two = norm_two(
        item_lengths,
        rows_product([active_own], full_down, (0, half), jnp.float32),
        other,
        normed_one_out,
        out_grad,
        down_bias,
        second_gain,
        second_shift,
        position,
    )
    grad_other = swap(grad_own)
    grad_upper_own, up_sum_own = back_slope(grad_own, full_down, slope_own)
    down_local = outer([grad_own, grad_other], [active_own, active_other])
    if staged:
        message = sum_first([down_local], spot)
        down_got = first_quad(message)
        grad_other, message = lax.optimization_barrier((grad_other, message))
    grad_upper_other, up_sum_other = back_slope(grad_other, full_down, slope_other)
    other = swap(rows_product([grad_upper_other], full_up, (0, half), jnp.bfloat16))
    up_local = outer([hidden_own, hidden_other], [grad_upper_own, grad_upper_other])
    grad_res_one, grad_proj_own, sums_one = norm_one_back(
        rows_product([grad_upper_own], full_up, (0, half), jnp.float32), other, grad_res_two, normed_one, inverse_one, first_gain
    )
    if staged:
        grad_proj_own, down_got = lax.optimization_barrier((grad_proj_own, down_got))
        down_message = sum_second([down_local], spot, down_got)
        down_two = second_quad(down_message)
        grad_proj_own, down_message = lax.optimization_barrier((grad_proj_own, down_message))
    grad_proj_other = swap(grad_proj_own)
    shared = jnp.concatenate([sums_one, sums_two], axis=0)
    shared_other = swap(shared)
    grad_attended = project_both(grad_proj_own, grad_proj_other, full_out)
    out_local = outer([grad_proj_own, grad_proj_other], [attended])

    mids = [out_local, up_local]
    split = pair_count - 1
    if staged:
        mid_message = sum_first(mids, spot)
        mid_got = first_quad(mid_message)
        grad_attended, mid_message = lax.optimization_barrier((grad_attended, mid_message))
    grads_a, sums_a = attention_backward(
        item_lengths, random_blocks, triple, grad_attended, range(split), position
    )
    if staged:
        grads_a, mid_got, down_two, grad_attended, shared_other = lax.optimization_barrier(
            (grads_a, mid_got, down_two, grad_attended, shared_other)
        )
        mid_message = sum_second(mids, spot, mid_got)
        mid_two = second_quad(mid_message)
        down_sum, *messages = sum_deep([[down_local]], spot, [down_got], [down_two])
        down_answers = [deep_step(m, deep, k + 1) for k, m in enumerate(messages)]
    local_a = outer([inputs, tokens_other], [grads_a])
    if staged:
        message_a = sum_first([local_a], spot)
        got_a = first_quad(message_a)
        grad_attended, message_a, mid_message, *messages = lax.optimization_barrier(
            (grad_attended, message_a, mid_message, *messages)
        )
    grads_b, sums_b = attention_backward(
        item_lengths, random_blocks, triple, grad_attended, range(split, pair_count), position
    )
    if staged:
        grads_b, got_a, mid_two, *down_answers = lax.optimization_barrier(
            (grads_b, got_a, mid_two, *down_answers)
        )
    local_b = outer([inputs, tokens_other], [grads_b])
    small = small_sums(shared, shared_other, up_sum_own, up_sum_other, [sums_a, sums_b])
    if staged:
        message_b = sum_first([local_b], spot, small)
        got_b = first_quad(message_b)
        message_a = sum_second([local_a], spot, after(got_a, message_b))
        two_a = second_quad(message_a)
        mid_got, message_a = lax.optimization_barrier((mid_got, message_a))
        mid_sum, *messages = sum_deep([mids], spot, [mid_got], [mid_two])
        mid_answers = [deep_step(m, deep, k + 1) for k, m in enumerate(messages)]
        grads_a, grads_b, *messages = lax.optimization_barrier((grads_a, grads_b, *messages))

    other = swap(rows_product([grads_a, grads_b], full_qkv, whole, jnp.bfloat16))
    mine = rows_product([grads_a, grads_b], full_qkv, (0, half), jnp.float32)
    if staged:
        mine, other, got_b, two_a = lax.optimization_barrier((mine, other, got_b, two_a))
        message, small = sum_second([local_b], spot, got_b, small)
        two_b = second_quad(message)
        other, message = lax.optimization_barrier((other, message))
    input_grad = low(mine + other.astype(jnp.float32) + grad_res_one)
    if staged:
        (grad_down,) = sum_last(down_sum, down_answers, [up_width])
        input_grad, grad_down, two_b = lax.optimization_barrier((input_grad, grad_down, two_b))
        small, qkv_sum, *messages = sum_deep(
            [[local_a], [local_b]], spot, [got_a, got_b], [two_a, two_b], small
        )
        answers = [deep_step(m, deep, k + 1) for k, m in enumerate(messages)]
        grad_out, grad_up = sum_last(mid_sum, mid_answers, [head_width, up_width])
        grad_out, grad_up, *answers = lax.optimization_barrier((grad_out, grad_up, *answers))
        grad_qkv, small = sum_last(qkv_sum, answers, [3 * head_width], small)
    else:
        grad_down, grad_up, grad_out = (scattered(v) for v in (down_local, up_local, out_local))
        grad_qkv = scattered(jnp.concatenate([local_a, local_b], axis=1))
        small = lax.psum(small, every)
        part = small.shape[0] // 3
        small = jnp.concatenate([small[n * part : (n + 1) * part] for n in range(3)], axis=1)

    totals = small[:, :width]
    rest = small[:, width : width + head_width]
    grad_up_bias = rest[: up_width // head_width].reshape(up_width)
    grad_qv_bias = rest[up_width // head_width :]
    return (
        layer_out,
        input_grad,
        by_kind(grad_qkv, 3),
        grad_qv_bias,
        grad_out,
        totals[0],
        totals[1],
        totals[2],
        grad_up,
        grad_up_bias,
        grad_down,
        totals[3],
        totals[4],
        totals[5],
    )


def solution(mesh):
    devices = mesh.devices.reshape(-1, QUAD, mesh.shape["head"])
    fine = Mesh(devices, ("deep", "quad", "head"))
    rows = ("deep", "quad", "head")
    dp = ("deep", "quad")
    in_specs = (
        P(rows, None),
        P(dp, None, "head"),
        P(None, "head"),
        P(dp, "head"),
        P(),
        P(),
        P(),
        P(dp, "head"),
        P("head"),
        P(dp, "head"),
        P(),
        P(),
        P(),
        P(dp, None),
        P(dp, "head", None, None),
        P(rows, None),
    )
    out_specs = (
        P(rows, None),
        P(rows, None),
        P(dp, None, "head"),
        P(None, "head"),
        P(dp, "head"),
        P(),
        P(),
        P(),
        P(dp, "head"),
        P("head"),
        P(dp, "head"),
        P(),
        P(),
        P(),
    )
    return jax.shard_map(
        on_device, mesh=fine, in_specs=in_specs, out_specs=out_specs, check_vma=False
    )
```

```python
import functools

import jax
import jax.numpy as jnp
import numpy as np
from jax import lax
from jax.experimental import pallas as pl
from jax.experimental.pallas import tpu as pltpu
from jax.sharding import Mesh
from jax.sharding import PartitionSpec as P

BLK = 64


norm_eps = 1e-06
negative = -1e30


def norm_forward(values, gain, shift):
    centered = values - jnp.mean(values, axis=-1, keepdims=True)
    inverse = lax.rsqrt(jnp.mean(centered * centered, axis=-1, keepdims=True) + norm_eps)
    normed = centered * inverse
    return (normed * gain + shift, normed, inverse)


def dot_nt(a, b):
    return lax.dot_general(a, b, (((1,), (1,)), ((), ())), preferred_element_type=jnp.float32)


def dot_nn(a, b):
    return lax.dot_general(a, b, (((1,), (0,)), ((), ())), preferred_element_type=jnp.float32)


def dot_tn(a, b):
    return lax.dot_general(a, b, (((0,), (0,)), ((), ())), preferred_element_type=jnp.float32)


PAIR = 2 * BLK


def even_lanes(rows):
    return lax.broadcasted_iota(jnp.int32, (rows, PAIR), 1) < BLK


def stacked(values):
    zero = jnp.zeros_like(values)
    even = even_lanes(BLK)
    return jnp.concatenate([jnp.where(even, values, zero), jnp.where(even, zero, values)], axis=0)


def unstacked(values):
    return jnp.where(even_lanes(BLK), values[:BLK], values[BLK:])


class Layout:
    def __init__(self, len_ref, rb_ref, blocks, position):
        self.len_ref, self.rb_ref, self.blocks = len_ref, rb_ref, blocks
        self.half = blocks // 2
        self.rand = rb_ref.shape[-1]
        self.shift = position * self.half

    def moved(self, index):
        at = index + self.shift
        return jnp.where(at >= self.blocks, at - self.blocks, at)

    def spot(self, index):
        return pl.ds(pl.multiple_of(self.moved(index) * BLK, BLK), BLK)

    def part(self, index):
        return pl.ds(pl.multiple_of(self.moved(index) * BLK, BLK), self.half * BLK)

    def counts(self):
        self.count0 = lax.div(self.len_ref[0, 0], BLK)
        self.count1 = lax.div(self.len_ref[0, 1], BLK)
        self.second = jnp.where(self.count1 > 0, 1, 0)
        self.inner = self.blocks - 2 - 2 * self.second

    def locate(self, i):
        in0 = i < self.count0 - 2
        self.b = b = jnp.where(in0, i + 1, i + 2 + self.second)
        self.live = live = b < self.count0 + self.count1
        self.first = first = jnp.where(in0, 0, jnp.where(live, self.count0, b))
        items = jnp.where(in0, self.count0, jnp.where(live, self.count1, 1))
        rel = b - first
        last = items - 1
        zero, neg = jnp.float32(0.0), jnp.float32(negative)
        self.fixed = [
            first,
            first + last,
            jnp.where(live, b - 1, b),
            jnp.where(live, b + 1, b),
            b,
        ]
        self.low_bias = jnp.where(live & (rel == 1), neg, zero)
        self.high_bias = jnp.where(live & (rel + 1 == last), neg, zero)
        return self

    def ends(self, item):
        first = jnp.where(item == 0, 0, self.count0)
        count = jnp.where(item == 0, self.count0, self.count1)
        return first, first + count - 1, lax.div(count, self.half)

    def chosen(self, head):
        return [
            jnp.where(self.live, self.first + self.rb_ref[0, head, self.b, k], self.b)
            for k in range(self.rand)
        ]


def gathered(ref, layout, column, picked):
    even = even_lanes(BLK)

    def rows(index):
        return ref[layout.spot(index), column : column + PAIR]

    return jnp.concatenate(
        [rows(i) for i in layout.fixed]
        + [jnp.where(even, rows(i), rows(j)) for i, j in zip(*picked)],
        axis=0,
    )


ROWS = 32


def soft_rows(held):
    probs, inverse = [], []
    for row in range(0, held.shape[0], ROWS):
        scores = held[row : row + ROWS, :]
        expo = jnp.exp(scores - jnp.max(scores, axis=1, keepdims=True))
        inverse.append(1.0 / jnp.sum(expo, axis=1, keepdims=True))
        probs.append(expo.astype(jnp.bfloat16))
    return jnp.concatenate(probs, axis=0), jnp.concatenate(inverse, axis=0)


def attn_fwd_kernel(pairs, position, len_ref, rb_ref, tri_ref, out_ref, wide, *held):
    blocks = tri_ref.shape[0] // BLK
    scale = jnp.bfloat16(BLK**-0.5)
    layout = Layout(len_ref, rb_ref, blocks, position())
    layout.counts()

    def query_of(p, b):
        at = layout.spot(b)
        return stacked(tri_ref[at, p * 3 * PAIR : p * 3 * PAIR + PAIR]) * scale

    def put(p, b, mixed):
        at = layout.spot(b)
        out_ref[at, p * PAIR : (p + 1) * PAIR] = unstacked(mixed).astype(jnp.bfloat16)

    def sparse_scores(i, held):
        at = layout.locate(i)
        lane = lax.broadcasted_iota(jnp.int32, (1, PAIR), 1) < BLK
        bias_row = jnp.where(lane, at.low_bias, at.high_bias)
        for n, p in enumerate(pairs):
            picked = [at.chosen(2 * p), at.chosen(2 * p + 1)]
            keys = gathered(tri_ref, at, (3 * p + 1) * PAIR, picked)
            scores = dot_nt(query_of(p, at.b), keys)
            held[n][...] = jnp.concatenate(
                [scores[:, :PAIR], scores[:, PAIR : 2 * PAIR] + bias_row, scores[:, 2 * PAIR :]],
                axis=1,
            )

    def sparse_mix(i, held):
        at = layout.locate(i)
        for n, p in enumerate(pairs):
            picked = [at.chosen(2 * p), at.chosen(2 * p + 1)]
            probs, inverse = soft_rows(held[n])
            values = gathered(tri_ref, at, (3 * p + 2) * PAIR, picked)
            put(p, at.b, dot_nn(probs, values) * inverse)

    held_a, held_b = held[: len(pairs)], held[len(pairs) :]
    sparse_scores(0, held_a)

    def two(j, carry):
        sparse_scores(2 * j + 1, held_b)
        sparse_mix(2 * j, held_a)
        sparse_scores(jnp.minimum(2 * j + 2, layout.inner - 1), held_a)
        sparse_mix(2 * j + 1, held_b)
        return carry

    lax.fori_loop(0, lax.div(layout.inner, 2), two, 0)

    def dense(item, carry):
        first, last, chunks = layout.ends(item)
        queries = [
            jnp.concatenate([query_of(p, first), query_of(p, last)], axis=0) for p in pairs
        ]

        def dense_of(spans):
            for query, p in zip(queries, pairs):
                span = layout.half * BLK
                for c, at in enumerate(spans):
                    keys = tri_ref[at, (3 * p + 1) * PAIR : (3 * p + 2) * PAIR]
                    wide[:, c * span : (c + 1) * span] = dot_nt(query, keys)
                probs, inverse = soft_rows(wide.at[:, : len(spans) * span])
                mixed = sum(
                    dot_nn(
                        probs[:, c * span : (c + 1) * span],
                        tri_ref[at, (3 * p + 2) * PAIR : (3 * p + 3) * PAIR],
                    )
                    for c, at in enumerate(spans)
                ) * inverse
                put(p, first, mixed[:PAIR])
                put(p, last, mixed[PAIR:])

        @pl.when(chunks == 1)
        def short():
            dense_of([layout.part(first)])

        @pl.when(chunks == 2)
        def long():
            dense_of([layout.part(first), layout.part(first + layout.half)])

        return carry

    lax.fori_loop(0, 1 + layout.second, dense, 0)


def grad_rows(held_scores, held_grads, probs_ref, grads_ref):
    for row in range(0, held_scores.shape[0], ROWS):
        at = slice(row, row + ROWS)
        scores = held_scores[at, :]
        grad_probs = held_grads[at, :]
        expo = jnp.exp(scores - jnp.max(scores, axis=1, keepdims=True))
        probs = expo * (1.0 / jnp.sum(expo, axis=1, keepdims=True))
        delta = jnp.sum(probs * grad_probs, axis=1, keepdims=True)
        probs_ref[at, :] = probs.astype(jnp.bfloat16)
        grads_ref[at, :] = (probs * (grad_probs - delta)).astype(jnp.bfloat16)


def attn_bwd_kernel(
    pairs, position, len_ref, rb_ref, tri_ref, grad_ref, out_ref, sum_ref, *scratch
):
    blocks = tri_ref.shape[0] // BLK
    scale = jnp.bfloat16(BLK**-0.5)
    back = BLK**-0.5
    layout = Layout(len_ref, rb_ref, blocks, position())
    layout.counts()
    count = len(pairs)
    key_acc, value_acc = scratch[:count], scratch[count : 2 * count]
    held_a, held_b, done = (scratch[n * count : (n + 2) * count] for n in (2, 4, 6))
    wide = scratch[8 * count :]

    def clear(r, carry):
        at = pl.ds(pl.multiple_of(r * BLK, BLK), BLK)
        for acc in scratch[: 2 * count]:
            acc[at, :] = jnp.zeros((BLK, PAIR), jnp.float32)
        return carry

    lax.fori_loop(0, blocks, clear, 0)

    def query_of(p, b):
        at = layout.spot(b)
        return stacked(tri_ref[at, p * 3 * PAIR : p * 3 * PAIR + PAIR]) * scale

    def grad_of(p, b):
        at = layout.spot(b)
        return stacked(grad_ref[at, p * PAIR : (p + 1) * PAIR])

    def put(i, b, grad_query):
        out_ref[layout.spot(b), i * 3 * PAIR : i * 3 * PAIR + PAIR] = unstacked(
            grad_query * back
        ).astype(jnp.bfloat16)

    def sparse_scores(n, held):
        at = layout.locate(n)
        lane = lax.broadcasted_iota(jnp.int32, (1, PAIR), 1) < BLK
        bias_row = jnp.where(lane, at.low_bias, at.high_bias)
        for i, p in enumerate(pairs):
            picked = [at.chosen(2 * p), at.chosen(2 * p + 1)]
            keys = gathered(tri_ref, at, (3 * p + 1) * PAIR, picked)
            values = gathered(tri_ref, at, (3 * p + 2) * PAIR, picked)
            scores = dot_nt(query_of(p, at.b), keys)
            held[2 * i][...] = jnp.concatenate(
                [scores[:, :PAIR], scores[:, PAIR : 2 * PAIR] + bias_row, scores[:, 2 * PAIR :]],
                axis=1,
            )
            held[2 * i + 1][...] = dot_nt(grad_of(p, at.b), values)

    def sparse_grads(n, held):
        at = layout.locate(n)
        even = even_lanes(BLK)
        for i, p in enumerate(pairs):
            grad_rows(held[2 * i], held[2 * i + 1], done[2 * i], done[2 * i + 1])
            picked = [at.chosen(2 * p), at.chosen(2 * p + 1)]
            spots = [at.spot(index) for index in at.fixed]
            spots += [(at.spot(one), at.spot(two)) for one, two in zip(*picked)]
            keys = gathered(tri_ref, at, (3 * p + 1) * PAIR, picked)
            put(i, at.b, dot_nn(done[2 * i + 1][...], keys))
            for acc, update in (
                (key_acc[i], dot_tn(done[2 * i + 1][...], query_of(p, at.b))),
                (value_acc[i], dot_tn(done[2 * i][...], grad_of(p, at.b))),
            ):
                for j, spot in enumerate(spots):
                    piece = update[j * BLK : (j + 1) * BLK]
                    if j < len(at.fixed):
                        acc[spot, :] += piece
                    else:
                        zero = jnp.zeros_like(piece)
                        acc[spot[0], :] += jnp.where(even, piece, zero)
                        acc[spot[1], :] += jnp.where(even, zero, piece)

    sparse_scores(0, held_a)

    def two(j, carry):
        sparse_scores(2 * j + 1, held_b)
        sparse_grads(2 * j, held_a)
        sparse_scores(jnp.minimum(2 * j + 2, layout.inner - 1), held_a)
        sparse_grads(2 * j + 1, held_b)
        return carry

    lax.fori_loop(0, lax.div(layout.inner, 2), two, 0)

    wide_scores, wide_grads, wide_probs, wide_out = wide

    def dense(item, carry):
        first, last, chunks = layout.ends(item)

        def dense_of(spans):
            span = layout.half * BLK
            cover = len(spans) * span
            def end(n, carry):
                b = jnp.where(n == 0, first, last)
                for i, p in enumerate(pairs):
                    query, grad = query_of(p, b), grad_of(p, b)
                    for c, at in enumerate(spans):
                        cut = slice(c * span, (c + 1) * span)
                        keys = tri_ref[at, (3 * p + 1) * PAIR : (3 * p + 2) * PAIR]
                        values = tri_ref[at, (3 * p + 2) * PAIR : (3 * p + 3) * PAIR]
                        wide_scores[:, cut] = dot_nt(query, keys)
                        wide_grads[:, cut] = dot_nt(grad, values)
                    grad_rows(*(ref.at[:, :cover] for ref in wide))
                    total = jnp.zeros((PAIR, PAIR), jnp.float32)
                    for c, at in enumerate(spans):
                        cut = slice(c * span, (c + 1) * span)
                        keys = tri_ref[at, (3 * p + 1) * PAIR : (3 * p + 2) * PAIR]
                        total += dot_nn(wide_out[:, cut], keys)
                        key_acc[i][at, :] += dot_tn(wide_out[:, cut], query)
                        value_acc[i][at, :] += dot_tn(wide_probs[:, cut], grad)
                    put(i, b, total)
                return carry

            lax.fori_loop(0, 2, end, 0)

        @pl.when(chunks == 1)
        def short():
            dense_of([layout.part(first)])

        @pl.when(chunks == 2)
        def long():
            dense_of([layout.part(first), layout.part(first + layout.half)])

        return carry

    lax.fori_loop(0, 1 + layout.second, dense, 0)

    sum_ref[...] = jnp.zeros_like(sum_ref)

    def finish(r, carry):
        at = pl.ds(pl.multiple_of(r * BLK, BLK), BLK)
        new = []
        for i in range(count):
            column = i * 3 * PAIR
            query_sum, value_sum = carry[i]
            out_ref[at, column + PAIR : column + 2 * PAIR] = key_acc[i][at, :].astype(jnp.bfloat16)
            value = value_acc[i][at, :].astype(jnp.bfloat16)
            out_ref[at, column + 2 * PAIR : column + 3 * PAIR] = value
            query = out_ref[at, column : column + PAIR].astype(jnp.float32)
            new.append(
                tuple(
                    total + jnp.sum(part.reshape(-1, 8, PAIR), axis=0)
                    for total, part in (
                        (query_sum, query),
                        (value_sum, value.astype(jnp.float32)),
                    )
                )
            )
        return tuple(new)

    zero = jnp.zeros((8, PAIR), jnp.float32)
    sums = lax.fori_loop(0, blocks, finish, tuple((zero, zero) for _ in pairs))
    for i, totals in enumerate(sums):
        for kind, total in enumerate(totals):
            sum_ref[kind : kind + 1, i * PAIR : (i + 1) * PAIR] = jnp.sum(
                total, axis=0, keepdims=True
            )


vmem = pl.BlockSpec(memory_space=pltpu.VMEM)
smem = pl.BlockSpec(memory_space=pltpu.SMEM)
def attention_forward(lengths, randoms, triple, position):
    pairs = randoms.shape[1] // 2
    rows = triple.shape[0]
    area = rows * rows // 3 * 2 * pairs
    return pl.pallas_call(
        functools.partial(attn_fwd_kernel, range(pairs), position),
        out_shape=jax.ShapeDtypeStruct((rows, pairs * PAIR), jnp.bfloat16),
        in_specs=[smem, smem, vmem],
        out_specs=vmem,
        name="attend_forward",
        scratch_shapes=[pltpu.VMEM((2 * PAIR, rows), jnp.float32)]
        + [pltpu.VMEM((PAIR, 8 * BLK), jnp.float32)] * (2 * pairs),
        cost_estimate=pl.CostEstimate(
            flops=16 * area * PAIR, transcendentals=area, bytes_accessed=rows * pairs * PAIR * 8
        ),
        compiler_params=pltpu.CompilerParams(vmem_limit_bytes=8 << 20),
    )(lengths, randoms, triple)


def attention_backward(lengths, randoms, triple, grad, pairs, position):
    rows = triple.shape[0]
    count = len(pairs)
    area = rows * rows // 3 * 2 * count
    return pl.pallas_call(
        functools.partial(attn_bwd_kernel, pairs, position),
        out_shape=(
            jax.ShapeDtypeStruct((rows, count * 3 * PAIR), jnp.bfloat16),
            jax.ShapeDtypeStruct((8, count * PAIR), jnp.float32),
        ),
        in_specs=[smem, smem, vmem, vmem],
        out_specs=(vmem, vmem),
        name="attend_backward",
        scratch_shapes=[pltpu.VMEM((rows, PAIR), jnp.float32)] * (2 * count)
        + [pltpu.VMEM((PAIR, 8 * BLK), jnp.float32)] * (4 * count)
        + [pltpu.VMEM((PAIR, 8 * BLK), jnp.bfloat16)] * (2 * count)
        + [pltpu.VMEM((PAIR, rows), kind) for kind in (jnp.float32,) * 2 + (jnp.bfloat16,) * 2],
        cost_estimate=pl.CostEstimate(
            flops=40 * area * PAIR, transcendentals=area, bytes_accessed=rows * count * PAIR * 20
        ),
        compiler_params=pltpu.CompilerParams(vmem_limit_bytes=20 << 20),
    )(lengths, randoms, triple, grad)


TILE = 256
EPS = 1e-06


def tile_at(n):
    return pl.ds(pl.multiple_of(n * TILE, TILE), TILE)


def up_kernel(rows_ref, weight_ref, bias_ref, active_ref, slope_ref, held_a, held_b):
    tiles = weight_ref.shape[1] // TILE
    root = (2.0 / np.pi) ** 0.5
    cube = 0.044715 * root

    def product(n, held):
        held[...] = dot_nn(rows_ref[...], weight_ref[:, tile_at(n)])

    def gelu(n, held):
        bias = bias_ref[:, tile_at(n)]
        for row in range(0, held.shape[0], ROWS):
            at = slice(row, row + ROWS)
            upper = (held[at, :] + bias).astype(jnp.bfloat16).astype(jnp.float32)
            square = upper * upper
            half = 0.5 + 0.5 * jnp.tanh(upper * (square * cube + root))
            active = upper * half
            active_ref[at, tile_at(n)] = active.astype(jnp.bfloat16)
            bend = (1.0 - half) * (square * (6.0 * cube) + 2.0 * root)
            slope_ref[at, tile_at(n)] = (half + active * bend).astype(jnp.bfloat16)

    product(0, held_a)

    def two(j, carry):
        product(2 * j + 1, held_b)
        gelu(2 * j, held_a)
        product(jnp.minimum(2 * j + 2, tiles - 1), held_a)
        gelu(2 * j + 1, held_b)
        return carry

    lax.fori_loop(0, tiles // 2, two, 0)


def up_gelu(rows, weight, bias):
    count, width = rows.shape[0], weight.shape[1]
    shape = jax.ShapeDtypeStruct((count, width), jnp.bfloat16)
    return pl.pallas_call(
        up_kernel,
        out_shape=(shape, shape),
        in_specs=[vmem] * 3,
        out_specs=(vmem, vmem),
        name="up_gelu",
        scratch_shapes=[pltpu.VMEM((count, TILE), jnp.float32)] * 2,
        cost_estimate=pl.CostEstimate(
            flops=2 * count * width * rows.shape[1],
            transcendentals=count * width,
            bytes_accessed=2 * (rows.size + weight.size + 2 * count * width),
        ),
        compiler_params=pltpu.CompilerParams(vmem_limit_bytes=12 << 20),
    )(rows, weight, bias.reshape(1, -1))


def back_kernel(grad_ref, weight_ref, slope_ref, out_ref, sum_ref):
    def step(n, carry):
        grad_active = dot_nn(grad_ref[...], weight_ref[:, tile_at(n)])
        total = jnp.zeros((8, TILE), jnp.float32)
        for row in range(0, grad_active.shape[0], ROWS):
            at = slice(row, row + ROWS)
            grad = grad_active[at] * slope_ref[at, tile_at(n)].astype(jnp.float32)
            grad = grad.astype(jnp.bfloat16)
            out_ref[at, tile_at(n)] = grad
            total += jnp.sum(grad.astype(jnp.float32).reshape(-1, 8, TILE), axis=0)
        sum_ref[:, tile_at(n)] = total
        return carry

    lax.fori_loop(0, weight_ref.shape[1] // TILE, step, 0)


def back_slope(grad, weight, slope):
    count, width = slope.shape
    return pl.pallas_call(
        back_kernel,
        out_shape=(
            jax.ShapeDtypeStruct((count, width), jnp.bfloat16),
            jax.ShapeDtypeStruct((8, width), jnp.float32),
        ),
        in_specs=[vmem] * 3,
        out_specs=(vmem, vmem),
        name="back_slope",
        cost_estimate=pl.CostEstimate(
            flops=2 * count * width * grad.shape[1],
            transcendentals=0,
            bytes_accessed=2 * (grad.size + weight.size + 2 * count * width),
        ),
        compiler_params=pltpu.CompilerParams(vmem_limit_bytes=12 << 20),
    )(grad, weight, slope)


def outer_kernel(count, *refs):
    lefts, rights, out_ref = refs[:count], refs[count:-1], refs[-1]
    if len(rights) < count:
        rows = lefts[0].shape[0]
        rights = [rights[0].at[n * rows : (n + 1) * rows] for n in range(count)]

    def step(at):
        total = sum(dot_tn(a[...], b[:, at]) for a, b in zip(lefts, rights))
        out_ref[:, at] = total.astype(jnp.bfloat16)

    width = out_ref.shape[1]
    if width % TILE:
        step(slice(0, width))
    else:

        def body(n, carry):
            step(tile_at(n))
            return carry

        lax.fori_loop(0, width // TILE, body, 0)


def outer(lefts, rights):
    shape = (lefts[0].shape[1], rights[0].shape[1])
    inner = sum(a.shape[0] for a in lefts)
    return pl.pallas_call(
        functools.partial(outer_kernel, len(lefts)),
        out_shape=jax.ShapeDtypeStruct(shape, jnp.bfloat16),
        in_specs=[vmem] * (len(lefts) + len(rights)),
        out_specs=vmem,
        name="outer",
        cost_estimate=pl.CostEstimate(
            flops=2 * inner * shape[0] * shape[1],
            transcendentals=0,
            bytes_accessed=2 * inner * sum(shape),
        ),
        compiler_params=pltpu.CompilerParams(vmem_limit_bytes=12 << 20),
    )(*lefts, *rights)


def project_kernel(own_ref, other_ref, weight_ref, out_ref):
    rows = own_ref.shape[0]
    for n, ref in enumerate((own_ref, other_ref)):
        product = dot_nn(ref[...], weight_ref[...])
        out_ref[n * rows : (n + 1) * rows, :] = product.astype(jnp.bfloat16)


def project_both(own, other, weight):
    return pl.pallas_call(
        project_kernel,
        out_shape=jax.ShapeDtypeStruct((2 * own.shape[0], weight.shape[1]), jnp.bfloat16),
        in_specs=[vmem] * 3,
        out_specs=vmem,
        name="project_both",
        compiler_params=pltpu.CompilerParams(vmem_limit_bytes=12 << 20),
    )(own, other, weight)


GROUP = 16
SPLIT = 4


def groups_at(r):
    return [
        (r * SPLIT + n, pl.ds(pl.multiple_of((r * SPLIT + n) * GROUP, GROUP), GROUP))
        for n in range(SPLIT)
    ]


def row_mean(values):
    return jnp.sum(values, axis=1, keepdims=True) * (1.0 / values.shape[1])


def folded(values):
    return jnp.sum(values.reshape(-1, 8, values.shape[1]), axis=0)


def norm_two_kernel(position, len_ref, down_ref, other_ref, resid_ref, cot_ref, vec_ref, out_ref, grad_ref, low_ref, sum_ref):
    count, width = down_ref.shape
    live_rows = len_ref[0, 0] + len_ref[0, 1] - position() * count
    bias, gain, shift = (vec_ref[n : n + 1, :] for n in range(3))

    def group(r, at, sums):
        row = r * GROUP + lax.broadcasted_iota(jnp.int32, (GROUP, 1), 0)
        live = jnp.where(row < live_rows, 1.0, 0.0)
        values = down_ref[at, :] + other_ref[at, :].astype(jnp.float32) + bias + resid_ref[at, :]
        centered = values - row_mean(values)
        inverse = lax.rsqrt(row_mean(centered * centered) + EPS)
        normed = centered * inverse
        out_ref[at, :] = ((normed * gain + shift) * live).astype(jnp.bfloat16)
        cot = cot_ref[at, :].astype(jnp.float32) * live
        scaled = cot * gain
        grad = inverse * (scaled - row_mean(scaled) - normed * row_mean(scaled * normed))
        grad_ref[at, :] = grad
        low_ref[at, :] = grad.astype(jnp.bfloat16)
        return tuple(s + folded(v) for s, v in zip(sums, (grad, cot * normed, cot)))

    def step(r, sums):
        for n, at in groups_at(r):
            sums = group(n, at, sums)
        return sums

    zero = jnp.zeros((8, width), jnp.float32)
    sums = lax.fori_loop(0, count // (GROUP * SPLIT), step, (zero,) * 3)
    for n, total in enumerate(sums):
        sum_ref[n : n + 1, :] = jnp.sum(total, axis=0, keepdims=True)
    sum_ref[3:8, :] = jnp.zeros((5, width), jnp.float32)


def norm_two(lengths, down, other, resid, cot, bias, gain, shift, position):
    shape = down.shape
    row = jax.ShapeDtypeStruct((8, shape[1]), jnp.float32)
    return pl.pallas_call(
        functools.partial(norm_two_kernel, position),
        out_shape=(
            jax.ShapeDtypeStruct(shape, jnp.bfloat16),
            jax.ShapeDtypeStruct(shape, jnp.float32),
            jax.ShapeDtypeStruct(shape, jnp.bfloat16),
            row,
        ),
        in_specs=[smem] + [vmem] * 5,
        out_specs=(vmem,) * 4,
        name="norm_two",
        cost_estimate=pl.CostEstimate(
            flops=40 * down.size, transcendentals=0, bytes_accessed=20 * down.size
        ),
        compiler_params=pltpu.CompilerParams(vmem_limit_bytes=12 << 20),
    )(lengths, down, other, resid, cot, jnp.stack([bias, gain, shift]))


def norm_one_kernel(own_ref, other_ref, grad_ref, normed_ref, inverse_ref, gain_ref, out_ref, low_ref, sum_ref):
    count, width = own_ref.shape
    gain = gain_ref[...]

    def group(r, at, sums):
        grad = own_ref[at, :] + other_ref[at, :].astype(jnp.float32) + grad_ref[at, :]
        normed = normed_ref[at, :]
        scaled = grad * gain
        result = inverse_ref[at, :] * (
            scaled - row_mean(scaled) - normed * row_mean(scaled * normed)
        )
        out_ref[at, :] = result
        low_ref[at, :] = result.astype(jnp.bfloat16)
        return tuple(s + folded(v) for s, v in zip(sums, (result, grad * normed, grad)))

    def step(r, sums):
        for n, at in groups_at(r):
            sums = group(n, at, sums)
        return sums

    zero = jnp.zeros((8, width), jnp.float32)
    sums = lax.fori_loop(0, count // (GROUP * SPLIT), step, (zero,) * 3)
    for n, total in enumerate(sums):
        sum_ref[n : n + 1, :] = jnp.sum(total, axis=0, keepdims=True)
    sum_ref[3:8, :] = jnp.zeros((5, width), jnp.float32)


def norm_one_back(own, other, grad, normed, inverse, gain):
    shape = own.shape
    return pl.pallas_call(
        norm_one_kernel,
        out_shape=(
            jax.ShapeDtypeStruct(shape, jnp.float32),
            jax.ShapeDtypeStruct(shape, jnp.bfloat16),
            jax.ShapeDtypeStruct((8, shape[1]), jnp.float32),
        ),
        in_specs=[vmem] * 6,
        out_specs=(vmem,) * 3,
        name="norm_one_back",
        cost_estimate=pl.CostEstimate(
            flops=20 * own.size, transcendentals=0, bytes_accessed=20 * own.size
        ),
        compiler_params=pltpu.CompilerParams(vmem_limit_bytes=12 << 20),
    )(own, other, grad, normed, inverse, gain.reshape(1, -1))


def pack_rows(ref, at, small):
    rows = small.shape[0]
    high = small.astype(jnp.bfloat16)
    ref[at : at + rows, :] = high
    ref[at + rows : at + 2 * rows, :] = (small - high.astype(jnp.float32)).astype(jnp.bfloat16)


def unpack_rows(ref, at, rows):
    high = ref[at : at + rows, :].astype(jnp.float32)
    return high + ref[at + rows : at + 2 * rows, :].astype(jnp.float32)


def slab_at(at_ref, place, z, rows):
    return pl.ds(pl.multiple_of((z * QUAD + at_ref[place]) * rows, rows), rows)


def columns_of(totals):
    cuts, low = [], 0
    for total in totals:
        cuts.append(slice(low, low + total.shape[1]))
        low += total.shape[1]
    return cuts


def sum_first_kernel(count, deep, apart, at_ref, *refs):
    totals, rest = refs[:count], refs[count:]
    rows = totals[0].shape[0] // (deep * QUAD)
    halves = [(1, 0), (3, deep * rows)]
    if apart:
        halves = [(1, 0), (3, 0)]
    for part, (place, low) in enumerate(halves):
        out_ref = rest[part - 2] if apart else rest[-1]
        for z in range(deep):
            row = low + z * rows
            for total, cut in zip(totals, columns_of(totals)):
                out_ref[row : row + rows, cut] = total[slab_at(at_ref, place, z, rows), :]
    if len(rest) > 1 and not apart:
        pack_rows(rest[-1], 2 * deep * rows, rest[0][...])


def sum_second_kernel(count, deep, at_ref, *refs):
    totals, got_ref = refs[:count], refs[count]
    rows = totals[0].shape[0] // (deep * QUAD)
    if len(refs) > count + 2:
        small_ref, out_ref, new_ref = refs[count + 1 :]
        small = small_ref[...] + unpack_rows(got_ref, 2 * deep * rows, small_ref.shape[0])
        new_ref[...] = small
        pack_rows(out_ref, deep * rows, small)
    else:
        out_ref = refs[-1]
    for z in range(deep):
        for total, cut in zip(totals, columns_of(totals)):
            far = total[slab_at(at_ref, 2, z, rows), :].astype(jnp.float32)
            row = z * rows + (deep * rows if got_ref.shape[0] >= 2 * deep * rows else 0)
            far = far + got_ref[row : row + rows, cut].astype(jnp.float32)
            out_ref[z * rows : (z + 1) * rows, cut] = far.astype(jnp.bfloat16)


def sum_deep_kernel(groups, deep, small_rows, at_ref, *refs):
    count = sum(groups)
    totals, refs = refs[:count], refs[count:]
    gots, twos, refs = refs[: len(groups)], refs[len(groups) : 2 * len(groups)], refs[2 * len(groups) :]
    rows = totals[0].shape[0] // (deep * QUAD)
    small = None
    if small_rows:
        small_ref, new_ref, refs = refs[0], refs[1], refs[2:]
        small = small_ref[...] + unpack_rows(twos[-1], deep * rows, small_rows)
        part = new_ref.shape[0]
        cuts = [small[n * part : (n + 1) * part] for n in range(small_rows // part)]
        small = jnp.concatenate(cuts, axis=1)
        new_ref[...] = small
    out_cuts = columns_of(totals)
    for k in range(deep):
        z = at_ref[QUAD] ^ k
        near = pl.ds(pl.multiple_of(z * rows, rows), rows)
        n = 0
        for group, got_ref, two_ref in zip(groups, gots, twos):
            members = totals[n : n + group]
            for total, cut, out_cut in zip(members, columns_of(members), out_cuts[n : n + group]):
                value = (
                    total[slab_at(at_ref, 0, z, rows), :].astype(jnp.float32)
                    + got_ref[near, cut].astype(jnp.float32)
                    + two_ref[near, cut].astype(jnp.float32)
                )
                refs[k][:rows, out_cut] = value.astype(refs[k].dtype)
            n += group
        if k and small is not None:
            pack_rows(refs[k], rows, small)


def sum_last_kernel(count, small_rows, *refs):
    own_ref, answers = refs[0], refs[1 : 1 + count]
    rows = own_ref.shape[0]
    own = own_ref[...]
    for answer in answers:
        own = own + answer[:rows, :].astype(jnp.float32)
    outs = refs[1 + count :]
    if small_rows:
        small_ref, new_ref, outs = outs[0], outs[-1], outs[1:-1]
        small = small_ref[...]
        for answer in answers:
            small = small + unpack_rows(answer, rows, small_rows)
        new_ref[...] = small
    if len(outs[0].shape) == 3:
        kinds = outs[0].shape[0]
        for n in range(own.shape[1] // PAIR):
            pair, kind = n // kinds, n % kinds
            cut = slice(pair * PAIR, (pair + 1) * PAIR)
            outs[0][kind, :, cut] = own[:, n * PAIR : (n + 1) * PAIR]
        return
    for out_ref, cut in zip(outs, columns_of(outs)):
        out_ref[...] = own[:, cut]


def vmem_call(kernel, outs, operands, name, scalars=1, limit=12):
    outs = [jax.ShapeDtypeStruct(shape, dtype) for shape, dtype in outs]
    return pl.pallas_call(
        kernel,
        out_shape=outs,
        in_specs=[smem] * scalars + [vmem] * (len(operands) - scalars),
        out_specs=[vmem] * len(outs),
        name=name,
        compiler_params=pltpu.CompilerParams(vmem_limit_bytes=limit << 20),
    )(*operands)


def sum_first_apart(total, spot):
    shape = (total.shape[0] // QUAD, total.shape[1])
    kernel = functools.partial(sum_first_kernel, 1, spot.deep, True)
    return vmem_call(kernel, [(shape, jnp.bfloat16)] * 2, [spot.at, total], "sum_first")


def sum_first(totals, spot, small=None):
    span = totals[0].shape[0] // QUAD
    extra = 0 if small is None else 2 * small.shape[0]
    shape = (2 * span + extra, sum(t.shape[1] for t in totals))
    operands = [spot.at, *totals] + ([] if small is None else [small])
    kernel = functools.partial(sum_first_kernel, len(totals), spot.deep, False)
    return vmem_call(kernel, [(shape, jnp.bfloat16)], operands, "sum_first")[0]


def sum_second(totals, spot, got, small=None):
    span = totals[0].shape[0] // QUAD
    kernel = functools.partial(sum_second_kernel, len(totals), spot.deep)
    operands = [spot.at, *totals, got]
    if small is None:
        outs = [((span, got.shape[1]), jnp.bfloat16)]
        return vmem_call(kernel, outs, operands, "sum_second")[0]
    outs = [((span + 2 * small.shape[0], got.shape[1]), jnp.bfloat16), (small.shape, jnp.float32)]
    return vmem_call(kernel, outs, operands + [small], "sum_second")


def sum_deep(groups, spot, gots, twos, small=None):
    totals = [total for group in groups for total in group]
    rows = totals[0].shape[0] // (QUAD * spot.deep)
    columns = sum(t.shape[1] for t in totals)
    small_rows = 0 if small is None else small.shape[0]
    kernel = functools.partial(
        sum_deep_kernel, [len(group) for group in groups], spot.deep, small_rows
    )
    operands = [spot.at, *totals, *gots, *twos] + ([] if small is None else [small])
    outs, extra = [], 0
    if small is not None:
        part = small_rows // 3
        outs, extra = [((part, columns), jnp.float32)], 2 * part
    outs += [((rows, columns), jnp.float32)]
    outs += [((rows + extra, columns), jnp.bfloat16)] * (spot.deep - 1)
    return vmem_call(kernel, outs, operands, "sum_deep")


def sum_last(own, answers, widths, small=None):
    kernel = functools.partial(
        sum_last_kernel, len(answers), 0 if small is None else small.shape[0]
    )
    operands = [own, *answers] + ([] if small is None else [small])
    outs = [((own.shape[0], w), jnp.float32) for w in widths]
    if small is not None:
        outs = [((3, own.shape[0], widths[0] // 3), jnp.float32)]
    outs += [] if small is None else [(small.shape, jnp.float32)]
    return vmem_call(kernel, outs, operands, "sum_last", scalars=0)


def small_kernel(own_ref, swapped_ref, up_one_ref, up_two_ref, *refs):
    out_ref = refs[-1]
    columns = out_ref.shape[1]
    both = own_ref[...] + swapped_ref[...]
    rows = [both[0:3], both[8:11]]
    row = 0
    for low in range(0, both.shape[1], columns):
        for part in rows:
            out_ref[row : row + 3, :] = part[:, low : low + columns]
            row += 3
    up = jnp.sum(up_one_ref[...] + up_two_ref[...], axis=0, keepdims=True)
    for low in range(0, up.shape[1], columns):
        out_ref[row : row + 1, :] = up[:, low : low + columns]
        row += 1
    low = 0
    for ref in refs[:-1]:
        out_ref[row : row + 2, low : low + ref.shape[1]] = ref[0:2, :]
        low += ref.shape[1]


def small_sums(own, swapped, up_one, up_two, sums):
    columns = sum(s.shape[1] for s in sums)
    rows = 6 * own.shape[1] // columns + up_one.shape[1] // columns + 2
    return vmem_call(
        small_kernel,
        [((rows, columns), jnp.float32)],
        [own, swapped, up_one, up_two, *sums],
        "small_sums",
        scalars=0,
    )[0]


def rows_kernel(window, cuts, *refs):
    lefts, weight_ref, out_ref = refs[:-2], refs[-2], refs[-1]
    rows = slice(*window)

    def step(n, carry):
        total = sum(
            dot_nt(left[rows, :], weight_ref[tile_at(n), cut]) for left, cut in zip(lefts, cuts)
        )
        out_ref[:, tile_at(n)] = total.astype(out_ref.dtype)
        return carry

    lax.fori_loop(0, out_ref.shape[1] // TILE, step, 0)


def rows_product(lefts, weight, window, dtype):
    shape = (window[1] - window[0], weight.shape[0])
    return pl.pallas_call(
        functools.partial(rows_kernel, window, columns_of(lefts)),
        out_shape=jax.ShapeDtypeStruct(shape, dtype),
        in_specs=[vmem] * (len(lefts) + 1),
        out_specs=vmem,
        name="rows_product",
        cost_estimate=pl.CostEstimate(
            flops=2 * shape[0] * weight.size,
            transcendentals=0,
            bytes_accessed=2 * (shape[0] * sum(weight.shape) + weight.size),
        ),
        compiler_params=pltpu.CompilerParams(vmem_limit_bytes=12 << 20),
    )(*lefts, weight)


def triple_kernel(own_ref, other_ref, weight_ref, bias_ref, out_ref):
    rows = own_ref.shape[0]
    span = 3 * PAIR

    def step(n, carry):
        at = pl.ds(pl.multiple_of(n * span, span), span)
        for k, ref in enumerate((own_ref, other_ref)):
            product = dot_nn(ref[...], weight_ref[:, at]) + bias_ref[:, at]
            out_ref[k * rows : (k + 1) * rows, at] = product.astype(jnp.bfloat16)
        return carry

    lax.fori_loop(0, out_ref.shape[1] // span, step, 0)


def triple_of(own, other, weight, bias):
    shape = (2 * own.shape[0], weight.shape[1])
    return pl.pallas_call(
        triple_kernel,
        out_shape=jax.ShapeDtypeStruct(shape, jnp.bfloat16),
        in_specs=[vmem] * 4,
        out_specs=vmem,
        name="triple",
        cost_estimate=pl.CostEstimate(
            flops=2 * shape[0] * weight.size,
            transcendentals=0,
            bytes_accessed=2 * (shape[0] * sum(weight.shape) + weight.size),
        ),
        compiler_params=pltpu.CompilerParams(vmem_limit_bytes=12 << 20),
    )(own, other, weight, bias.reshape(1, -1))


QUAD = 4


def group_permute(value, deep, target):
    pairs = []
    for z in range(deep):
        for q in range(QUAD):
            for h in range(2):
                to_z, to_q = target(z, q, h)
                pairs.append(((z * QUAD + q) * 2 + h, (to_z * QUAD + to_q) * 2 + h))
    return lax.ppermute(value, ("deep", "quad", "head"), pairs)


def deep_step(value, deep, bit):
    return group_permute(value, deep, lambda z, q, h: (z ^ bit, q))


def quad_step(value, deep, second):
    return group_permute(value, deep, lambda z, q, h: (z, q ^ ((2 >> h) if second else (1 << h))))


def swap(value):
    return lax.ppermute(value, "head", [(0, 1), (1, 0)])


def after(value, *others):
    return lax.optimization_barrier((value,) + others)[0]


class Spot:
    def __init__(self):
        self.z, self.q, self.h = (lax.axis_index(a) for a in ("deep", "quad", "head"))
        self.deep = lax.axis_size("deep")
        one, two = 1 << self.h, 2 >> self.h
        self.places = [self.q, self.q ^ one, self.q ^ two, self.q ^ 3]
        self.at = jnp.stack(self.places + [self.z]).astype(jnp.int32)


def deep_pieces(value, spot):
    return [deep_step(value, spot.deep, k) for k in range(1, spot.deep)]


def place_kernel(deep, windows, kinds, at_ref, *refs):
    pieces, outs = refs[:QUAD], refs[QUAD:]
    rows = pieces[0].shape[1] // kinds
    for k in range(deep):
        for j, piece in enumerate(pieces):
            row = pl.multiple_of(((at_ref[QUAD] ^ k) * QUAD + at_ref[j]) * rows, rows)
            at = pl.ds(row, rows)
            if kinds > 1:
                for n in range(kinds * piece.shape[2] // PAIR):
                    pair, kind = n // kinds, n % kinds
                    outs[0][at, n * PAIR : (n + 1) * PAIR] = piece[
                        k, kind * rows : (kind + 1) * rows, pair * PAIR : (pair + 1) * PAIR
                    ]
                continue
            for out, (low, high) in zip(outs, windows):
                out[at, :] = piece[k, :, low:high]


def place(spot, pieces, widths, kinds=1):
    windows, low = [], 0
    for width in widths:
        windows.append((low, low + width))
        low += width
    deep, rows = pieces[0].shape[0], pieces[0].shape[1] // kinds
    outs = [((deep * QUAD * rows, width), pieces[0].dtype) for width in widths]
    kernel = functools.partial(place_kernel, deep, windows, kinds)
    return vmem_call(kernel, outs, [spot.at, *pieces], "place_pieces", limit=8)


def low(value):
    return value.astype(jnp.bfloat16)


def by_pair(value):
    lead, kinds, columns = value.shape[:-2], value.shape[-2], value.shape[-1]
    split = value.reshape(lead + (kinds, columns // PAIR, PAIR))
    return jnp.swapaxes(split, -3, -2).reshape(lead + (kinds * columns,))


def by_kind(value, kinds):
    lead, columns = value.shape[:-1], value.shape[-1]
    split = value.reshape(lead + (columns // (kinds * PAIR), kinds, PAIR))
    return jnp.swapaxes(split, -3, -2).reshape(lead + (kinds, columns // kinds))


def on_device(
    inputs,
    qkv_weight,
    qv_bias,
    out_weight,
    out_bias,
    first_gain,
    first_shift,
    up_weight,
    up_bias,
    down_weight,
    down_bias,
    second_gain,
    second_shift,
    item_lengths,
    random_blocks,
    out_grad,
):
    half, width = inputs.shape
    spot = Spot()
    deep = spot.deep
    shard = qkv_weight.shape[0]
    head_width = qkv_weight.shape[2]
    up_width = up_weight.shape[1]
    pair_count = head_width // PAIR

    def position():
        return lax.axis_index("head")

    staged = deep == 4 and shard % 16 == 0
    every = ("deep", "quad")

    def gathered_whole(block):
        return lax.all_gather(block, every, axis=0, tiled=True)

    def scattered(total):
        return lax.psum_scatter(total, every, scatter_dimension=0, tiled=True).astype(jnp.float32)

    def first_quad(block):
        return quad_step(block, deep, False)

    def second_quad(block):
        return quad_step(block, deep, True)

    tokens_other = swap(inputs)
    mid = jnp.concatenate([out_weight, up_weight], axis=1)
    if staged:
        qkv_block = jnp.swapaxes(qkv_weight, 0, 1).reshape(3 * shard, head_width)
        qkv_pieces = deep_pieces(qkv_block, spot)
        mid_pieces = deep_pieces(after(mid, *qkv_pieces), spot)
        qkv_deep = jnp.stack([qkv_block] + qkv_pieces)
        qkv_other, qkv_far = first_quad(qkv_deep), second_quad(qkv_deep)
        qkv_other, qkv_far, *mid_pieces = lax.optimization_barrier(
            (qkv_other, qkv_far, *mid_pieces)
        )
        qkv_across = second_quad(qkv_other)
        (full_qkv,) = place(
            spot, (qkv_deep, qkv_other, qkv_far, qkv_across), [3 * head_width], kinds=3
        )
        full_qkv, *mid_pieces = lax.optimization_barrier((full_qkv, *mid_pieces))
        mid_deep = jnp.stack([mid] + mid_pieces)
        mid_other, mid_far = first_quad(mid_deep), second_quad(mid_deep)
        full_qkv, mid_deep = lax.optimization_barrier((full_qkv, mid_deep))
        down_pieces = deep_pieces(after(down_weight, *mid_pieces), spot)
    else:
        full_qkv = gathered_whole(by_pair(qkv_weight))
        full_mid = gathered_whole(mid)
        full_out, full_up = full_mid[:, :head_width], full_mid[:, head_width:]
        full_down = gathered_whole(down_weight)

    bias = by_pair(jnp.stack([qv_bias[0], jnp.zeros_like(qv_bias[0]), qv_bias[1]]))
    triple = triple_of(inputs, tokens_other, full_qkv, bias)
    attended = attention_forward(item_lengths, random_blocks, triple, position)
    if staged:
        attended, mid_other, mid_far, *down_pieces = lax.optimization_barrier(
            (attended, mid_other, mid_far, *down_pieces)
        )
        mid_across = second_quad(mid_other)
        down_deep = jnp.stack([down_weight] + down_pieces)
        down_other, down_far = first_quad(down_deep), second_quad(down_deep)
        mid_across, down_other = lax.optimization_barrier((mid_across, down_other))
        down_across = second_quad(down_other)
        full_out, full_up = place(
            spot, (mid_deep, mid_other, mid_far, mid_across), [head_width, up_width]
        )

    whole = (half, 2 * half)
    other = swap(rows_product([attended], full_out, whole, jnp.bfloat16))
    proj = rows_product([attended], full_out, (0, half), jnp.float32) + other.astype(jnp.float32)
    normed_one_out, normed_one, inverse_one = norm_forward(
        proj + out_bias + inputs.astype(jnp.float32), first_gain, first_shift
    )
    hidden_own = low(normed_one_out)
    hidden_other = swap(hidden_own)
    active_own, slope_own = up_gelu(hidden_own, full_up, up_bias)
    if staged:
        active_own, hidden_other, down_across = lax.optimization_barrier(
            (active_own, hidden_other, down_across)
        )
    active_other, slope_other = up_gelu(hidden_other, full_up, up_bias)
    if staged:
        active_other, active_own, down_far = lax.optimization_barrier(
            (active_other, active_own, down_far)
        )
        (full_down,) = place(spot, (down_deep, down_other, down_far, down_across), [up_width])
    other = swap(rows_product([active_other], full_down, (0, half), jnp.bfloat16))
    layer_out, grad_res_two, grad_own, sums_two = norm_two(
        item_lengths,
        rows_product([active_own], full_down, (0, half), jnp.float32),
        other,
        normed_one_out,
        out_grad,
        down_bias,
        second_gain,
        second_shift,
        position,
    )
    grad_other = swap(grad_own)
    grad_upper_own, up_sum_own = back_slope(grad_own, full_down, slope_own)
    down_local = outer([grad_own, grad_other], [active_own, active_other])
    if staged:
        near_message, far_message = sum_first_apart(down_local, spot)
        down_far_got = first_quad(far_message)
        grad_other, near_message = lax.optimization_barrier((grad_other, near_message))
        down_got = first_quad(near_message)
    grad_upper_other, up_sum_other = back_slope(grad_other, full_down, slope_other)
    other = swap(rows_product([grad_upper_other], full_up, (0, half), jnp.bfloat16))
    up_local = outer([hidden_own, hidden_other], [grad_upper_own, grad_upper_other])
    grad_res_one, grad_proj_own, sums_one = norm_one_back(
        rows_product([grad_upper_own], full_up, (0, half), jnp.float32), other, grad_res_two, normed_one, inverse_one, first_gain
    )
    if staged:
        grad_proj_own, down_far_got = lax.optimization_barrier((grad_proj_own, down_far_got))
        down_message = sum_second([down_local], spot, down_far_got)
        down_two = second_quad(down_message)
        grad_proj_own, down_message = lax.optimization_barrier((grad_proj_own, down_message))
    grad_proj_other = swap(grad_proj_own)
    shared = jnp.concatenate([sums_one, sums_two], axis=0)
    shared_other = swap(shared)
    grad_attended = project_both(grad_proj_own, grad_proj_other, full_out)
    out_local = outer([grad_proj_own, grad_proj_other], [attended])

    mids = [out_local, up_local]
    split = pair_count - 1
    if staged:
        mid_message = sum_first(mids, spot)
        mid_got = first_quad(mid_message)
        grad_attended, down_got = lax.optimization_barrier((grad_attended, down_got))
        grad_attended, mid_message = lax.optimization_barrier((grad_attended, mid_message))
    grads_a, sums_a = attention_backward(
        item_lengths, random_blocks, triple, grad_attended, range(split), position
    )
    if staged:
        grads_a, mid_got, down_two, grad_attended, shared_other = lax.optimization_barrier(
            (grads_a, mid_got, down_two, grad_attended, shared_other)
        )
        mid_message = sum_second(mids, spot, mid_got)
        mid_two = second_quad(mid_message)
        down_sum, *messages = sum_deep([[down_local]], spot, [down_got], [down_two])
        down_answers = [deep_step(m, deep, k + 1) for k, m in enumerate(messages)]
    local_a = outer([inputs, tokens_other], [grads_a])
    if staged:
        message_a = sum_first([local_a], spot)
        got_a = first_quad(message_a)
        grad_attended, message_a, mid_message, *messages = lax.optimization_barrier(
            (grad_attended, message_a, mid_message, *messages)
        )
    grads_b, sums_b = attention_backward(
        item_lengths, random_blocks, triple, grad_attended, range(split, pair_count), position
    )
    if staged:
        grads_b, got_a, mid_two, *down_answers = lax.optimization_barrier(
            (grads_b, got_a, mid_two, *down_answers)
        )
    local_b = outer([inputs, tokens_other], [grads_b])
    small = small_sums(shared, shared_other, up_sum_own, up_sum_other, [sums_a, sums_b])
    if staged:
        message_b = sum_first([local_b], spot, small)
        got_b = first_quad(message_b)
        message_a = sum_second([local_a], spot, after(got_a, message_b))
        two_a = second_quad(message_a)
        grads_a, grads_b, message_a = lax.optimization_barrier((grads_a, grads_b, message_a))
    product = rows_product([grads_a, grads_b], full_qkv, whole, jnp.bfloat16)
    if staged:
        mid_got, product = lax.optimization_barrier((mid_got, product))
        mid_sum, *messages = sum_deep([mids], spot, [mid_got], [mid_two])
        mid_answers = [deep_step(m, deep, k + 1) for k, m in enumerate(messages)]
        product, *messages = lax.optimization_barrier((product, *messages))
    other = swap(product)
    if staged:
        grads_a, other, got_b, two_a = lax.optimization_barrier((grads_a, other, got_b, two_a))
        message, small = sum_second([local_b], spot, got_b, small)
        two_b = second_quad(message)
        grads_a, message = lax.optimization_barrier((grads_a, message))
    mine = rows_product([grads_a, grads_b], full_qkv, (0, half), jnp.float32)
    input_grad = low(mine + other.astype(jnp.float32) + grad_res_one)
    if staged:
        (grad_down,) = sum_last(down_sum, down_answers, [up_width])
        input_grad, grad_down, two_b = lax.optimization_barrier((input_grad, grad_down, two_b))
        small, qkv_sum, *messages = sum_deep(
            [[local_a], [local_b]], spot, [got_a, got_b], [two_a, two_b], small
        )
        answers = [deep_step(m, deep, k + 1) for k, m in enumerate(messages)]
        grad_out, grad_up = sum_last(mid_sum, mid_answers, [head_width, up_width])
        grad_out, grad_up, *answers = lax.optimization_barrier((grad_out, grad_up, *answers))
        grad_qkv, small = sum_last(qkv_sum, answers, [3 * head_width], small)
        grad_qkv = jnp.swapaxes(grad_qkv, 0, 1)
    else:
        grad_down, grad_up, grad_out = (scattered(v) for v in (down_local, up_local, out_local))
        grad_qkv = by_kind(scattered(jnp.concatenate([local_a, local_b], axis=1)), 3)
        small = lax.psum(small, every)
        part = small.shape[0] // 3
        small = jnp.concatenate([small[n * part : (n + 1) * part] for n in range(3)], axis=1)

    totals = small[:, :width]
    rest = small[:, width : width + head_width]
    grad_up_bias = rest[: up_width // head_width].reshape(up_width)
    grad_qv_bias = rest[up_width // head_width :]
    return (
        layer_out,
        input_grad,
        grad_qkv,
        grad_qv_bias,
        grad_out,
        totals[0],
        totals[1],
        totals[2],
        grad_up,
        grad_up_bias,
        grad_down,
        totals[3],
        totals[4],
        totals[5],
    )


def solution(mesh):
    devices = mesh.devices.reshape(-1, QUAD, mesh.shape["head"])
    fine = Mesh(devices, ("deep", "quad", "head"))
    rows = ("deep", "quad", "head")
    dp = ("deep", "quad")
    in_specs = (
        P(rows, None),
        P(dp, None, "head"),
        P(None, "head"),
        P(dp, "head"),
        P(),
        P(),
        P(),
        P(dp, "head"),
        P("head"),
        P(dp, "head"),
        P(),
        P(),
        P(),
        P(dp, None),
        P(dp, "head", None, None),
        P(rows, None),
    )
    out_specs = (
        P(rows, None),
        P(rows, None),
        P(dp, None, "head"),
        P(None, "head"),
        P(dp, "head"),
        P(),
        P(),
        P(),
        P(dp, "head"),
        P("head"),
        P(dp, "head"),
        P(),
        P(),
        P(),
    )
    return jax.shard_map(
        on_device, mesh=fine, in_specs=in_specs, out_specs=out_specs, check_vma=False
    )
```

```python
import functools

import jax
import jax.numpy as jnp
import numpy as np
from jax import lax
from jax.experimental import pallas as pl
from jax.experimental.pallas import tpu as pltpu
from jax.sharding import Mesh
from jax.sharding import PartitionSpec as P

BLK = 64


norm_eps = 1e-06
negative = -1e30


def norm_forward(values, gain, shift):
    centered = values - jnp.mean(values, axis=-1, keepdims=True)
    inverse = lax.rsqrt(jnp.mean(centered * centered, axis=-1, keepdims=True) + norm_eps)
    normed = centered * inverse
    return (normed * gain + shift, normed, inverse)


def dot_nt(a, b):
    return lax.dot_general(a, b, (((1,), (1,)), ((), ())), preferred_element_type=jnp.float32)


def dot_nn(a, b):
    return lax.dot_general(a, b, (((1,), (0,)), ((), ())), preferred_element_type=jnp.float32)


def dot_tn(a, b):
    return lax.dot_general(a, b, (((0,), (0,)), ((), ())), preferred_element_type=jnp.float32)


PAIR = 2 * BLK


def even_lanes(rows):
    return lax.broadcasted_iota(jnp.int32, (rows, PAIR), 1) < BLK


def stacked(values):
    zero = jnp.zeros_like(values)
    even = even_lanes(BLK)
    return jnp.concatenate([jnp.where(even, values, zero), jnp.where(even, zero, values)], axis=0)


def unstacked(values):
    return jnp.where(even_lanes(BLK), values[:BLK], values[BLK:])


class Layout:
    def __init__(self, len_ref, rb_ref, blocks, position):
        self.len_ref, self.rb_ref, self.blocks = len_ref, rb_ref, blocks
        self.half = blocks // 2
        self.rand = rb_ref.shape[-1]
        self.shift = position * self.half

    def moved(self, index):
        at = index + self.shift
        return jnp.where(at >= self.blocks, at - self.blocks, at)

    def spot(self, index):
        return pl.ds(pl.multiple_of(self.moved(index) * BLK, BLK), BLK)

    def part(self, index):
        return pl.ds(pl.multiple_of(self.moved(index) * BLK, BLK), self.half * BLK)

    def counts(self):
        self.count0 = lax.div(self.len_ref[0, 0], BLK)
        self.count1 = lax.div(self.len_ref[0, 1], BLK)
        self.second = jnp.where(self.count1 > 0, 1, 0)
        self.inner = self.blocks - 2 - 2 * self.second

    def locate(self, i):
        in0 = i < self.count0 - 2
        self.b = b = jnp.where(in0, i + 1, i + 2 + self.second)
        self.live = live = b < self.count0 + self.count1
        self.first = first = jnp.where(in0, 0, jnp.where(live, self.count0, b))
        items = jnp.where(in0, self.count0, jnp.where(live, self.count1, 1))
        rel = b - first
        last = items - 1
        zero, neg = jnp.float32(0.0), jnp.float32(negative)
        self.fixed = [
            first,
            first + last,
            jnp.where(live, b - 1, b),
            jnp.where(live, b + 1, b),
            b,
        ]
        self.low_bias = jnp.where(live & (rel == 1), neg, zero)
        self.high_bias = jnp.where(live & (rel + 1 == last), neg, zero)
        return self

    def ends(self, item):
        first = jnp.where(item == 0, 0, self.count0)
        count = jnp.where(item == 0, self.count0, self.count1)
        return first, first + count - 1, lax.div(count, self.half)

    def chosen(self, head):
        return [
            jnp.where(self.live, self.first + self.rb_ref[0, head, self.b, k], self.b)
            for k in range(self.rand)
        ]


def gathered(ref, layout, column, picked):
    even = even_lanes(BLK)

    def rows(index):
        return ref[layout.spot(index), column : column + PAIR]

    return jnp.concatenate(
        [rows(i) for i in layout.fixed]
        + [jnp.where(even, rows(i), rows(j)) for i, j in zip(*picked)],
        axis=0,
    )


ROWS = 32


def soft_rows(held):
    probs, inverse = [], []
    for row in range(0, held.shape[0], ROWS):
        scores = held[row : row + ROWS, :]
        expo = jnp.exp(scores - jnp.max(scores, axis=1, keepdims=True))
        inverse.append(1.0 / jnp.sum(expo, axis=1, keepdims=True))
        probs.append(expo.astype(jnp.bfloat16))
    return jnp.concatenate(probs, axis=0), jnp.concatenate(inverse, axis=0)


def attn_fwd_kernel(pairs, position, len_ref, rb_ref, tri_ref, out_ref, wide, *held):
    blocks = tri_ref.shape[0] // BLK
    scale = jnp.bfloat16(BLK**-0.5)
    layout = Layout(len_ref, rb_ref, blocks, position())
    layout.counts()

    def query_of(p, b):
        at = layout.spot(b)
        return stacked(tri_ref[at, p * 3 * PAIR : p * 3 * PAIR + PAIR]) * scale

    def put(p, b, mixed):
        at = layout.spot(b)
        out_ref[at, p * PAIR : (p + 1) * PAIR] = unstacked(mixed).astype(jnp.bfloat16)

    def sparse_scores(i, held):
        at = layout.locate(i)
        lane = lax.broadcasted_iota(jnp.int32, (1, PAIR), 1) < BLK
        bias_row = jnp.where(lane, at.low_bias, at.high_bias)
        for n, p in enumerate(pairs):
            picked = [at.chosen(2 * p), at.chosen(2 * p + 1)]
            keys = gathered(tri_ref, at, (3 * p + 1) * PAIR, picked)
            scores = dot_nt(query_of(p, at.b), keys)
            held[n][...] = jnp.concatenate(
                [scores[:, :PAIR], scores[:, PAIR : 2 * PAIR] + bias_row, scores[:, 2 * PAIR :]],
                axis=1,
            )

    def sparse_mix(i, held):
        at = layout.locate(i)
        for n, p in enumerate(pairs):
            picked = [at.chosen(2 * p), at.chosen(2 * p + 1)]
            probs, inverse = soft_rows(held[n])
            values = gathered(tri_ref, at, (3 * p + 2) * PAIR, picked)
            put(p, at.b, dot_nn(probs, values) * inverse)

    held_a, held_b = held[: len(pairs)], held[len(pairs) :]
    sparse_scores(0, held_a)

    def two(j, carry):
        sparse_scores(2 * j + 1, held_b)
        sparse_mix(2 * j, held_a)
        sparse_scores(jnp.minimum(2 * j + 2, layout.inner - 1), held_a)
        sparse_mix(2 * j + 1, held_b)
        return carry

    lax.fori_loop(0, lax.div(layout.inner, 2), two, 0)

    def dense(item, carry):
        first, last, chunks = layout.ends(item)
        queries = [
            jnp.concatenate([query_of(p, first), query_of(p, last)], axis=0) for p in pairs
        ]

        def dense_of(spans):
            for query, p in zip(queries, pairs):
                span = layout.half * BLK
                for c, at in enumerate(spans):
                    keys = tri_ref[at, (3 * p + 1) * PAIR : (3 * p + 2) * PAIR]
                    wide[:, c * span : (c + 1) * span] = dot_nt(query, keys)
                probs, inverse = soft_rows(wide.at[:, : len(spans) * span])
                mixed = sum(
                    dot_nn(
                        probs[:, c * span : (c + 1) * span],
                        tri_ref[at, (3 * p + 2) * PAIR : (3 * p + 3) * PAIR],
                    )
                    for c, at in enumerate(spans)
                ) * inverse
                put(p, first, mixed[:PAIR])
                put(p, last, mixed[PAIR:])

        @pl.when(chunks == 1)
        def short():
            dense_of([layout.part(first)])

        @pl.when(chunks == 2)
        def long():
            dense_of([layout.part(first), layout.part(first + layout.half)])

        return carry

    lax.fori_loop(0, 1 + layout.second, dense, 0)


def grad_rows(held_scores, held_grads, probs_ref, grads_ref):
    for row in range(0, held_scores.shape[0], ROWS):
        at = slice(row, row + ROWS)
        scores = held_scores[at, :]
        grad_probs = held_grads[at, :]
        expo = jnp.exp(scores - jnp.max(scores, axis=1, keepdims=True))
        probs = expo * (1.0 / jnp.sum(expo, axis=1, keepdims=True))
        delta = jnp.sum(probs * grad_probs, axis=1, keepdims=True)
        probs_ref[at, :] = probs.astype(jnp.bfloat16)
        grads_ref[at, :] = (probs * (grad_probs - delta)).astype(jnp.bfloat16)


def attn_bwd_kernel(
    pairs, position, len_ref, rb_ref, tri_ref, grad_ref, out_ref, sum_ref, *scratch
):
    blocks = tri_ref.shape[0] // BLK
    scale = jnp.bfloat16(BLK**-0.5)
    back = BLK**-0.5
    layout = Layout(len_ref, rb_ref, blocks, position())
    layout.counts()
    count = len(pairs)
    key_acc, value_acc = scratch[:count], scratch[count : 2 * count]
    held_a, held_b, done = (scratch[n * count : (n + 2) * count] for n in (2, 4, 6))
    wide = scratch[8 * count :]

    def clear(r, carry):
        at = pl.ds(pl.multiple_of(r * BLK, BLK), BLK)
        for acc in scratch[: 2 * count]:
            acc[at, :] = jnp.zeros((BLK, PAIR), jnp.float32)
        return carry

    lax.fori_loop(0, blocks, clear, 0)

    def query_of(p, b):
        at = layout.spot(b)
        return stacked(tri_ref[at, p * 3 * PAIR : p * 3 * PAIR + PAIR]) * scale

    def grad_of(p, b):
        at = layout.spot(b)
        return stacked(grad_ref[at, p * PAIR : (p + 1) * PAIR])

    def put(i, b, grad_query):
        out_ref[layout.spot(b), i * 3 * PAIR : i * 3 * PAIR + PAIR] = unstacked(
            grad_query * back
        ).astype(jnp.bfloat16)

    def sparse_scores(n, held):
        at = layout.locate(n)
        lane = lax.broadcasted_iota(jnp.int32, (1, PAIR), 1) < BLK
        bias_row = jnp.where(lane, at.low_bias, at.high_bias)
        for i, p in enumerate(pairs):
            picked = [at.chosen(2 * p), at.chosen(2 * p + 1)]
            keys = gathered(tri_ref, at, (3 * p + 1) * PAIR, picked)
            values = gathered(tri_ref, at, (3 * p + 2) * PAIR, picked)
            scores = dot_nt(query_of(p, at.b), keys)
            held[2 * i][...] = jnp.concatenate(
                [scores[:, :PAIR], scores[:, PAIR : 2 * PAIR] + bias_row, scores[:, 2 * PAIR :]],
                axis=1,
            )
            held[2 * i + 1][...] = dot_nt(grad_of(p, at.b), values)

    def sparse_grads(n, held):
        at = layout.locate(n)
        even = even_lanes(BLK)
        for i, p in enumerate(pairs):
            grad_rows(held[2 * i], held[2 * i + 1], done[2 * i], done[2 * i + 1])
            picked = [at.chosen(2 * p), at.chosen(2 * p + 1)]
            spots = [at.spot(index) for index in at.fixed]
            spots += [(at.spot(one), at.spot(two)) for one, two in zip(*picked)]
            keys = gathered(tri_ref, at, (3 * p + 1) * PAIR, picked)
            put(i, at.b, dot_nn(done[2 * i + 1][...], keys))
            for acc, update in (
                (key_acc[i], dot_tn(done[2 * i + 1][...], query_of(p, at.b))),
                (value_acc[i], dot_tn(done[2 * i][...], grad_of(p, at.b))),
            ):
                for j, spot in enumerate(spots):
                    piece = update[j * BLK : (j + 1) * BLK]
                    if j < len(at.fixed):
                        acc[spot, :] += piece
                    else:
                        zero = jnp.zeros_like(piece)
                        acc[spot[0], :] += jnp.where(even, piece, zero)
                        acc[spot[1], :] += jnp.where(even, zero, piece)

    sparse_scores(0, held_a)

    def two(j, carry):
        sparse_scores(2 * j + 1, held_b)
        sparse_grads(2 * j, held_a)
        sparse_scores(jnp.minimum(2 * j + 2, layout.inner - 1), held_a)
        sparse_grads(2 * j + 1, held_b)
        return carry

    lax.fori_loop(0, lax.div(layout.inner, 2), two, 0)

    wide_scores, wide_grads, wide_probs, wide_out = wide

    def dense(item, carry):
        first, last, chunks = layout.ends(item)

        def dense_of(spans):
            span = layout.half * BLK
            cover = len(spans) * span
            def end(n, carry):
                b = jnp.where(n == 0, first, last)
                for i, p in enumerate(pairs):
                    query, grad = query_of(p, b), grad_of(p, b)
                    for c, at in enumerate(spans):
                        cut = slice(c * span, (c + 1) * span)
                        keys = tri_ref[at, (3 * p + 1) * PAIR : (3 * p + 2) * PAIR]
                        values = tri_ref[at, (3 * p + 2) * PAIR : (3 * p + 3) * PAIR]
                        wide_scores[:, cut] = dot_nt(query, keys)
                        wide_grads[:, cut] = dot_nt(grad, values)
                    grad_rows(*(ref.at[:, :cover] for ref in wide))
                    total = jnp.zeros((PAIR, PAIR), jnp.float32)
                    for c, at in enumerate(spans):
                        cut = slice(c * span, (c + 1) * span)
                        keys = tri_ref[at, (3 * p + 1) * PAIR : (3 * p + 2) * PAIR]
                        total += dot_nn(wide_out[:, cut], keys)
                        key_acc[i][at, :] += dot_tn(wide_out[:, cut], query)
                        value_acc[i][at, :] += dot_tn(wide_probs[:, cut], grad)
                    put(i, b, total)
                return carry

            lax.fori_loop(0, 2, end, 0)

        @pl.when(chunks == 1)
        def short():
            dense_of([layout.part(first)])

        @pl.when(chunks == 2)
        def long():
            dense_of([layout.part(first), layout.part(first + layout.half)])

        return carry

    lax.fori_loop(0, 1 + layout.second, dense, 0)

    sum_ref[...] = jnp.zeros_like(sum_ref)

    def finish(r, carry):
        at = pl.ds(pl.multiple_of(r * BLK, BLK), BLK)
        new = []
        for i in range(count):
            column = i * 3 * PAIR
            query_sum, value_sum = carry[i]
            out_ref[at, column + PAIR : column + 2 * PAIR] = key_acc[i][at, :].astype(jnp.bfloat16)
            value = value_acc[i][at, :].astype(jnp.bfloat16)
            out_ref[at, column + 2 * PAIR : column + 3 * PAIR] = value
            query = out_ref[at, column : column + PAIR].astype(jnp.float32)
            new.append(
                tuple(
                    total + jnp.sum(part.reshape(-1, 8, PAIR), axis=0)
                    for total, part in (
                        (query_sum, query),
                        (value_sum, value.astype(jnp.float32)),
                    )
                )
            )
        return tuple(new)

    zero = jnp.zeros((8, PAIR), jnp.float32)
    sums = lax.fori_loop(0, blocks, finish, tuple((zero, zero) for _ in pairs))
    for i, totals in enumerate(sums):
        for kind, total in enumerate(totals):
            sum_ref[kind : kind + 1, i * PAIR : (i + 1) * PAIR] = jnp.sum(
                total, axis=0, keepdims=True
            )


vmem = pl.BlockSpec(memory_space=pltpu.VMEM)
smem = pl.BlockSpec(memory_space=pltpu.SMEM)
def attention_forward(lengths, randoms, triple, position):
    pairs = randoms.shape[1] // 2
    rows = triple.shape[0]
    area = rows * rows // 3 * 2 * pairs
    return pl.pallas_call(
        functools.partial(attn_fwd_kernel, range(pairs), position),
        out_shape=jax.ShapeDtypeStruct((rows, pairs * PAIR), jnp.bfloat16),
        in_specs=[smem, smem, vmem],
        out_specs=vmem,
        name="attend_forward",
        scratch_shapes=[pltpu.VMEM((2 * PAIR, rows), jnp.float32)]
        + [pltpu.VMEM((PAIR, 8 * BLK), jnp.float32)] * (2 * pairs),
        cost_estimate=pl.CostEstimate(
            flops=16 * area * PAIR, transcendentals=area, bytes_accessed=rows * pairs * PAIR * 8
        ),
        compiler_params=pltpu.CompilerParams(vmem_limit_bytes=8 << 20),
    )(lengths, randoms, triple)


def attention_backward(lengths, randoms, triple, grad, pairs, position):
    rows = triple.shape[0]
    count = len(pairs)
    area = rows * rows // 3 * 2 * count
    return pl.pallas_call(
        functools.partial(attn_bwd_kernel, pairs, position),
        out_shape=(
            jax.ShapeDtypeStruct((rows, count * 3 * PAIR), jnp.bfloat16),
            jax.ShapeDtypeStruct((8, count * PAIR), jnp.float32),
        ),
        in_specs=[smem, smem, vmem, vmem],
        out_specs=(vmem, vmem),
        name="attend_backward",
        scratch_shapes=[pltpu.VMEM((rows, PAIR), jnp.float32)] * (2 * count)
        + [pltpu.VMEM((PAIR, 8 * BLK), jnp.float32)] * (4 * count)
        + [pltpu.VMEM((PAIR, 8 * BLK), jnp.bfloat16)] * (2 * count)
        + [pltpu.VMEM((PAIR, rows), kind) for kind in (jnp.float32,) * 2 + (jnp.bfloat16,) * 2],
        cost_estimate=pl.CostEstimate(
            flops=40 * area * PAIR, transcendentals=area, bytes_accessed=rows * count * PAIR * 20
        ),
        compiler_params=pltpu.CompilerParams(vmem_limit_bytes=20 << 20),
    )(lengths, randoms, triple, grad)


TILE = 256
EPS = 1e-06


def tile_at(n):
    return pl.ds(pl.multiple_of(n * TILE, TILE), TILE)


def up_kernel(rows_ref, weight_ref, bias_ref, active_ref, slope_ref, held_a, held_b):
    tiles = weight_ref.shape[1] // TILE
    root = (2.0 / np.pi) ** 0.5
    cube = 0.044715 * root

    def product(n, held):
        held[...] = dot_nn(rows_ref[...], weight_ref[:, tile_at(n)])

    def gelu(n, held):
        bias = bias_ref[:, tile_at(n)]
        for row in range(0, held.shape[0], ROWS):
            at = slice(row, row + ROWS)
            upper = (held[at, :] + bias).astype(jnp.bfloat16).astype(jnp.float32)
            square = upper * upper
            half = 0.5 + 0.5 * jnp.tanh(upper * (square * cube + root))
            active = upper * half
            active_ref[at, tile_at(n)] = active.astype(jnp.bfloat16)
            bend = (1.0 - half) * (square * (6.0 * cube) + 2.0 * root)
            slope_ref[at, tile_at(n)] = (half + active * bend).astype(jnp.bfloat16)

    product(0, held_a)

    def two(j, carry):
        product(2 * j + 1, held_b)
        gelu(2 * j, held_a)
        product(jnp.minimum(2 * j + 2, tiles - 1), held_a)
        gelu(2 * j + 1, held_b)
        return carry

    lax.fori_loop(0, tiles // 2, two, 0)


def up_gelu(rows, weight, bias):
    count, width = rows.shape[0], weight.shape[1]
    shape = jax.ShapeDtypeStruct((count, width), jnp.bfloat16)
    return pl.pallas_call(
        up_kernel,
        out_shape=(shape, shape),
        in_specs=[vmem] * 3,
        out_specs=(vmem, vmem),
        name="up_gelu",
        scratch_shapes=[pltpu.VMEM((count, TILE), jnp.float32)] * 2,
        cost_estimate=pl.CostEstimate(
            flops=2 * count * width * rows.shape[1],
            transcendentals=count * width,
            bytes_accessed=2 * (rows.size + weight.size + 2 * count * width),
        ),
        compiler_params=pltpu.CompilerParams(vmem_limit_bytes=12 << 20),
    )(rows, weight, bias.reshape(1, -1))


def back_kernel(grad_ref, weight_ref, slope_ref, out_ref, sum_ref):
    def step(n, carry):
        grad_active = dot_nn(grad_ref[...], weight_ref[:, tile_at(n)])
        total = jnp.zeros((8, TILE), jnp.float32)
        for row in range(0, grad_active.shape[0], ROWS):
            at = slice(row, row + ROWS)
            grad = grad_active[at] * slope_ref[at, tile_at(n)].astype(jnp.float32)
            grad = grad.astype(jnp.bfloat16)
            out_ref[at, tile_at(n)] = grad
            total += jnp.sum(grad.astype(jnp.float32).reshape(-1, 8, TILE), axis=0)
        sum_ref[:, tile_at(n)] = total
        return carry

    lax.fori_loop(0, weight_ref.shape[1] // TILE, step, 0)


def back_slope(grad, weight, slope):
    count, width = slope.shape
    return pl.pallas_call(
        back_kernel,
        out_shape=(
            jax.ShapeDtypeStruct((count, width), jnp.bfloat16),
            jax.ShapeDtypeStruct((8, width), jnp.float32),
        ),
        in_specs=[vmem] * 3,
        out_specs=(vmem, vmem),
        name="back_slope",
        cost_estimate=pl.CostEstimate(
            flops=2 * count * width * grad.shape[1],
            transcendentals=0,
            bytes_accessed=2 * (grad.size + weight.size + 2 * count * width),
        ),
        compiler_params=pltpu.CompilerParams(vmem_limit_bytes=12 << 20),
    )(grad, weight, slope)


def outer_kernel(count, *refs):
    lefts, rights, out_ref = refs[:count], refs[count:-1], refs[-1]
    if len(rights) < count:
        rows = lefts[0].shape[0]
        rights = [rights[0].at[n * rows : (n + 1) * rows] for n in range(count)]

    def step(at):
        total = sum(dot_tn(a[...], b[:, at]) for a, b in zip(lefts, rights))
        out_ref[:, at] = total.astype(jnp.bfloat16)

    width = out_ref.shape[1]
    if width % TILE:
        step(slice(0, width))
    else:

        def body(n, carry):
            step(tile_at(n))
            return carry

        lax.fori_loop(0, width // TILE, body, 0)


def outer(lefts, rights):
    shape = (lefts[0].shape[1], rights[0].shape[1])
    inner = sum(a.shape[0] for a in lefts)
    return pl.pallas_call(
        functools.partial(outer_kernel, len(lefts)),
        out_shape=jax.ShapeDtypeStruct(shape, jnp.bfloat16),
        in_specs=[vmem] * (len(lefts) + len(rights)),
        out_specs=vmem,
        name="outer",
        cost_estimate=pl.CostEstimate(
            flops=2 * inner * shape[0] * shape[1],
            transcendentals=0,
            bytes_accessed=2 * inner * sum(shape),
        ),
        compiler_params=pltpu.CompilerParams(vmem_limit_bytes=12 << 20),
    )(*lefts, *rights)


def project_kernel(own_ref, other_ref, weight_ref, out_ref):
    rows = own_ref.shape[0]
    for n, ref in enumerate((own_ref, other_ref)):
        product = dot_nn(ref[...], weight_ref[...])
        out_ref[n * rows : (n + 1) * rows, :] = product.astype(jnp.bfloat16)


def project_both(own, other, weight):
    return pl.pallas_call(
        project_kernel,
        out_shape=jax.ShapeDtypeStruct((2 * own.shape[0], weight.shape[1]), jnp.bfloat16),
        in_specs=[vmem] * 3,
        out_specs=vmem,
        name="project_both",
        compiler_params=pltpu.CompilerParams(vmem_limit_bytes=12 << 20),
    )(own, other, weight)


GROUP = 16
SPLIT = 12


def groups_at(r):
    return [
        (r * SPLIT + n, pl.ds(pl.multiple_of((r * SPLIT + n) * GROUP, GROUP), GROUP))
        for n in range(SPLIT)
    ]


def row_mean(values):
    return jnp.sum(values, axis=1, keepdims=True) * (1.0 / values.shape[1])


def folded(values):
    return jnp.sum(values.reshape(-1, 8, values.shape[1]), axis=0)


def norm_two_kernel(position, len_ref, down_ref, other_ref, resid_ref, cot_ref, vec_ref, out_ref, grad_ref, low_ref, sum_ref):
    count, width = down_ref.shape
    live_rows = len_ref[0, 0] + len_ref[0, 1] - position() * count
    bias, gain, shift = (vec_ref[n : n + 1, :] for n in range(3))

    def group(r, at, sums):
        row = r * GROUP + lax.broadcasted_iota(jnp.int32, (GROUP, 1), 0)
        live = jnp.where(row < live_rows, 1.0, 0.0)
        values = down_ref[at, :] + other_ref[at, :].astype(jnp.float32) + bias + resid_ref[at, :]
        centered = values - row_mean(values)
        inverse = lax.rsqrt(row_mean(centered * centered) + EPS)
        normed = centered * inverse
        out_ref[at, :] = ((normed * gain + shift) * live).astype(jnp.bfloat16)
        cot = cot_ref[at, :].astype(jnp.float32) * live
        scaled = cot * gain
        grad = inverse * (scaled - row_mean(scaled) - normed * row_mean(scaled * normed))
        grad_ref[at, :] = grad
        low_ref[at, :] = grad.astype(jnp.bfloat16)
        return tuple(s + folded(v) for s, v in zip(sums, (grad, cot * normed, cot)))

    def step(r, sums):
        for n, at in groups_at(r):
            sums = group(n, at, sums)
        return sums

    zero = jnp.zeros((8, width), jnp.float32)
    sums = lax.fori_loop(0, count // (GROUP * SPLIT), step, (zero,) * 3)
    for n, total in enumerate(sums):
        sum_ref[n : n + 1, :] = jnp.sum(total, axis=0, keepdims=True)
    sum_ref[3:8, :] = jnp.zeros((5, width), jnp.float32)


def norm_two(lengths, down, other, resid, cot, bias, gain, shift, position):
    shape = down.shape
    row = jax.ShapeDtypeStruct((8, shape[1]), jnp.float32)
    return pl.pallas_call(
        functools.partial(norm_two_kernel, position),
        out_shape=(
            jax.ShapeDtypeStruct(shape, jnp.bfloat16),
            jax.ShapeDtypeStruct(shape, jnp.float32),
            jax.ShapeDtypeStruct(shape, jnp.bfloat16),
            row,
        ),
        in_specs=[smem] + [vmem] * 5,
        out_specs=(vmem,) * 4,
        name="norm_two",
        cost_estimate=pl.CostEstimate(
            flops=40 * down.size, transcendentals=0, bytes_accessed=20 * down.size
        ),
        compiler_params=pltpu.CompilerParams(vmem_limit_bytes=12 << 20),
    )(lengths, down, other, resid, cot, jnp.stack([bias, gain, shift]))


def norm_one_kernel(own_ref, other_ref, grad_ref, normed_ref, inverse_ref, gain_ref, out_ref, low_ref, sum_ref):
    count, width = own_ref.shape
    gain = gain_ref[...]

    def group(r, at, sums):
        grad = own_ref[at, :] + other_ref[at, :].astype(jnp.float32) + grad_ref[at, :]
        normed = normed_ref[at, :]
        scaled = grad * gain
        result = inverse_ref[at, :] * (
            scaled - row_mean(scaled) - normed * row_mean(scaled * normed)
        )
        out_ref[at, :] = result
        low_ref[at, :] = result.astype(jnp.bfloat16)
        return tuple(s + folded(v) for s, v in zip(sums, (result, grad * normed, grad)))

    def step(r, sums):
        for n, at in groups_at(r):
            sums = group(n, at, sums)
        return sums

    zero = jnp.zeros((8, width), jnp.float32)
    sums = lax.fori_loop(0, count // (GROUP * SPLIT), step, (zero,) * 3)
    for n, total in enumerate(sums):
        sum_ref[n : n + 1, :] = jnp.sum(total, axis=0, keepdims=True)
    sum_ref[3:8, :] = jnp.zeros((5, width), jnp.float32)


def norm_one_back(own, other, grad, normed, inverse, gain):
    shape = own.shape
    return pl.pallas_call(
        norm_one_kernel,
        out_shape=(
            jax.ShapeDtypeStruct(shape, jnp.float32),
            jax.ShapeDtypeStruct(shape, jnp.bfloat16),
            jax.ShapeDtypeStruct((8, shape[1]), jnp.float32),
        ),
        in_specs=[vmem] * 6,
        out_specs=(vmem,) * 3,
        name="norm_one_back",
        cost_estimate=pl.CostEstimate(
            flops=20 * own.size, transcendentals=0, bytes_accessed=20 * own.size
        ),
        compiler_params=pltpu.CompilerParams(vmem_limit_bytes=12 << 20),
    )(own, other, grad, normed, inverse, gain.reshape(1, -1))


def pack_rows(ref, at, small):
    rows = small.shape[0]
    high = small.astype(jnp.bfloat16)
    ref[at : at + rows, :] = high
    ref[at + rows : at + 2 * rows, :] = (small - high.astype(jnp.float32)).astype(jnp.bfloat16)


def unpack_rows(ref, at, rows):
    high = ref[at : at + rows, :].astype(jnp.float32)
    return high + ref[at + rows : at + 2 * rows, :].astype(jnp.float32)


def slab_at(at_ref, place, z, rows):
    return pl.ds(pl.multiple_of((z * QUAD + at_ref[place]) * rows, rows), rows)


def columns_of(totals):
    cuts, low = [], 0
    for total in totals:
        cuts.append(slice(low, low + total.shape[1]))
        low += total.shape[1]
    return cuts


def sum_first_kernel(count, deep, apart, at_ref, *refs):
    totals, rest = refs[:count], refs[count:]
    rows = totals[0].shape[0] // (deep * QUAD)
    halves = [(1, 0), (3, deep * rows)]
    if apart:
        halves = [(1, 0), (3, 0)]
    for part, (place, low) in enumerate(halves):
        out_ref = rest[part - 2] if apart else rest[-1]
        for z in range(deep):
            row = low + z * rows
            for total, cut in zip(totals, columns_of(totals)):
                out_ref[row : row + rows, cut] = total[slab_at(at_ref, place, z, rows), :]
    if len(rest) > 1 and not apart:
        pack_rows(rest[-1], 2 * deep * rows, rest[0][...])


def sum_second_kernel(count, deep, at_ref, *refs):
    totals, got_ref = refs[:count], refs[count]
    rows = totals[0].shape[0] // (deep * QUAD)
    if len(refs) > count + 2:
        small_ref, out_ref, new_ref = refs[count + 1 :]
        small = small_ref[...] + unpack_rows(got_ref, 2 * deep * rows, small_ref.shape[0])
        new_ref[...] = small
        pack_rows(out_ref, deep * rows, small)
    else:
        out_ref = refs[-1]
    for z in range(deep):
        for total, cut in zip(totals, columns_of(totals)):
            far = total[slab_at(at_ref, 2, z, rows), :].astype(jnp.float32)
            row = z * rows + (deep * rows if got_ref.shape[0] >= 2 * deep * rows else 0)
            far = far + got_ref[row : row + rows, cut].astype(jnp.float32)
            out_ref[z * rows : (z + 1) * rows, cut] = far.astype(jnp.bfloat16)


def sum_deep_kernel(groups, deep, small_rows, at_ref, *refs):
    count = sum(groups)
    totals, refs = refs[:count], refs[count:]
    gots, twos, refs = refs[: len(groups)], refs[len(groups) : 2 * len(groups)], refs[2 * len(groups) :]
    rows = totals[0].shape[0] // (deep * QUAD)
    small = None
    if small_rows:
        small_ref, new_ref, refs = refs[0], refs[1], refs[2:]
        small = small_ref[...] + unpack_rows(twos[-1], deep * rows, small_rows)
        part = new_ref.shape[0]
        cuts = [small[n * part : (n + 1) * part] for n in range(small_rows // part)]
        small = jnp.concatenate(cuts, axis=1)
        new_ref[...] = small
    out_cuts = columns_of(totals)
    for k in range(deep):
        z = at_ref[QUAD] ^ k
        near = pl.ds(pl.multiple_of(z * rows, rows), rows)
        n = 0
        for group, got_ref, two_ref in zip(groups, gots, twos):
            members = totals[n : n + group]
            for total, cut, out_cut in zip(members, columns_of(members), out_cuts[n : n + group]):
                value = (
                    total[slab_at(at_ref, 0, z, rows), :].astype(jnp.float32)
                    + got_ref[near, cut].astype(jnp.float32)
                    + two_ref[near, cut].astype(jnp.float32)
                )
                refs[k][:rows, out_cut] = value.astype(refs[k].dtype)
            n += group
        if k and small is not None:
            pack_rows(refs[k], rows, small)


def sum_last_kernel(count, small_rows, *refs):
    own_ref, answers = refs[0], refs[1 : 1 + count]
    rows = own_ref.shape[0]
    own = own_ref[...]
    for answer in answers:
        own = own + answer[:rows, :].astype(jnp.float32)
    outs = refs[1 + count :]
    if small_rows:
        small_ref, new_ref, outs = outs[0], outs[-1], outs[1:-1]
        small = small_ref[...]
        for answer in answers:
            small = small + unpack_rows(answer, rows, small_rows)
        new_ref[...] = small
    if len(outs[0].shape) == 3:
        kinds = outs[0].shape[0]
        for n in range(own.shape[1] // PAIR):
            pair, kind = n // kinds, n % kinds
            cut = slice(pair * PAIR, (pair + 1) * PAIR)
            outs[0][kind, :, cut] = own[:, n * PAIR : (n + 1) * PAIR]
        up_ref, qv_ref = outs[1:]
        wide = qv_ref.shape[1]
        rest = small[:, -wide:]
        ups = up_ref.shape[1] // wide
        for n in range(ups):
            up_ref[:, n * wide : (n + 1) * wide] = rest[n : n + 1]
        qv_ref[...] = rest[ups : ups + 2]
        return
    for out_ref, cut in zip(outs, columns_of(outs)):
        out_ref[...] = own[:, cut]


def vmem_call(kernel, outs, operands, name, scalars=1, limit=12):
    outs = [jax.ShapeDtypeStruct(shape, dtype) for shape, dtype in outs]
    return pl.pallas_call(
        kernel,
        out_shape=outs,
        in_specs=[smem] * scalars + [vmem] * (len(operands) - scalars),
        out_specs=[vmem] * len(outs),
        name=name,
        compiler_params=pltpu.CompilerParams(vmem_limit_bytes=limit << 20),
    )(*operands)


def sum_first_apart(total, spot):
    shape = (total.shape[0] // QUAD, total.shape[1])
    kernel = functools.partial(sum_first_kernel, 1, spot.deep, True)
    return vmem_call(kernel, [(shape, jnp.bfloat16)] * 2, [spot.at, total], "sum_first")


def sum_first(totals, spot, small=None):
    span = totals[0].shape[0] // QUAD
    extra = 0 if small is None else 2 * small.shape[0]
    shape = (2 * span + extra, sum(t.shape[1] for t in totals))
    operands = [spot.at, *totals] + ([] if small is None else [small])
    kernel = functools.partial(sum_first_kernel, len(totals), spot.deep, False)
    return vmem_call(kernel, [(shape, jnp.bfloat16)], operands, "sum_first")[0]


def sum_second(totals, spot, got, small=None):
    span = totals[0].shape[0] // QUAD
    kernel = functools.partial(sum_second_kernel, len(totals), spot.deep)
    operands = [spot.at, *totals, got]
    if small is None:
        outs = [((span, got.shape[1]), jnp.bfloat16)]
        return vmem_call(kernel, outs, operands, "sum_second")[0]
    outs = [((span + 2 * small.shape[0], got.shape[1]), jnp.bfloat16), (small.shape, jnp.float32)]
    return vmem_call(kernel, outs, operands + [small], "sum_second")


def sum_deep(groups, spot, gots, twos, small=None):
    totals = [total for group in groups for total in group]
    rows = totals[0].shape[0] // (QUAD * spot.deep)
    columns = sum(t.shape[1] for t in totals)
    small_rows = 0 if small is None else small.shape[0]
    kernel = functools.partial(
        sum_deep_kernel, [len(group) for group in groups], spot.deep, small_rows
    )
    operands = [spot.at, *totals, *gots, *twos] + ([] if small is None else [small])
    outs, extra = [], 0
    if small is not None:
        part = small_rows // 3
        outs, extra = [((part, columns), jnp.float32)], 2 * part
    outs += [((rows, columns), jnp.float32)]
    outs += [((rows + extra, columns), jnp.bfloat16)] * (spot.deep - 1)
    return vmem_call(kernel, outs, operands, "sum_deep")


def sum_last(own, answers, widths, small=None, up_width=0):
    kernel = functools.partial(
        sum_last_kernel, len(answers), 0 if small is None else small.shape[0]
    )
    operands = [own, *answers] + ([] if small is None else [small])
    outs = [((own.shape[0], w), jnp.float32) for w in widths]
    if small is not None:
        width = widths[0] // 3
        outs = [((3, own.shape[0], width), jnp.float32)]
        outs += [((1, up_width), jnp.float32), ((2, width), jnp.float32)]
    outs += [] if small is None else [(small.shape, jnp.float32)]
    return vmem_call(kernel, outs, operands, "sum_last", scalars=0)


def small_kernel(own_ref, swapped_ref, up_one_ref, up_two_ref, *refs):
    out_ref = refs[-1]
    columns = out_ref.shape[1]
    both = own_ref[...] + swapped_ref[...]
    rows = [both[0:3], both[8:11]]
    row = 0
    for low in range(0, both.shape[1], columns):
        for part in rows:
            out_ref[row : row + 3, :] = part[:, low : low + columns]
            row += 3
    up = jnp.sum(up_one_ref[...] + up_two_ref[...], axis=0, keepdims=True)
    for low in range(0, up.shape[1], columns):
        out_ref[row : row + 1, :] = up[:, low : low + columns]
        row += 1
    low = 0
    for ref in refs[:-1]:
        out_ref[row : row + 2, low : low + ref.shape[1]] = ref[0:2, :]
        low += ref.shape[1]


def small_sums(own, swapped, up_one, up_two, sums):
    columns = sum(s.shape[1] for s in sums)
    rows = 6 * own.shape[1] // columns + up_one.shape[1] // columns + 2
    return vmem_call(
        small_kernel,
        [((rows, columns), jnp.float32)],
        [own, swapped, up_one, up_two, *sums],
        "small_sums",
        scalars=0,
    )[0]


def rows_kernel(window, cuts, *refs):
    lefts, weight_ref, out_ref = refs[:-2], refs[-2], refs[-1]
    rows = slice(*window)

    def step(n, carry):
        total = sum(
            dot_nt(left[rows, :], weight_ref[tile_at(n), cut]) for left, cut in zip(lefts, cuts)
        )
        out_ref[:, tile_at(n)] = total.astype(out_ref.dtype)
        return carry

    lax.fori_loop(0, out_ref.shape[1] // TILE, step, 0)


def rows_product(lefts, weight, window, dtype):
    shape = (window[1] - window[0], weight.shape[0])
    return pl.pallas_call(
        functools.partial(rows_kernel, window, columns_of(lefts)),
        out_shape=jax.ShapeDtypeStruct(shape, dtype),
        in_specs=[vmem] * (len(lefts) + 1),
        out_specs=vmem,
        name="rows_product",
        cost_estimate=pl.CostEstimate(
            flops=2 * shape[0] * weight.size,
            transcendentals=0,
            bytes_accessed=2 * (shape[0] * sum(weight.shape) + weight.size),
        ),
        compiler_params=pltpu.CompilerParams(vmem_limit_bytes=12 << 20),
    )(*lefts, weight)


def triple_kernel(own_ref, other_ref, weight_ref, bias_ref, out_ref):
    rows = own_ref.shape[0]
    span = 3 * PAIR

    def step(n, carry):
        at = pl.ds(pl.multiple_of(n * span, span), span)
        for k, ref in enumerate((own_ref, other_ref)):
            product = dot_nn(ref[...], weight_ref[:, at]) + bias_ref[:, at]
            out_ref[k * rows : (k + 1) * rows, at] = product.astype(jnp.bfloat16)
        return carry

    lax.fori_loop(0, out_ref.shape[1] // span, step, 0)


def triple_of(own, other, weight, bias):
    shape = (2 * own.shape[0], weight.shape[1])
    return pl.pallas_call(
        triple_kernel,
        out_shape=jax.ShapeDtypeStruct(shape, jnp.bfloat16),
        in_specs=[vmem] * 4,
        out_specs=vmem,
        name="triple",
        cost_estimate=pl.CostEstimate(
            flops=2 * shape[0] * weight.size,
            transcendentals=0,
            bytes_accessed=2 * (shape[0] * sum(weight.shape) + weight.size),
        ),
        compiler_params=pltpu.CompilerParams(vmem_limit_bytes=12 << 20),
    )(own, other, weight, bias.reshape(1, -1))


QUAD = 4


def group_permute(value, deep, target):
    pairs = []
    for z in range(deep):
        for q in range(QUAD):
            for h in range(2):
                to_z, to_q = target(z, q, h)
                pairs.append(((z * QUAD + q) * 2 + h, (to_z * QUAD + to_q) * 2 + h))
    return lax.ppermute(value, ("deep", "quad", "head"), pairs)


def deep_step(value, deep, bit):
    return group_permute(value, deep, lambda z, q, h: (z ^ bit, q))


def quad_step(value, deep, second):
    return group_permute(value, deep, lambda z, q, h: (z, q ^ ((2 >> h) if second else (1 << h))))


def swap(value):
    return lax.ppermute(value, "head", [(0, 1), (1, 0)])


def after(value, *others):
    return lax.optimization_barrier((value,) + others)[0]


class Spot:
    def __init__(self):
        self.z, self.q, self.h = (lax.axis_index(a) for a in ("deep", "quad", "head"))
        self.deep = lax.axis_size("deep")
        one, two = 1 << self.h, 2 >> self.h
        self.places = [self.q, self.q ^ one, self.q ^ two, self.q ^ 3]
        self.at = jnp.stack(self.places + [self.z]).astype(jnp.int32)


def deep_pieces(value, spot):
    return [deep_step(value, spot.deep, k) for k in range(1, spot.deep)]


def place_kernel(deep, windows, kinds, at_ref, *refs):
    pieces, outs = refs[:QUAD], refs[QUAD:]
    rows = pieces[0].shape[1] // kinds
    for k in range(deep):
        for j, piece in enumerate(pieces):
            row = pl.multiple_of(((at_ref[QUAD] ^ k) * QUAD + at_ref[j]) * rows, rows)
            at = pl.ds(row, rows)
            if kinds > 1:
                for n in range(kinds * piece.shape[2] // PAIR):
                    pair, kind = n // kinds, n % kinds
                    outs[0][at, n * PAIR : (n + 1) * PAIR] = piece[
                        k, kind * rows : (kind + 1) * rows, pair * PAIR : (pair + 1) * PAIR
                    ]
                continue
            for out, (low, high) in zip(outs, windows):
                out[at, :] = piece[k, :, low:high]


def place(spot, pieces, widths, kinds=1):
    windows, low = [], 0
    for width in widths:
        windows.append((low, low + width))
        low += width
    deep, rows = pieces[0].shape[0], pieces[0].shape[1] // kinds
    outs = [((deep * QUAD * rows, width), pieces[0].dtype) for width in widths]
    kernel = functools.partial(place_kernel, deep, windows, kinds)
    return vmem_call(kernel, outs, [spot.at, *pieces], "place_pieces", limit=8)


def low(value):
    return value.astype(jnp.bfloat16)


def by_pair(value):
    lead, kinds, columns = value.shape[:-2], value.shape[-2], value.shape[-1]
    split = value.reshape(lead + (kinds, columns // PAIR, PAIR))
    return jnp.swapaxes(split, -3, -2).reshape(lead + (kinds * columns,))


def by_kind(value, kinds):
    lead, columns = value.shape[:-1], value.shape[-1]
    split = value.reshape(lead + (columns // (kinds * PAIR), kinds, PAIR))
    return jnp.swapaxes(split, -3, -2).reshape(lead + (kinds, columns // kinds))


def on_device(
    inputs,
    qkv_weight,
    qv_bias,
    out_weight,
    out_bias,
    first_gain,
    first_shift,
    up_weight,
    up_bias,
    down_weight,
    down_bias,
    second_gain,
    second_shift,
    item_lengths,
    random_blocks,
    out_grad,
):
    half, width = inputs.shape
    spot = Spot()
    deep = spot.deep
    shard = qkv_weight.shape[0]
    head_width = qkv_weight.shape[2]
    up_width = up_weight.shape[1]
    pair_count = head_width // PAIR

    def position():
        return lax.axis_index("head")

    staged = deep == 4 and shard % 16 == 0
    every = ("deep", "quad")

    def gathered_whole(block):
        return lax.all_gather(block, every, axis=0, tiled=True)

    def scattered(total):
        return lax.psum_scatter(total, every, scatter_dimension=0, tiled=True).astype(jnp.float32)

    def first_quad(block):
        return quad_step(block, deep, False)

    def second_quad(block):
        return quad_step(block, deep, True)

    tokens_other = swap(inputs)
    mid = jnp.concatenate([out_weight, up_weight], axis=1)
    if staged:
        qkv_block = jnp.swapaxes(qkv_weight, 0, 1).reshape(3 * shard, head_width)
        qkv_pieces = deep_pieces(qkv_block, spot)
        mid_pieces = deep_pieces(after(mid, *qkv_pieces), spot)
        qkv_deep = jnp.stack([qkv_block] + qkv_pieces)
        qkv_other, qkv_far = first_quad(qkv_deep), second_quad(qkv_deep)
        qkv_other, qkv_far, *mid_pieces = lax.optimization_barrier(
            (qkv_other, qkv_far, *mid_pieces)
        )
        qkv_across = second_quad(qkv_other)
        (full_qkv,) = place(
            spot, (qkv_deep, qkv_other, qkv_far, qkv_across), [3 * head_width], kinds=3
        )
        full_qkv, *mid_pieces = lax.optimization_barrier((full_qkv, *mid_pieces))
        mid_deep = jnp.stack([mid] + mid_pieces)
        mid_other, mid_far = first_quad(mid_deep), second_quad(mid_deep)
        full_qkv, mid_deep = lax.optimization_barrier((full_qkv, mid_deep))
        down_pieces = deep_pieces(after(down_weight, *mid_pieces), spot)
    else:
        full_qkv = gathered_whole(by_pair(qkv_weight))
        full_mid = gathered_whole(mid)
        full_out, full_up = full_mid[:, :head_width], full_mid[:, head_width:]
        full_down = gathered_whole(down_weight)

    bias = by_pair(jnp.stack([qv_bias[0], jnp.zeros_like(qv_bias[0]), qv_bias[1]]))
    triple = triple_of(inputs, tokens_other, full_qkv, bias)
    attended = attention_forward(item_lengths, random_blocks, triple, position)
    if staged:
        attended, mid_other, mid_far, *down_pieces = lax.optimization_barrier(
            (attended, mid_other, mid_far, *down_pieces)
        )
        mid_across = second_quad(mid_other)
        down_deep = jnp.stack([down_weight] + down_pieces)
        down_other, down_far = first_quad(down_deep), second_quad(down_deep)
        mid_across, down_other = lax.optimization_barrier((mid_across, down_other))
        down_across = second_quad(down_other)
        full_out, full_up = place(
            spot, (mid_deep, mid_other, mid_far, mid_across), [head_width, up_width]
        )

    whole = (half, 2 * half)
    other = swap(rows_product([attended], full_out, whole, jnp.bfloat16))
    proj = rows_product([attended], full_out, (0, half), jnp.float32) + other.astype(jnp.float32)
    normed_one_out, normed_one, inverse_one = norm_forward(
        proj + out_bias + inputs.astype(jnp.float32), first_gain, first_shift
    )
    hidden_own = low(normed_one_out)
    hidden_other = swap(hidden_own)
    active_own, slope_own = up_gelu(hidden_own, full_up, up_bias)
    if staged:
        active_own, hidden_other, down_across = lax.optimization_barrier(
            (active_own, hidden_other, down_across)
        )
    active_other, slope_other = up_gelu(hidden_other, full_up, up_bias)
    if staged:
        active_other, active_own, down_far = lax.optimization_barrier(
            (active_other, active_own, down_far)
        )
        (full_down,) = place(spot, (down_deep, down_other, down_far, down_across), [up_width])
    other = swap(rows_product([active_other], full_down, (0, half), jnp.bfloat16))
    layer_out, grad_res_two, grad_own, sums_two = norm_two(
        item_lengths,
        rows_product([active_own], full_down, (0, half), jnp.float32),
        other,
        normed_one_out,
        out_grad,
        down_bias,
        second_gain,
        second_shift,
        position,
    )
    grad_other = swap(grad_own)
    grad_upper_own, up_sum_own = back_slope(grad_own, full_down, slope_own)
    down_local = outer([grad_own, grad_other], [active_own, active_other])
    if staged:
        near_message, far_message = sum_first_apart(down_local, spot)
        down_far_got = first_quad(far_message)
        grad_other, near_message = lax.optimization_barrier((grad_other, near_message))
        down_got = first_quad(near_message)
    grad_upper_other, up_sum_other = back_slope(grad_other, full_down, slope_other)
    other = swap(rows_product([grad_upper_other], full_up, (0, half), jnp.bfloat16))
    up_local = outer([hidden_own, hidden_other], [grad_upper_own, grad_upper_other])
    grad_res_one, grad_proj_own, sums_one = norm_one_back(
        rows_product([grad_upper_own], full_up, (0, half), jnp.float32), other, grad_res_two, normed_one, inverse_one, first_gain
    )
    if staged:
        grad_proj_own, down_far_got = lax.optimization_barrier((grad_proj_own, down_far_got))
        down_message = sum_second([down_local], spot, down_far_got)
        down_two = second_quad(down_message)
        grad_proj_own, down_message = lax.optimization_barrier((grad_proj_own, down_message))
    grad_proj_other = swap(grad_proj_own)
    shared = jnp.concatenate([sums_one, sums_two], axis=0)
    shared_other = swap(shared)
    grad_attended = project_both(grad_proj_own, grad_proj_other, full_out)
    out_local = outer([grad_proj_own, grad_proj_other], [attended])

    mids = [out_local, up_local]
    split = pair_count - 1
    if staged:
        mid_message = sum_first(mids, spot)
        mid_got = first_quad(mid_message)
        grad_attended, down_got = lax.optimization_barrier((grad_attended, down_got))
        grad_attended, mid_message = lax.optimization_barrier((grad_attended, mid_message))
    grads_a, sums_a = attention_backward(
        item_lengths, random_blocks, triple, grad_attended, range(split), position
    )
    if staged:
        grads_a, mid_got, down_two, grad_attended, shared_other = lax.optimization_barrier(
            (grads_a, mid_got, down_two, grad_attended, shared_other)
        )
        mid_message = sum_second(mids, spot, mid_got)
        mid_two = second_quad(mid_message)
        down_sum, *messages = sum_deep([[down_local]], spot, [down_got], [down_two])
        down_answers = [deep_step(m, deep, k + 1) for k, m in enumerate(messages)]
    local_a = outer([inputs, tokens_other], [grads_a])
    if staged:
        message_a = sum_first([local_a], spot)
        got_a = first_quad(message_a)
        grad_attended, message_a, mid_message, *messages = lax.optimization_barrier(
            (grad_attended, message_a, mid_message, *messages)
        )
    grads_b, sums_b = attention_backward(
        item_lengths, random_blocks, triple, grad_attended, range(split, pair_count), position
    )
    if staged:
        grads_b, got_a, mid_two, *down_answers = lax.optimization_barrier(
            (grads_b, got_a, mid_two, *down_answers)
        )
    local_b = outer([inputs, tokens_other], [grads_b])
    small = small_sums(shared, shared_other, up_sum_own, up_sum_other, [sums_a, sums_b])
    if staged:
        message_b = sum_first([local_b], spot, small)
        got_b = first_quad(message_b)
        message_a = sum_second([local_a], spot, after(got_a, message_b))
        two_a = second_quad(message_a)
        grads_a, grads_b, message_a = lax.optimization_barrier((grads_a, grads_b, message_a))
    product = rows_product([grads_a, grads_b], full_qkv, whole, jnp.bfloat16)
    if staged:
        mid_got, product = lax.optimization_barrier((mid_got, product))
        mid_sum, *messages = sum_deep([mids], spot, [mid_got], [mid_two])
        mid_answers = [deep_step(m, deep, k + 1) for k, m in enumerate(messages)]
        product, *messages = lax.optimization_barrier((product, *messages))
    other = swap(product)
    if staged:
        grads_a, other, got_b, two_a = lax.optimization_barrier((grads_a, other, got_b, two_a))
        message, small = sum_second([local_b], spot, got_b, small)
        two_b = second_quad(message)
        grads_a, message = lax.optimization_barrier((grads_a, message))
    mine = rows_product([grads_a, grads_b], full_qkv, (0, half), jnp.float32)
    input_grad = low(mine + other.astype(jnp.float32) + grad_res_one)
    if staged:
        (grad_down,) = sum_last(down_sum, down_answers, [up_width])
        input_grad, grad_down, two_b = lax.optimization_barrier((input_grad, grad_down, two_b))
        small, qkv_sum, *messages = sum_deep(
            [[local_a], [local_b]], spot, [got_a, got_b], [two_a, two_b], small
        )
        answers = [deep_step(m, deep, k + 1) for k, m in enumerate(messages)]
        grad_out, grad_up = sum_last(mid_sum, mid_answers, [head_width, up_width])
        grad_out, grad_up, *answers = lax.optimization_barrier((grad_out, grad_up, *answers))
        grad_qkv, grad_up_bias, grad_qv_bias, small = sum_last(
            qkv_sum, answers, [3 * head_width], small, up_width
        )
        grad_qkv = jnp.swapaxes(grad_qkv, 0, 1)
        grad_up_bias = grad_up_bias.reshape(up_width)
    else:
        grad_down, grad_up, grad_out = (scattered(v) for v in (down_local, up_local, out_local))
        grad_qkv = by_kind(scattered(jnp.concatenate([local_a, local_b], axis=1)), 3)
        small = lax.psum(small, every)
        part = small.shape[0] // 3
        small = jnp.concatenate([small[n * part : (n + 1) * part] for n in range(3)], axis=1)
        rest = small[:, width : width + head_width]
        grad_up_bias = rest[: up_width // head_width].reshape(up_width)
        grad_qv_bias = rest[up_width // head_width :]
    totals = small[:, :width]
    return (
        layer_out,
        input_grad,
        grad_qkv,
        grad_qv_bias,
        grad_out,
        totals[0],
        totals[1],
        totals[2],
        grad_up,
        grad_up_bias,
        grad_down,
        totals[3],
        totals[4],
        totals[5],
    )


def solution(mesh):
    devices = mesh.devices.reshape(-1, QUAD, mesh.shape["head"])
    fine = Mesh(devices, ("deep", "quad", "head"))
    rows = ("deep", "quad", "head")
    dp = ("deep", "quad")
    in_specs = (
        P(rows, None),
        P(dp, None, "head"),
        P(None, "head"),
        P(dp, "head"),
        P(),
        P(),
        P(),
        P(dp, "head"),
        P("head"),
        P(dp, "head"),
        P(),
        P(),
        P(),
        P(dp, None),
        P(dp, "head", None, None),
        P(rows, None),
    )
    out_specs = (
        P(rows, None),
        P(rows, None),
        P(dp, None, "head"),
        P(None, "head"),
        P(dp, "head"),
        P(),
        P(),
        P(),
        P(dp, "head"),
        P("head"),
        P(dp, "head"),
        P(),
        P(),
        P(),
    )
    return jax.shard_map(
        on_device, mesh=fine, in_specs=in_specs, out_specs=out_specs, check_vma=False
    )
```

```python
import functools

import jax
import jax.numpy as jnp
import numpy as np
from jax import lax
from jax.experimental import pallas as pl
from jax.experimental.pallas import tpu as pltpu
from jax.sharding import Mesh
from jax.sharding import PartitionSpec as P

BLK = 64


norm_eps = 1e-06
negative = -1e30


def norm_forward(values, gain, shift):
    centered = values - jnp.mean(values, axis=-1, keepdims=True)
    inverse = lax.rsqrt(jnp.mean(centered * centered, axis=-1, keepdims=True) + norm_eps)
    normed = centered * inverse
    return (normed * gain + shift, normed, inverse)


def dot_nt(a, b):
    return lax.dot_general(a, b, (((1,), (1,)), ((), ())), preferred_element_type=jnp.float32)


def dot_nn(a, b):
    return lax.dot_general(a, b, (((1,), (0,)), ((), ())), preferred_element_type=jnp.float32)


def dot_tn(a, b):
    return lax.dot_general(a, b, (((0,), (0,)), ((), ())), preferred_element_type=jnp.float32)


PAIR = 2 * BLK


def even_lanes(rows):
    return lax.broadcasted_iota(jnp.int32, (rows, PAIR), 1) < BLK


def stacked(values):
    zero = jnp.zeros_like(values)
    even = even_lanes(BLK)
    return jnp.concatenate([jnp.where(even, values, zero), jnp.where(even, zero, values)], axis=0)


def unstacked(values):
    return jnp.where(even_lanes(BLK), values[:BLK], values[BLK:])


class Layout:
    def __init__(self, len_ref, rb_ref, blocks, position):
        self.len_ref, self.rb_ref, self.blocks = len_ref, rb_ref, blocks
        self.half = blocks // 2
        self.rand = rb_ref.shape[-1]
        self.shift = position * self.half

    def moved(self, index):
        at = index + self.shift
        return jnp.where(at >= self.blocks, at - self.blocks, at)

    def spot(self, index):
        return pl.ds(pl.multiple_of(self.moved(index) * BLK, BLK), BLK)

    def part(self, index):
        return pl.ds(pl.multiple_of(self.moved(index) * BLK, BLK), self.half * BLK)

    def counts(self):
        self.count0 = lax.div(self.len_ref[0, 0], BLK)
        self.count1 = lax.div(self.len_ref[0, 1], BLK)
        self.second = jnp.where(self.count1 > 0, 1, 0)
        self.inner = self.blocks - 2 - 2 * self.second

    def locate(self, i):
        in0 = i < self.count0 - 2
        self.b = b = jnp.where(in0, i + 1, i + 2 + self.second)
        self.live = live = b < self.count0 + self.count1
        self.first = first = jnp.where(in0, 0, jnp.where(live, self.count0, b))
        items = jnp.where(in0, self.count0, jnp.where(live, self.count1, 1))
        rel = b - first
        last = items - 1
        zero, neg = jnp.float32(0.0), jnp.float32(negative)
        self.fixed = [
            first,
            first + last,
            jnp.where(live, b - 1, b),
            jnp.where(live, b + 1, b),
            b,
        ]
        self.low_bias = jnp.where(live & (rel == 1), neg, zero)
        self.high_bias = jnp.where(live & (rel + 1 == last), neg, zero)
        return self

    def ends(self, item):
        first = jnp.where(item == 0, 0, self.count0)
        count = jnp.where(item == 0, self.count0, self.count1)
        return first, first + count - 1, lax.div(count, self.half)

    def chosen(self, head):
        return [
            jnp.where(self.live, self.first + self.rb_ref[0, head, self.b, k], self.b)
            for k in range(self.rand)
        ]


def gathered(ref, layout, column, picked):
    even = even_lanes(BLK)

    def rows(index):
        return ref[layout.spot(index), column : column + PAIR]

    return jnp.concatenate(
        [rows(i) for i in layout.fixed]
        + [jnp.where(even, rows(i), rows(j)) for i, j in zip(*picked)],
        axis=0,
    )


ROWS = 32


def soft_rows(held):
    probs, inverse = [], []
    for row in range(0, held.shape[0], ROWS):
        scores = held[row : row + ROWS, :]
        expo = jnp.exp(scores - jnp.max(scores, axis=1, keepdims=True))
        inverse.append(1.0 / jnp.sum(expo, axis=1, keepdims=True))
        probs.append(expo.astype(jnp.bfloat16))
    return jnp.concatenate(probs, axis=0), jnp.concatenate(inverse, axis=0)


def attn_fwd_kernel(pairs, position, len_ref, rb_ref, tri_ref, out_ref, wide, *held):
    blocks = tri_ref.shape[0] // BLK
    scale = jnp.bfloat16(BLK**-0.5)
    layout = Layout(len_ref, rb_ref, blocks, position())
    layout.counts()

    def query_of(p, b):
        at = layout.spot(b)
        return stacked(tri_ref[at, p * 3 * PAIR : p * 3 * PAIR + PAIR]) * scale

    def put(p, b, mixed):
        at = layout.spot(b)
        out_ref[at, p * PAIR : (p + 1) * PAIR] = unstacked(mixed).astype(jnp.bfloat16)

    def sparse_scores(i, held):
        at = layout.locate(i)
        lane = lax.broadcasted_iota(jnp.int32, (1, PAIR), 1) < BLK
        bias_row = jnp.where(lane, at.low_bias, at.high_bias)
        for n, p in enumerate(pairs):
            picked = [at.chosen(2 * p), at.chosen(2 * p + 1)]
            keys = gathered(tri_ref, at, (3 * p + 1) * PAIR, picked)
            scores = dot_nt(query_of(p, at.b), keys)
            held[n][...] = jnp.concatenate(
                [scores[:, :PAIR], scores[:, PAIR : 2 * PAIR] + bias_row, scores[:, 2 * PAIR :]],
                axis=1,
            )

    def sparse_mix(i, held):
        at = layout.locate(i)
        for n, p in enumerate(pairs):
            picked = [at.chosen(2 * p), at.chosen(2 * p + 1)]
            probs, inverse = soft_rows(held[n])
            values = gathered(tri_ref, at, (3 * p + 2) * PAIR, picked)
            put(p, at.b, dot_nn(probs, values) * inverse)

    held_a, held_b = held[: len(pairs)], held[len(pairs) :]
    sparse_scores(0, held_a)

    def two(j, carry):
        sparse_scores(2 * j + 1, held_b)
        sparse_mix(2 * j, held_a)
        sparse_scores(jnp.minimum(2 * j + 2, layout.inner - 1), held_a)
        sparse_mix(2 * j + 1, held_b)
        return carry

    lax.fori_loop(0, lax.div(layout.inner, 2), two, 0)

    def dense(item, carry):
        first, last, chunks = layout.ends(item)
        queries = [
            jnp.concatenate([query_of(p, first), query_of(p, last)], axis=0) for p in pairs
        ]

        def dense_of(spans):
            for query, p in zip(queries, pairs):
                span = layout.half * BLK
                for c, at in enumerate(spans):
                    keys = tri_ref[at, (3 * p + 1) * PAIR : (3 * p + 2) * PAIR]
                    wide[:, c * span : (c + 1) * span] = dot_nt(query, keys)
                probs, inverse = soft_rows(wide.at[:, : len(spans) * span])
                mixed = sum(
                    dot_nn(
                        probs[:, c * span : (c + 1) * span],
                        tri_ref[at, (3 * p + 2) * PAIR : (3 * p + 3) * PAIR],
                    )
                    for c, at in enumerate(spans)
                ) * inverse
                put(p, first, mixed[:PAIR])
                put(p, last, mixed[PAIR:])

        @pl.when(chunks == 1)
        def short():
            dense_of([layout.part(first)])

        @pl.when(chunks == 2)
        def long():
            dense_of([layout.part(first), layout.part(first + layout.half)])

        return carry

    lax.fori_loop(0, 1 + layout.second, dense, 0)


def grad_rows(held_scores, held_grads, probs_ref, grads_ref):
    for row in range(0, held_scores.shape[0], ROWS):
        at = slice(row, row + ROWS)
        scores = held_scores[at, :]
        grad_probs = held_grads[at, :]
        expo = jnp.exp(scores - jnp.max(scores, axis=1, keepdims=True))
        probs = expo * (1.0 / jnp.sum(expo, axis=1, keepdims=True))
        delta = jnp.sum(probs * grad_probs, axis=1, keepdims=True)
        probs_ref[at, :] = probs.astype(jnp.bfloat16)
        grads_ref[at, :] = (probs * (grad_probs - delta)).astype(jnp.bfloat16)


def attn_bwd_kernel(
    pairs, position, len_ref, rb_ref, tri_ref, grad_ref, out_ref, sum_ref, *scratch
):
    blocks = tri_ref.shape[0] // BLK
    scale = jnp.bfloat16(BLK**-0.5)
    back = BLK**-0.5
    layout = Layout(len_ref, rb_ref, blocks, position())
    layout.counts()
    count = len(pairs)
    key_acc, value_acc = scratch[:count], scratch[count : 2 * count]
    held_a, held_b, done = (scratch[n * count : (n + 2) * count] for n in (2, 4, 6))
    wide = scratch[8 * count :]

    def clear(r, carry):
        at = pl.ds(pl.multiple_of(r * BLK, BLK), BLK)
        for acc in scratch[: 2 * count]:
            acc[at, :] = jnp.zeros((BLK, PAIR), jnp.float32)
        return carry

    lax.fori_loop(0, blocks, clear, 0)

    def query_of(p, b):
        at = layout.spot(b)
        return stacked(tri_ref[at, p * 3 * PAIR : p * 3 * PAIR + PAIR]) * scale

    def grad_of(p, b):
        at = layout.spot(b)
        return stacked(grad_ref[at, p * PAIR : (p + 1) * PAIR])

    def put(i, b, grad_query):
        out_ref[layout.spot(b), i * 3 * PAIR : i * 3 * PAIR + PAIR] = unstacked(
            grad_query * back
        ).astype(jnp.bfloat16)

    def sparse_scores(n, held):
        at = layout.locate(n)
        lane = lax.broadcasted_iota(jnp.int32, (1, PAIR), 1) < BLK
        bias_row = jnp.where(lane, at.low_bias, at.high_bias)
        for i, p in enumerate(pairs):
            picked = [at.chosen(2 * p), at.chosen(2 * p + 1)]
            keys = gathered(tri_ref, at, (3 * p + 1) * PAIR, picked)
            values = gathered(tri_ref, at, (3 * p + 2) * PAIR, picked)
            scores = dot_nt(query_of(p, at.b), keys)
            held[2 * i][...] = jnp.concatenate(
                [scores[:, :PAIR], scores[:, PAIR : 2 * PAIR] + bias_row, scores[:, 2 * PAIR :]],
                axis=1,
            )
            held[2 * i + 1][...] = dot_nt(grad_of(p, at.b), values)

    def sparse_grads(n, held):
        at = layout.locate(n)
        even = even_lanes(BLK)
        for i, p in enumerate(pairs):
            grad_rows(held[2 * i], held[2 * i + 1], done[2 * i], done[2 * i + 1])
            picked = [at.chosen(2 * p), at.chosen(2 * p + 1)]
            spots = [at.spot(index) for index in at.fixed]
            spots += [(at.spot(one), at.spot(two)) for one, two in zip(*picked)]
            keys = gathered(tri_ref, at, (3 * p + 1) * PAIR, picked)
            put(i, at.b, dot_nn(done[2 * i + 1][...], keys))
            for acc, update in (
                (key_acc[i], dot_tn(done[2 * i + 1][...], query_of(p, at.b))),
                (value_acc[i], dot_tn(done[2 * i][...], grad_of(p, at.b))),
            ):
                for j, spot in enumerate(spots):
                    piece = update[j * BLK : (j + 1) * BLK]
                    if j < len(at.fixed):
                        acc[spot, :] += piece
                    else:
                        zero = jnp.zeros_like(piece)
                        acc[spot[0], :] += jnp.where(even, piece, zero)
                        acc[spot[1], :] += jnp.where(even, zero, piece)

    sparse_scores(0, held_a)

    def two(j, carry):
        sparse_scores(2 * j + 1, held_b)
        sparse_grads(2 * j, held_a)
        sparse_scores(jnp.minimum(2 * j + 2, layout.inner - 1), held_a)
        sparse_grads(2 * j + 1, held_b)
        return carry

    lax.fori_loop(0, lax.div(layout.inner, 2), two, 0)

    wide_scores, wide_grads, wide_probs, wide_out = wide

    def dense(item, carry):
        first, last, chunks = layout.ends(item)

        def dense_of(spans):
            span = layout.half * BLK
            cover = len(spans) * span
            def end(n, carry):
                b = jnp.where(n == 0, first, last)
                for i, p in enumerate(pairs):
                    query, grad = query_of(p, b), grad_of(p, b)
                    for c, at in enumerate(spans):
                        cut = slice(c * span, (c + 1) * span)
                        keys = tri_ref[at, (3 * p + 1) * PAIR : (3 * p + 2) * PAIR]
                        values = tri_ref[at, (3 * p + 2) * PAIR : (3 * p + 3) * PAIR]
                        wide_scores[:, cut] = dot_nt(query, keys)
                        wide_grads[:, cut] = dot_nt(grad, values)
                    grad_rows(*(ref.at[:, :cover] for ref in wide))
                    total = jnp.zeros((PAIR, PAIR), jnp.float32)
                    for c, at in enumerate(spans):
                        cut = slice(c * span, (c + 1) * span)
                        keys = tri_ref[at, (3 * p + 1) * PAIR : (3 * p + 2) * PAIR]
                        total += dot_nn(wide_out[:, cut], keys)
                        key_acc[i][at, :] += dot_tn(wide_out[:, cut], query)
                        value_acc[i][at, :] += dot_tn(wide_probs[:, cut], grad)
                    put(i, b, total)
                return carry

            lax.fori_loop(0, 2, end, 0)

        @pl.when(chunks == 1)
        def short():
            dense_of([layout.part(first)])

        @pl.when(chunks == 2)
        def long():
            dense_of([layout.part(first), layout.part(first + layout.half)])

        return carry

    lax.fori_loop(0, 1 + layout.second, dense, 0)

    sum_ref[...] = jnp.zeros_like(sum_ref)

    def finish(r, carry):
        at = pl.ds(pl.multiple_of(r * BLK, BLK), BLK)
        new = []
        for i in range(count):
            column = i * 3 * PAIR
            query_sum, value_sum = carry[i]
            out_ref[at, column + PAIR : column + 2 * PAIR] = key_acc[i][at, :].astype(jnp.bfloat16)
            value = value_acc[i][at, :].astype(jnp.bfloat16)
            out_ref[at, column + 2 * PAIR : column + 3 * PAIR] = value
            query = out_ref[at, column : column + PAIR].astype(jnp.float32)
            new.append(
                tuple(
                    total + jnp.sum(part.reshape(-1, 8, PAIR), axis=0)
                    for total, part in (
                        (query_sum, query),
                        (value_sum, value.astype(jnp.float32)),
                    )
                )
            )
        return tuple(new)

    zero = jnp.zeros((8, PAIR), jnp.float32)
    sums = lax.fori_loop(0, blocks, finish, tuple((zero, zero) for _ in pairs))
    for i, totals in enumerate(sums):
        for kind, total in enumerate(totals):
            sum_ref[kind : kind + 1, i * PAIR : (i + 1) * PAIR] = jnp.sum(
                total, axis=0, keepdims=True
            )


vmem = pl.BlockSpec(memory_space=pltpu.VMEM)
smem = pl.BlockSpec(memory_space=pltpu.SMEM)
def attention_forward(lengths, randoms, triple, position):
    pairs = randoms.shape[1] // 2
    rows = triple.shape[0]
    area = rows * rows // 3 * 2 * pairs
    return pl.pallas_call(
        functools.partial(attn_fwd_kernel, range(pairs), position),
        out_shape=jax.ShapeDtypeStruct((rows, pairs * PAIR), jnp.bfloat16),
        in_specs=[smem, smem, vmem],
        out_specs=vmem,
        name="attend_forward",
        scratch_shapes=[pltpu.VMEM((2 * PAIR, rows), jnp.float32)]
        + [pltpu.VMEM((PAIR, 8 * BLK), jnp.float32)] * (2 * pairs),
        cost_estimate=pl.CostEstimate(
            flops=16 * area * PAIR, transcendentals=area, bytes_accessed=rows * pairs * PAIR * 8
        ),
        compiler_params=pltpu.CompilerParams(vmem_limit_bytes=8 << 20),
    )(lengths, randoms, triple)


def attention_backward(lengths, randoms, triple, grad, pairs, position):
    rows = triple.shape[0]
    count = len(pairs)
    area = rows * rows // 3 * 2 * count
    return pl.pallas_call(
        functools.partial(attn_bwd_kernel, pairs, position),
        out_shape=(
            jax.ShapeDtypeStruct((rows, count * 3 * PAIR), jnp.bfloat16),
            jax.ShapeDtypeStruct((8, count * PAIR), jnp.float32),
        ),
        in_specs=[smem, smem, vmem, vmem],
        out_specs=(vmem, vmem),
        name="attend_backward",
        scratch_shapes=[pltpu.VMEM((rows, PAIR), jnp.float32)] * (2 * count)
        + [pltpu.VMEM((PAIR, 8 * BLK), jnp.float32)] * (4 * count)
        + [pltpu.VMEM((PAIR, 8 * BLK), jnp.bfloat16)] * (2 * count)
        + [pltpu.VMEM((PAIR, rows), kind) for kind in (jnp.float32,) * 2 + (jnp.bfloat16,) * 2],
        cost_estimate=pl.CostEstimate(
            flops=40 * area * PAIR, transcendentals=area, bytes_accessed=rows * count * PAIR * 20
        ),
        compiler_params=pltpu.CompilerParams(vmem_limit_bytes=20 << 20),
    )(lengths, randoms, triple, grad)


TILE = 256
EPS = 1e-06


def tile_at(n):
    return pl.ds(pl.multiple_of(n * TILE, TILE), TILE)


def up_kernel(rows_ref, weight_ref, bias_ref, active_ref, slope_ref, held_a, held_b):
    tiles = weight_ref.shape[1] // TILE
    root = (2.0 / np.pi) ** 0.5
    cube = 0.044715 * root

    def product(n, held):
        held[...] = dot_nn(rows_ref[...], weight_ref[:, tile_at(n)])

    def gelu(n, held):
        bias = bias_ref[:, tile_at(n)]
        for row in range(0, held.shape[0], ROWS):
            at = slice(row, row + ROWS)
            upper = (held[at, :] + bias).astype(jnp.bfloat16).astype(jnp.float32)
            square = upper * upper
            half = 0.5 + 0.5 * jnp.tanh(upper * (square * cube + root))
            active = upper * half
            active_ref[at, tile_at(n)] = active.astype(jnp.bfloat16)
            bend = (1.0 - half) * (square * (6.0 * cube) + 2.0 * root)
            slope_ref[at, tile_at(n)] = (half + active * bend).astype(jnp.bfloat16)

    product(0, held_a)

    def two(j, carry):
        product(2 * j + 1, held_b)
        gelu(2 * j, held_a)
        product(jnp.minimum(2 * j + 2, tiles - 1), held_a)
        gelu(2 * j + 1, held_b)
        return carry

    lax.fori_loop(0, tiles // 2, two, 0)


def up_gelu(rows, weight, bias):
    count, width = rows.shape[0], weight.shape[1]
    shape = jax.ShapeDtypeStruct((count, width), jnp.bfloat16)
    return pl.pallas_call(
        up_kernel,
        out_shape=(shape, shape),
        in_specs=[vmem] * 3,
        out_specs=(vmem, vmem),
        name="up_gelu",
        scratch_shapes=[pltpu.VMEM((count, TILE), jnp.float32)] * 2,
        cost_estimate=pl.CostEstimate(
            flops=2 * count * width * rows.shape[1],
            transcendentals=count * width,
            bytes_accessed=2 * (rows.size + weight.size + 2 * count * width),
        ),
        compiler_params=pltpu.CompilerParams(vmem_limit_bytes=12 << 20),
    )(rows, weight, bias.reshape(1, -1))


def back_kernel(grad_ref, weight_ref, slope_ref, out_ref, sum_ref):
    def step(n, carry):
        grad_active = dot_nn(grad_ref[...], weight_ref[:, tile_at(n)])
        total = jnp.zeros((8, TILE), jnp.float32)
        for row in range(0, grad_active.shape[0], ROWS):
            at = slice(row, row + ROWS)
            grad = grad_active[at] * slope_ref[at, tile_at(n)].astype(jnp.float32)
            grad = grad.astype(jnp.bfloat16)
            out_ref[at, tile_at(n)] = grad
            total += jnp.sum(grad.astype(jnp.float32).reshape(-1, 8, TILE), axis=0)
        sum_ref[:, tile_at(n)] = total
        return carry

    lax.fori_loop(0, weight_ref.shape[1] // TILE, step, 0)


def back_slope(grad, weight, slope):
    count, width = slope.shape
    return pl.pallas_call(
        back_kernel,
        out_shape=(
            jax.ShapeDtypeStruct((count, width), jnp.bfloat16),
            jax.ShapeDtypeStruct((8, width), jnp.float32),
        ),
        in_specs=[vmem] * 3,
        out_specs=(vmem, vmem),
        name="back_slope",
        cost_estimate=pl.CostEstimate(
            flops=2 * count * width * grad.shape[1],
            transcendentals=0,
            bytes_accessed=2 * (grad.size + weight.size + 2 * count * width),
        ),
        compiler_params=pltpu.CompilerParams(vmem_limit_bytes=12 << 20),
    )(grad, weight, slope)


def outer_kernel(count, *refs):
    lefts, rights, out_ref = refs[:count], refs[count:-1], refs[-1]
    if len(rights) < count:
        rows = lefts[0].shape[0]
        rights = [rights[0].at[n * rows : (n + 1) * rows] for n in range(count)]

    def step(at):
        total = sum(dot_tn(a[...], b[:, at]) for a, b in zip(lefts, rights))
        out_ref[:, at] = total.astype(jnp.bfloat16)

    width = out_ref.shape[1]
    if width % TILE:
        step(slice(0, width))
    else:

        def body(n, carry):
            step(tile_at(n))
            return carry

        lax.fori_loop(0, width // TILE, body, 0)


def outer(lefts, rights):
    shape = (lefts[0].shape[1], rights[0].shape[1])
    inner = sum(a.shape[0] for a in lefts)
    return pl.pallas_call(
        functools.partial(outer_kernel, len(lefts)),
        out_shape=jax.ShapeDtypeStruct(shape, jnp.bfloat16),
        in_specs=[vmem] * (len(lefts) + len(rights)),
        out_specs=vmem,
        name="outer",
        cost_estimate=pl.CostEstimate(
            flops=2 * inner * shape[0] * shape[1],
            transcendentals=0,
            bytes_accessed=2 * inner * sum(shape),
        ),
        compiler_params=pltpu.CompilerParams(vmem_limit_bytes=12 << 20),
    )(*lefts, *rights)


def project_kernel(own_ref, other_ref, weight_ref, out_ref):
    rows = own_ref.shape[0]
    for n, ref in enumerate((own_ref, other_ref)):
        product = dot_nn(ref[...], weight_ref[...])
        out_ref[n * rows : (n + 1) * rows, :] = product.astype(jnp.bfloat16)


def project_both(own, other, weight):
    return pl.pallas_call(
        project_kernel,
        out_shape=jax.ShapeDtypeStruct((2 * own.shape[0], weight.shape[1]), jnp.bfloat16),
        in_specs=[vmem] * 3,
        out_specs=vmem,
        name="project_both",
        compiler_params=pltpu.CompilerParams(vmem_limit_bytes=12 << 20),
    )(own, other, weight)


GROUP = 16
SPLIT = 12


def groups_at(r):
    return [
        (r * SPLIT + n, pl.ds(pl.multiple_of((r * SPLIT + n) * GROUP, GROUP), GROUP))
        for n in range(SPLIT)
    ]


def row_mean(values):
    return jnp.sum(values, axis=1, keepdims=True) * (1.0 / values.shape[1])


def folded(values):
    return jnp.sum(values.reshape(-1, 8, values.shape[1]), axis=0)


def norm_two_kernel(position, len_ref, down_ref, other_ref, resid_ref, cot_ref, vec_ref, out_ref, grad_ref, low_ref, sum_ref):
    count, width = down_ref.shape
    live_rows = len_ref[0, 0] + len_ref[0, 1] - position() * count
    bias, gain, shift = (vec_ref[n : n + 1, :] for n in range(3))

    def group(r, at, sums):
        row = r * GROUP + lax.broadcasted_iota(jnp.int32, (GROUP, 1), 0)
        live = jnp.where(row < live_rows, 1.0, 0.0)
        values = down_ref[at, :] + other_ref[at, :].astype(jnp.float32) + bias + resid_ref[at, :]
        centered = values - row_mean(values)
        inverse = lax.rsqrt(row_mean(centered * centered) + EPS)
        normed = centered * inverse
        out_ref[at, :] = ((normed * gain + shift) * live).astype(jnp.bfloat16)
        cot = cot_ref[at, :].astype(jnp.float32) * live
        scaled = cot * gain
        grad = inverse * (scaled - row_mean(scaled) - normed * row_mean(scaled * normed))
        grad_ref[at, :] = grad
        low_ref[at, :] = grad.astype(jnp.bfloat16)
        return tuple(s + folded(v) for s, v in zip(sums, (grad, cot * normed, cot)))

    def step(r, sums):
        for n, at in groups_at(r):
            sums = group(n, at, sums)
        return sums

    zero = jnp.zeros((8, width), jnp.float32)
    sums = lax.fori_loop(0, count // (GROUP * SPLIT), step, (zero,) * 3)
    for n, total in enumerate(sums):
        sum_ref[n : n + 1, :] = jnp.sum(total, axis=0, keepdims=True)
    sum_ref[3:8, :] = jnp.zeros((5, width), jnp.float32)


def norm_two(lengths, down, other, resid, cot, bias, gain, shift, position):
    shape = down.shape
    row = jax.ShapeDtypeStruct((8, shape[1]), jnp.float32)
    return pl.pallas_call(
        functools.partial(norm_two_kernel, position),
        out_shape=(
            jax.ShapeDtypeStruct(shape, jnp.bfloat16),
            jax.ShapeDtypeStruct(shape, jnp.float32),
            jax.ShapeDtypeStruct(shape, jnp.bfloat16),
            row,
        ),
        in_specs=[smem] + [vmem] * 5,
        out_specs=(vmem,) * 4,
        name="norm_two",
        cost_estimate=pl.CostEstimate(
            flops=40 * down.size, transcendentals=0, bytes_accessed=20 * down.size
        ),
        compiler_params=pltpu.CompilerParams(vmem_limit_bytes=12 << 20),
    )(lengths, down, other, resid, cot, jnp.stack([bias, gain, shift]))


def norm_one_kernel(own_ref, other_ref, grad_ref, normed_ref, inverse_ref, gain_ref, out_ref, low_ref, sum_ref):
    count, width = own_ref.shape
    gain = gain_ref[...]

    def group(r, at, sums):
        grad = own_ref[at, :] + other_ref[at, :].astype(jnp.float32) + grad_ref[at, :]
        normed = normed_ref[at, :]
        scaled = grad * gain
        result = inverse_ref[at, :] * (
            scaled - row_mean(scaled) - normed * row_mean(scaled * normed)
        )
        out_ref[at, :] = result
        low_ref[at, :] = result.astype(jnp.bfloat16)
        return tuple(s + folded(v) for s, v in zip(sums, (result, grad * normed, grad)))

    def step(r, sums):
        for n, at in groups_at(r):
            sums = group(n, at, sums)
        return sums

    zero = jnp.zeros((8, width), jnp.float32)
    sums = lax.fori_loop(0, count // (GROUP * SPLIT), step, (zero,) * 3)
    for n, total in enumerate(sums):
        sum_ref[n : n + 1, :] = jnp.sum(total, axis=0, keepdims=True)
    sum_ref[3:8, :] = jnp.zeros((5, width), jnp.float32)


def norm_one_back(own, other, grad, normed, inverse, gain):
    shape = own.shape
    return pl.pallas_call(
        norm_one_kernel,
        out_shape=(
            jax.ShapeDtypeStruct(shape, jnp.float32),
            jax.ShapeDtypeStruct(shape, jnp.bfloat16),
            jax.ShapeDtypeStruct((8, shape[1]), jnp.float32),
        ),
        in_specs=[vmem] * 6,
        out_specs=(vmem,) * 3,
        name="norm_one_back",
        cost_estimate=pl.CostEstimate(
            flops=20 * own.size, transcendentals=0, bytes_accessed=20 * own.size
        ),
        compiler_params=pltpu.CompilerParams(vmem_limit_bytes=12 << 20),
    )(own, other, grad, normed, inverse, gain.reshape(1, -1))


def pack_rows(ref, at, small):
    rows = small.shape[0]
    high = small.astype(jnp.bfloat16)
    ref[at : at + rows, :] = high
    ref[at + rows : at + 2 * rows, :] = (small - high.astype(jnp.float32)).astype(jnp.bfloat16)


def unpack_rows(ref, at, rows):
    high = ref[at : at + rows, :].astype(jnp.float32)
    return high + ref[at + rows : at + 2 * rows, :].astype(jnp.float32)


def slab_at(at_ref, place, z, rows):
    return pl.ds(pl.multiple_of((z * QUAD + at_ref[place]) * rows, rows), rows)


def columns_of(totals):
    cuts, low = [], 0
    for total in totals:
        cuts.append(slice(low, low + total.shape[1]))
        low += total.shape[1]
    return cuts


def sum_first_kernel(count, deep, apart, at_ref, *refs):
    totals, rest = refs[:count], refs[count:]
    rows = totals[0].shape[0] // (deep * QUAD)
    halves = [(1, 0), (3, deep * rows)]
    if apart:
        halves = [(1, 0), (3, 0)]
    for part, (place, low) in enumerate(halves):
        out_ref = rest[part - 2] if apart else rest[-1]
        for z in range(deep):
            row = low + z * rows
            for total, cut in zip(totals, columns_of(totals)):
                out_ref[row : row + rows, cut] = total[slab_at(at_ref, place, z, rows), :]
    if len(rest) > 1 and not apart:
        pack_rows(rest[-1], 2 * deep * rows, rest[0][...])


def sum_second_kernel(count, deep, at_ref, *refs):
    totals, got_ref = refs[:count], refs[count]
    rows = totals[0].shape[0] // (deep * QUAD)
    if len(refs) > count + 2:
        small_ref, out_ref, new_ref = refs[count + 1 :]
        small = small_ref[...] + unpack_rows(got_ref, 2 * deep * rows, small_ref.shape[0])
        new_ref[...] = small
        pack_rows(out_ref, deep * rows, small)
    else:
        out_ref = refs[-1]
    for z in range(deep):
        for total, cut in zip(totals, columns_of(totals)):
            far = total[slab_at(at_ref, 2, z, rows), :].astype(jnp.float32)
            row = z * rows + (deep * rows if got_ref.shape[0] >= 2 * deep * rows else 0)
            far = far + got_ref[row : row + rows, cut].astype(jnp.float32)
            out_ref[z * rows : (z + 1) * rows, cut] = far.astype(jnp.bfloat16)


def sum_deep_kernel(groups, deep, small_rows, at_ref, *refs):
    count = sum(groups)
    totals, refs = refs[:count], refs[count:]
    gots, twos, refs = refs[: len(groups)], refs[len(groups) : 2 * len(groups)], refs[2 * len(groups) :]
    rows = totals[0].shape[0] // (deep * QUAD)
    small = None
    if small_rows:
        small_ref, new_ref, refs = refs[0], refs[1], refs[2:]
        small = small_ref[...] + unpack_rows(twos[-1], deep * rows, small_rows)
        part = new_ref.shape[0]
        cuts = [small[n * part : (n + 1) * part] for n in range(small_rows // part)]
        small = jnp.concatenate(cuts, axis=1)
        new_ref[...] = small
    out_cuts = columns_of(totals)
    for k in range(deep):
        z = at_ref[QUAD] ^ k
        near = pl.ds(pl.multiple_of(z * rows, rows), rows)
        n = 0
        for group, got_ref, two_ref in zip(groups, gots, twos):
            members = totals[n : n + group]
            for total, cut, out_cut in zip(members, columns_of(members), out_cuts[n : n + group]):
                value = (
                    total[slab_at(at_ref, 0, z, rows), :].astype(jnp.float32)
                    + got_ref[near, cut].astype(jnp.float32)
                    + two_ref[near, cut].astype(jnp.float32)
                )
                refs[k][:rows, out_cut] = value.astype(refs[k].dtype)
            n += group
        if k and small is not None:
            pack_rows(refs[k], rows, small)


def sum_last_kernel(count, small_rows, *refs):
    own_ref, answers = refs[0], refs[1 : 1 + count]
    rows = own_ref.shape[0]
    own = own_ref[...]
    for answer in answers:
        own = own + answer[:rows, :].astype(jnp.float32)
    outs = refs[1 + count :]
    if small_rows:
        small_ref, new_ref, outs = outs[0], outs[-1], outs[1:-1]
        small = small_ref[...]
        for answer in answers:
            small = small + unpack_rows(answer, rows, small_rows)
        new_ref[...] = small
    if len(outs[0].shape) == 3:
        kinds = outs[0].shape[0]
        for n in range(own.shape[1] // PAIR):
            pair, kind = n // kinds, n % kinds
            cut = slice(pair * PAIR, (pair + 1) * PAIR)
            outs[0][kind, :, cut] = own[:, n * PAIR : (n + 1) * PAIR]
        up_ref, qv_ref = outs[1:]
        wide = qv_ref.shape[1]
        rest = small[:, -wide:]
        ups = up_ref.shape[1] // wide
        for n in range(ups):
            up_ref[:, n * wide : (n + 1) * wide] = rest[n : n + 1]
        qv_ref[...] = rest[ups : ups + 2]
        return
    for out_ref, cut in zip(outs, columns_of(outs)):
        out_ref[...] = own[:, cut]


def vmem_call(kernel, outs, operands, name, scalars=1, limit=12):
    outs = [jax.ShapeDtypeStruct(shape, dtype) for shape, dtype in outs]
    return pl.pallas_call(
        kernel,
        out_shape=outs,
        in_specs=[smem] * scalars + [vmem] * (len(operands) - scalars),
        out_specs=[vmem] * len(outs),
        name=name,
        compiler_params=pltpu.CompilerParams(vmem_limit_bytes=limit << 20),
    )(*operands)


def sum_first_apart(total, spot):
    shape = (total.shape[0] // QUAD, total.shape[1])
    kernel = functools.partial(sum_first_kernel, 1, spot.deep, True)
    return vmem_call(kernel, [(shape, jnp.bfloat16)] * 2, [spot.at, total], "sum_first")


def sum_first(totals, spot, small=None):
    span = totals[0].shape[0] // QUAD
    extra = 0 if small is None else 2 * small.shape[0]
    shape = (2 * span + extra, sum(t.shape[1] for t in totals))
    operands = [spot.at, *totals] + ([] if small is None else [small])
    kernel = functools.partial(sum_first_kernel, len(totals), spot.deep, False)
    return vmem_call(kernel, [(shape, jnp.bfloat16)], operands, "sum_first")[0]


def sum_second(totals, spot, got, small=None):
    span = totals[0].shape[0] // QUAD
    kernel = functools.partial(sum_second_kernel, len(totals), spot.deep)
    operands = [spot.at, *totals, got]
    if small is None:
        outs = [((span, got.shape[1]), jnp.bfloat16)]
        return vmem_call(kernel, outs, operands, "sum_second")[0]
    outs = [((span + 2 * small.shape[0], got.shape[1]), jnp.bfloat16), (small.shape, jnp.float32)]
    return vmem_call(kernel, outs, operands + [small], "sum_second")


def sum_deep(groups, spot, gots, twos, small=None):
    totals = [total for group in groups for total in group]
    rows = totals[0].shape[0] // (QUAD * spot.deep)
    columns = sum(t.shape[1] for t in totals)
    small_rows = 0 if small is None else small.shape[0]
    kernel = functools.partial(
        sum_deep_kernel, [len(group) for group in groups], spot.deep, small_rows
    )
    operands = [spot.at, *totals, *gots, *twos] + ([] if small is None else [small])
    outs, extra = [], 0
    if small is not None:
        part = small_rows // 3
        outs, extra = [((part, columns), jnp.float32)], 2 * part
    outs += [((rows, columns), jnp.float32)]
    outs += [((rows + extra, columns), jnp.bfloat16)] * (spot.deep - 1)
    return vmem_call(kernel, outs, operands, "sum_deep")


def sum_last(own, answers, widths, small=None, up_width=0):
    kernel = functools.partial(
        sum_last_kernel, len(answers), 0 if small is None else small.shape[0]
    )
    operands = [own, *answers] + ([] if small is None else [small])
    outs = [((own.shape[0], w), jnp.float32) for w in widths]
    if small is not None:
        width = widths[0] // 3
        outs = [((3, own.shape[0], width), jnp.float32)]
        outs += [((1, up_width), jnp.float32), ((2, width), jnp.float32)]
    outs += [] if small is None else [(small.shape, jnp.float32)]
    return vmem_call(kernel, outs, operands, "sum_last", scalars=0)


def small_kernel(own_ref, swapped_ref, up_one_ref, up_two_ref, *refs):
    out_ref = refs[-1]
    columns = out_ref.shape[1]
    both = own_ref[...] + swapped_ref[...]
    rows = [both[0:3], both[8:11]]
    row = 0
    for low in range(0, both.shape[1], columns):
        for part in rows:
            out_ref[row : row + 3, :] = part[:, low : low + columns]
            row += 3
    up = jnp.sum(up_one_ref[...] + up_two_ref[...], axis=0, keepdims=True)
    for low in range(0, up.shape[1], columns):
        out_ref[row : row + 1, :] = up[:, low : low + columns]
        row += 1
    low = 0
    for ref in refs[:-1]:
        out_ref[row : row + 2, low : low + ref.shape[1]] = ref[0:2, :]
        low += ref.shape[1]


def small_sums(own, swapped, up_one, up_two, sums):
    columns = sum(s.shape[1] for s in sums)
    rows = 6 * own.shape[1] // columns + up_one.shape[1] // columns + 2
    return vmem_call(
        small_kernel,
        [((rows, columns), jnp.float32)],
        [own, swapped, up_one, up_two, *sums],
        "small_sums",
        scalars=0,
    )[0]


def rows_kernel(window, cuts, *refs):
    lefts, weight_ref, out_ref = refs[:-2], refs[-2], refs[-1]
    rows = slice(*window)

    def step(n, carry):
        total = sum(
            dot_nt(left[rows, :], weight_ref[tile_at(n), cut]) for left, cut in zip(lefts, cuts)
        )
        out_ref[:, tile_at(n)] = total.astype(out_ref.dtype)
        return carry

    lax.fori_loop(0, out_ref.shape[1] // TILE, step, 0)


def rows_product(lefts, weight, window, dtype):
    shape = (window[1] - window[0], weight.shape[0])
    return pl.pallas_call(
        functools.partial(rows_kernel, window, columns_of(lefts)),
        out_shape=jax.ShapeDtypeStruct(shape, dtype),
        in_specs=[vmem] * (len(lefts) + 1),
        out_specs=vmem,
        name="rows_product",
        cost_estimate=pl.CostEstimate(
            flops=2 * shape[0] * weight.size,
            transcendentals=0,
            bytes_accessed=2 * (shape[0] * sum(weight.shape) + weight.size),
        ),
        compiler_params=pltpu.CompilerParams(vmem_limit_bytes=12 << 20),
    )(*lefts, weight)


def triple_kernel(own_ref, other_ref, weight_ref, bias_ref, out_ref):
    rows = own_ref.shape[0]
    span = 3 * PAIR

    def step(n, carry):
        at = pl.ds(pl.multiple_of(n * span, span), span)
        for k, ref in enumerate((own_ref, other_ref)):
            product = dot_nn(ref[...], weight_ref[:, at]) + bias_ref[:, at]
            out_ref[k * rows : (k + 1) * rows, at] = product.astype(jnp.bfloat16)
        return carry

    lax.fori_loop(0, out_ref.shape[1] // span, step, 0)


def triple_of(own, other, weight, bias):
    shape = (2 * own.shape[0], weight.shape[1])
    return pl.pallas_call(
        triple_kernel,
        out_shape=jax.ShapeDtypeStruct(shape, jnp.bfloat16),
        in_specs=[vmem] * 4,
        out_specs=vmem,
        name="triple",
        cost_estimate=pl.CostEstimate(
            flops=2 * shape[0] * weight.size,
            transcendentals=0,
            bytes_accessed=2 * (shape[0] * sum(weight.shape) + weight.size),
        ),
        compiler_params=pltpu.CompilerParams(vmem_limit_bytes=12 << 20),
    )(own, other, weight, bias.reshape(1, -1))


QUAD = 4


def group_permute(value, deep, target):
    pairs = []
    for z in range(deep):
        for q in range(QUAD):
            for h in range(2):
                to_z, to_q = target(z, q, h)
                pairs.append(((z * QUAD + q) * 2 + h, (to_z * QUAD + to_q) * 2 + h))
    return lax.ppermute(value, ("deep", "quad", "head"), pairs)


def deep_step(value, deep, bit):
    return group_permute(value, deep, lambda z, q, h: (z ^ bit, q))


def quad_step(value, deep, second):
    return group_permute(value, deep, lambda z, q, h: (z, q ^ ((2 >> h) if second else (1 << h))))


def swap(value):
    return lax.ppermute(value, "head", [(0, 1), (1, 0)])


def after(value, *others):
    return lax.optimization_barrier((value,) + others)[0]


class Spot:
    def __init__(self):
        self.z, self.q, self.h = (lax.axis_index(a) for a in ("deep", "quad", "head"))
        self.deep = lax.axis_size("deep")
        one, two = 1 << self.h, 2 >> self.h
        self.places = [self.q, self.q ^ one, self.q ^ two, self.q ^ 3]
        self.at = jnp.stack(self.places + [self.z]).astype(jnp.int32)


def deep_pieces(value, spot):
    return [deep_step(value, spot.deep, k) for k in range(1, spot.deep)]


def place_kernel(deep, windows, kinds, at_ref, *refs):
    pieces, outs = refs[:QUAD], refs[QUAD:]
    rows = pieces[0].shape[1] // kinds
    for k in range(deep):
        for j, piece in enumerate(pieces):
            row = pl.multiple_of(((at_ref[QUAD] ^ k) * QUAD + at_ref[j]) * rows, rows)
            at = pl.ds(row, rows)
            if kinds > 1:
                for n in range(kinds * piece.shape[2] // PAIR):
                    pair, kind = n // kinds, n % kinds
                    outs[0][at, n * PAIR : (n + 1) * PAIR] = piece[
                        k, kind * rows : (kind + 1) * rows, pair * PAIR : (pair + 1) * PAIR
                    ]
                continue
            for out, (low, high) in zip(outs, windows):
                out[at, :] = piece[k, :, low:high]


def place(spot, pieces, widths, kinds=1):
    windows, low = [], 0
    for width in widths:
        windows.append((low, low + width))
        low += width
    deep, rows = pieces[0].shape[0], pieces[0].shape[1] // kinds
    outs = [((deep * QUAD * rows, width), pieces[0].dtype) for width in widths]
    kernel = functools.partial(place_kernel, deep, windows, kinds)
    return vmem_call(kernel, outs, [spot.at, *pieces], "place_pieces", limit=8)


def low(value):
    return value.astype(jnp.bfloat16)


def by_pair(value):
    lead, kinds, columns = value.shape[:-2], value.shape[-2], value.shape[-1]
    split = value.reshape(lead + (kinds, columns // PAIR, PAIR))
    return jnp.swapaxes(split, -3, -2).reshape(lead + (kinds * columns,))


def by_kind(value, kinds):
    lead, columns = value.shape[:-1], value.shape[-1]
    split = value.reshape(lead + (columns // (kinds * PAIR), kinds, PAIR))
    return jnp.swapaxes(split, -3, -2).reshape(lead + (kinds, columns // kinds))


def on_device(
    inputs,
    qkv_weight,
    qv_bias,
    out_weight,
    out_bias,
    first_gain,
    first_shift,
    up_weight,
    up_bias,
    down_weight,
    down_bias,
    second_gain,
    second_shift,
    item_lengths,
    random_blocks,
    out_grad,
):
    half, width = inputs.shape
    spot = Spot()
    deep = spot.deep
    shard = qkv_weight.shape[0]
    head_width = qkv_weight.shape[2]
    up_width = up_weight.shape[1]
    pair_count = head_width // PAIR

    def position():
        return lax.axis_index("head")

    staged = deep == 4 and shard % 16 == 0
    every = ("deep", "quad")

    def gathered_whole(block):
        return lax.all_gather(block, every, axis=0, tiled=True)

    def scattered(total):
        return lax.psum_scatter(total, every, scatter_dimension=0, tiled=True).astype(jnp.float32)

    def first_quad(block):
        return quad_step(block, deep, False)

    def second_quad(block):
        return quad_step(block, deep, True)

    tokens_other = swap(inputs)
    mid = jnp.concatenate([out_weight, up_weight], axis=1)
    if staged:
        qkv_block = jnp.swapaxes(qkv_weight, 0, 1).reshape(3 * shard, head_width)
        qkv_pieces = deep_pieces(qkv_block, spot)
        mid_pieces = deep_pieces(after(mid, *qkv_pieces), spot)
        qkv_deep = jnp.stack([qkv_block] + qkv_pieces)
        qkv_other, qkv_far = first_quad(qkv_deep), second_quad(qkv_deep)
        qkv_other, qkv_far, *mid_pieces = lax.optimization_barrier(
            (qkv_other, qkv_far, *mid_pieces)
        )
        qkv_across = second_quad(qkv_other)
        (full_qkv,) = place(
            spot, (qkv_deep, qkv_other, qkv_far, qkv_across), [3 * head_width], kinds=3
        )
        full_qkv, *mid_pieces = lax.optimization_barrier((full_qkv, *mid_pieces))
        mid_deep = jnp.stack([mid] + mid_pieces)
        mid_other, mid_far = first_quad(mid_deep), second_quad(mid_deep)
        full_qkv, mid_deep = lax.optimization_barrier((full_qkv, mid_deep))
        down_pieces = deep_pieces(after(down_weight, *mid_pieces), spot)
    else:
        full_qkv = gathered_whole(by_pair(qkv_weight))
        full_mid = gathered_whole(mid)
        full_out, full_up = full_mid[:, :head_width], full_mid[:, head_width:]
        full_down = gathered_whole(down_weight)

    bias = by_pair(jnp.stack([qv_bias[0], jnp.zeros_like(qv_bias[0]), qv_bias[1]]))
    triple = triple_of(inputs, tokens_other, full_qkv, bias)
    attended = attention_forward(item_lengths, random_blocks, triple, position)
    if staged:
        attended, mid_other, mid_far, *down_pieces = lax.optimization_barrier(
            (attended, mid_other, mid_far, *down_pieces)
        )
        mid_across = second_quad(mid_other)
        down_deep = jnp.stack([down_weight] + down_pieces)
        down_other, down_far = first_quad(down_deep), second_quad(down_deep)
        mid_across, down_other = lax.optimization_barrier((mid_across, down_other))
        down_across = second_quad(down_other)
        full_out, full_up = place(
            spot, (mid_deep, mid_other, mid_far, mid_across), [head_width, up_width]
        )

    whole = (half, 2 * half)
    other = swap(rows_product([attended], full_out, whole, jnp.bfloat16))
    proj = rows_product([attended], full_out, (0, half), jnp.float32) + other.astype(jnp.float32)
    normed_one_out, normed_one, inverse_one = norm_forward(
        proj + out_bias + inputs.astype(jnp.float32), first_gain, first_shift
    )
    hidden_own = low(normed_one_out)
    hidden_other = swap(hidden_own)
    active_own, slope_own = up_gelu(hidden_own, full_up, up_bias)
    if staged:
        active_own, hidden_other, down_across = lax.optimization_barrier(
            (active_own, hidden_other, down_across)
        )
    active_other, slope_other = up_gelu(hidden_other, full_up, up_bias)
    if staged:
        active_other, active_own, down_far = lax.optimization_barrier(
            (active_other, active_own, down_far)
        )
        (full_down,) = place(spot, (down_deep, down_other, down_far, down_across), [up_width])
    other = swap(rows_product([active_other], full_down, (0, half), jnp.bfloat16))
    layer_out, grad_res_two, grad_own, sums_two = norm_two(
        item_lengths,
        rows_product([active_own], full_down, (0, half), jnp.float32),
        other,
        normed_one_out,
        out_grad,
        down_bias,
        second_gain,
        second_shift,
        position,
    )
    grad_other = swap(grad_own)
    grad_upper_own, up_sum_own = back_slope(grad_own, full_down, slope_own)
    down_local = outer([grad_own, grad_other], [active_own, active_other])
    if staged:
        near_message, far_message = sum_first_apart(down_local, spot)
        down_far_got = first_quad(far_message)
        grad_other, near_message = lax.optimization_barrier((grad_other, near_message))
        down_got = first_quad(near_message)
    grad_upper_other, up_sum_other = back_slope(grad_other, full_down, slope_other)
    other = swap(rows_product([grad_upper_other], full_up, (0, half), jnp.bfloat16))
    up_local = outer([hidden_own, hidden_other], [grad_upper_own, grad_upper_other])
    grad_res_one, grad_proj_own, sums_one = norm_one_back(
        rows_product([grad_upper_own], full_up, (0, half), jnp.float32), other, grad_res_two, normed_one, inverse_one, first_gain
    )
    if staged:
        grad_proj_own, down_far_got = lax.optimization_barrier((grad_proj_own, down_far_got))
        down_message = sum_second([down_local], spot, down_far_got)
        down_two = second_quad(down_message)
        grad_proj_own, down_message = lax.optimization_barrier((grad_proj_own, down_message))
    grad_proj_other = swap(grad_proj_own)
    shared = jnp.concatenate([sums_one, sums_two], axis=0)
    shared_other = swap(shared)
    grad_attended = project_both(grad_proj_own, grad_proj_other, full_out)
    out_local = outer([grad_proj_own, grad_proj_other], [attended])

    mids = [out_local, up_local]
    split = pair_count - 1
    if staged:
        mid_message = sum_first(mids, spot)
        mid_got = first_quad(mid_message)
        grad_attended, down_got = lax.optimization_barrier((grad_attended, down_got))
        grad_attended, mid_message = lax.optimization_barrier((grad_attended, mid_message))
    grads_a, sums_a = attention_backward(
        item_lengths, random_blocks, triple, grad_attended, range(split), position
    )
    if staged:
        grads_a, mid_got, down_two, grad_attended, shared_other = lax.optimization_barrier(
            (grads_a, mid_got, down_two, grad_attended, shared_other)
        )
        mid_message = sum_second(mids, spot, mid_got)
        mid_two = second_quad(mid_message)
        down_sum, *messages = sum_deep([[down_local]], spot, [down_got], [down_two])
        down_answers = [deep_step(m, deep, k + 1) for k, m in enumerate(messages)]
    local_a = outer([inputs, tokens_other], [grads_a])
    if staged:
        message_a = sum_first([local_a], spot)
        got_a = first_quad(message_a)
        grad_attended, message_a, mid_message, *messages = lax.optimization_barrier(
            (grad_attended, message_a, mid_message, *messages)
        )
    grads_b, sums_b = attention_backward(
        item_lengths, random_blocks, triple, grad_attended, range(split, pair_count), position
    )
    if staged:
        grads_b, got_a, mid_two, *down_answers = lax.optimization_barrier(
            (grads_b, got_a, mid_two, *down_answers)
        )
    local_b = outer([inputs, tokens_other], [grads_b])
    small = small_sums(shared, shared_other, up_sum_own, up_sum_other, [sums_a, sums_b])
    if staged:
        message_b = sum_first([local_b], spot, small)
        got_b = first_quad(message_b)
        message_a = sum_second([local_a], spot, after(got_a, message_b))
        two_a = second_quad(message_a)
        grads_a, grads_b, message_a = lax.optimization_barrier((grads_a, grads_b, message_a))
    product = rows_product([grads_a, grads_b], full_qkv, whole, jnp.bfloat16)
    if staged:
        mid_got, product = lax.optimization_barrier((mid_got, product))
        mid_sum, *messages = sum_deep([mids], spot, [mid_got], [mid_two])
        mid_answers = [deep_step(m, deep, k + 1) for k, m in enumerate(messages[:-1])]
        mid_last = messages[-1]
        product, *messages = lax.optimization_barrier((product, *messages))
    other = swap(product)
    if staged:
        grads_a, other, got_b, two_a = lax.optimization_barrier((grads_a, other, got_b, two_a))
        message, small = sum_second([local_b], spot, got_b, small)
        two_b = second_quad(message)
        grads_a, message, mid_last = lax.optimization_barrier((grads_a, message, mid_last))
        mid_answers.append(deep_step(mid_last, deep, deep - 1))
    mine = rows_product([grads_a, grads_b], full_qkv, (0, half), jnp.float32)
    input_grad = low(mine + other.astype(jnp.float32) + grad_res_one)
    if staged:
        (grad_down,) = sum_last(down_sum, down_answers, [up_width])
        input_grad, grad_down, two_b = lax.optimization_barrier((input_grad, grad_down, two_b))
        small, qkv_sum, *messages = sum_deep(
            [[local_a], [local_b]], spot, [got_a, got_b], [two_a, two_b], small
        )
        answers = [deep_step(m, deep, k + 1) for k, m in enumerate(messages)]
        grad_out, grad_up = sum_last(mid_sum, mid_answers, [head_width, up_width])
        grad_out, grad_up, *answers = lax.optimization_barrier((grad_out, grad_up, *answers))
        grad_qkv, grad_up_bias, grad_qv_bias, small = sum_last(
            qkv_sum, answers, [3 * head_width], small, up_width
        )
        grad_qkv = jnp.swapaxes(grad_qkv, 0, 1)
        grad_up_bias = grad_up_bias.reshape(up_width)
    else:
        grad_down, grad_up, grad_out = (scattered(v) for v in (down_local, up_local, out_local))
        grad_qkv = by_kind(scattered(jnp.concatenate([local_a, local_b], axis=1)), 3)
        small = lax.psum(small, every)
        part = small.shape[0] // 3
        small = jnp.concatenate([small[n * part : (n + 1) * part] for n in range(3)], axis=1)
        rest = small[:, width : width + head_width]
        grad_up_bias = rest[: up_width // head_width].reshape(up_width)
        grad_qv_bias = rest[up_width // head_width :]
    totals = small[:, :width]
    return (
        layer_out,
        input_grad,
        grad_qkv,
        grad_qv_bias,
        grad_out,
        totals[0],
        totals[1],
        totals[2],
        grad_up,
        grad_up_bias,
        grad_down,
        totals[3],
        totals[4],
        totals[5],
    )


def solution(mesh):
    devices = mesh.devices.reshape(-1, QUAD, mesh.shape["head"])
    fine = Mesh(devices, ("deep", "quad", "head"))
    rows = ("deep", "quad", "head")
    dp = ("deep", "quad")
    in_specs = (
        P(rows, None),
        P(dp, None, "head"),
        P(None, "head"),
        P(dp, "head"),
        P(),
        P(),
        P(),
        P(dp, "head"),
        P("head"),
        P(dp, "head"),
        P(),
        P(),
        P(),
        P(dp, None),
        P(dp, "head", None, None),
        P(rows, None),
    )
    out_specs = (
        P(rows, None),
        P(rows, None),
        P(dp, None, "head"),
        P(None, "head"),
        P(dp, "head"),
        P(),
        P(),
        P(),
        P(dp, "head"),
        P("head"),
        P(dp, "head"),
        P(),
        P(),
        P(),
    )
    return jax.shard_map(
        on_device, mesh=fine, in_specs=in_specs, out_specs=out_specs, check_vma=False
    )
```
